128 devices in a mesh: slab: 32 (over y, z, core), col: 4 (over x).
Axes of the slice: x: 4, y: 4, z: 4, core: 2. Of those that a mesh axis runs over, the one named last changes fastest.
Arguments:
- input_map: float32 [64, 64, 192, 128], P('col', 'slab'), may hold values from -24 to 24
- output_map: float32 [64, 64, 192, 128], P('col', 'slab'), may hold values from -24 to 24
- region_ids: int32 [64, 192, 128], P('slab'), may hold values from 0 to 7
- region_cond: float32 [8], replicated, may hold values from 0.3 to 3
- shift_ids: int32 [2], replicated, may hold values from 0 to 7
Outputs:
- ctrl_factor: float32 [2, 64, 64, 192, 128], P(None, None, 'slab', 'col')
- obsv_factor: float32 [2, 64, 64, 192, 128], P(None, None, 'slab', 'col')
- cross_gram: float32 [128, 128], P('slab', 'col')
The draws below stay inside these ranges and needn't reach their ends.
All inputs are finite; a program needn't handle non-finite values.
Results may differ from the reference program's by a relative error of at most 0.000098.
Values sent between devices are 32-bit elements; how exact they have to be, the bound alone decides.
A program may use at most 192 MiB of HBM per device.

```python
import math
import jax
import jax.numpy as jnp
from jax import lax

K = 64
ADI = 2
STEPS = 3
NY = 192
NZ = 128
REGIONS = 8
SHIFTS = 8
NX = 64
NCELLS = 1572864


def with_ends(entries, own_key, smallest, top_value):
    index_at = [jax.random.randint(jax.random.fold_in(own_key, axis), (), 0, length) for axis, length in enumerate(entries.shape)]
    main_axis = entries.shape.index(max(entries.shape))
    next_to = index_at[:main_axis] + [(index_at[main_axis] + 1) % entries.shape[main_axis]] + index_at[main_axis + 1:]
    return entries.at[tuple(index_at)].set(smallest).at[tuple(next_to)].set(top_value)


def shard_levels(own_key, dims, shards, least, high):
    def one(axis_at, parts):
        heights = jax.random.uniform(jax.random.fold_in(jax.random.fold_in(own_key, 6), axis_at), (parts,), jnp.float32, least / len(shards), high / len(shards))
        return jnp.repeat(jnp.exp(heights), dims[axis_at] // parts).reshape((-1,) + (1,) * (len(dims) - axis_at - 1))

    loudness = one(*shards[0])
    for cut in shards[1:]:
        loudness = loudness * one(*cut)
    return loudness


def normal_values(own_key, shape, scale, limit, cuts=(), held_as=jnp.bfloat16):
    values = jax.random.normal(own_key, shape, jnp.float32) * scale
    if len(cuts) > 0:
        values = shard_levels(own_key, shape, cuts, -0.22, 0.18) * values
    return jnp.clip(values, min=-limit, max=limit).astype(held_as)


def setup_inputs(seed: int = 0) -> dict:
    splits = jax.random.split(jax.random.key(seed), 6)
    input_map = normal_values(splits[0], (K, NX, NY, NZ), 4.0, 24.0, ((0, 4), (1, 32)), jnp.float32)
    output_map = normal_values(splits[1], (K, NX, NY, NZ), 4.0, 24.0, ((0, 4), (1, 32)), jnp.float32)
    region_ids = with_ends(jax.random.randint(splits[2], (NX, NY, NZ), 0, REGIONS), jax.random.fold_in(splits[2], 1), 0, REGIONS - 1).astype(jnp.int32)
    region_cond = jnp.clip(jnp.exp(jax.random.uniform(splits[3], (REGIONS,), jnp.float32, math.log(0.3), math.log(3.0))), 0.3, 3.0)
    shift_ids = jax.random.randint(splits[4], (ADI,), 0, SHIFTS).astype(jnp.int32)
    return dict(input_map=input_map, output_map=output_map, region_ids=region_ids, region_cond=region_cond, shift_ids=shift_ids)


def lookup(region_ids, region_cond):
    summed = jnp.zeros(region_ids.shape, jnp.float32)
    for region in range(region_cond.shape[0]):
        summed = summed + jnp.where(region_ids == region, region_cond[region], jnp.float32(0.0))
    return summed

def conduction(field_in, cond_ext):
    centre = field_in[:, 1:-1]
    cond_mid = cond_ext[1:-1]
    summed = 0.5 * (cond_mid + cond_ext[2:]) * (centre - field_in[:, 2:])
    summed = summed + 0.5 * (cond_mid + cond_ext[:-2]) * (centre - field_in[:, :-2])
    cond_y = jnp.pad(cond_mid, ((0, 0), (1, 1), (0, 0)))
    field_y = jnp.pad(centre, ((0, 0), (0, 0), (1, 1), (0, 0)))
    summed = summed + 0.5 * (cond_mid + cond_y[:, 2:]) * (centre - field_y[:, :, 2:])
    summed = summed + 0.5 * (cond_mid + cond_y[:, :-2]) * (centre - field_y[:, :, :-2])
    cond_z = jnp.pad(cond_mid, ((0, 0), (0, 0), (1, 1)))
    field_z = jnp.pad(centre, ((0, 0), (0, 0), (0, 0), (1, 1)))
    summed = summed + 0.5 * (cond_mid + cond_z[:, :, 2:]) * (centre - field_z[:, :, :, 2:])
    summed = summed + 0.5 * (cond_mid + cond_z[:, :, :-2]) * (centre - field_z[:, :, :, :-2])
    return summed

def bounds(shift_val, cond_max):
    low_eig = shift_val
    high_eig = shift_val + 12.0 * cond_max
    mid_eig = 0.5 * (high_eig + low_eig)
    half_span = 0.5 * (high_eig - low_eig)
    return (mid_eig, half_span, mid_eig / half_span)

def reference(input_map, output_map, region_ids, region_cond, shift_ids):
    cond_cells = lookup(region_ids, region_cond)
    cond_pad = jnp.pad(cond_cells, ((1, 1), (0, 0), (0, 0)))
    cond_max = jnp.max(region_cond)
    shifts = 0.25 * jnp.exp2(shift_ids.astype(jnp.float32))

    def chebyshev(right_side, shift_val):
        mid_eig, half_span, ratio_eig = bounds(shift_val, cond_max)
        rho_now = 1.0 / ratio_eig
        solution = jnp.zeros_like(right_side)
        residual = right_side
        direction = right_side / mid_eig
        for sweep_idx in range(STEPS):
            solution = solution + direction
            if sweep_idx < STEPS - 1:
                padded = jnp.pad(direction, ((0, 0), (1, 1), (0, 0), (0, 0)))
                applied = conduction(padded, cond_pad) + shift_val * direction
                residual = residual - applied
                rho_next = 1.0 / (2.0 * ratio_eig - rho_now)
                direction = rho_next * rho_now * direction + 2.0 * rho_next / half_span * residual
                rho_now = rho_next
        return solution
    stacked = jnp.concatenate([input_map, output_map], 0)
    factors = []
    current = stacked
    for segment_idx in range(ADI):
        shift_val = shifts[segment_idx]
        if segment_idx == 0:
            current = chebyshev(stacked, shift_val)
        else:
            current = current - (shifts[segment_idx - 1] + shift_val) * chebyshev(current, shift_val)
        factors.append(jnp.sqrt(2.0 * shift_val) * current)
    ctrl_factor = jnp.stack([factor_part[:K] for factor_part in factors])
    obsv_factor = jnp.stack([factor_part[K:] for factor_part in factors])
    ctrl_flat = ctrl_factor.reshape(ADI * K, -1)
    obsv_flat = obsv_factor.reshape(ADI * K, -1)
    cross_sum = lax.dot_general(ctrl_flat, obsv_flat, (((1,), (1,)), ((), ())), precision=lax.Precision.HIGHEST, preferred_element_type=jnp.float32)
    cross_gram = cross_sum * (1.0 / math.sqrt(NCELLS))
    return (ctrl_factor, obsv_factor, cross_gram)
```

```python
import math

import jax
import jax.numpy as jnp
from jax import lax
from jax.sharding import PartitionSpec as P

ADI = 2
STEPS = 3


def extended(block, sides, width):
    for axis, dim in sides:
        count = lax.axis_size(axis)
        forward = [(i, i + 1) for i in range(count - 1)]
        backward = [(target, source) for source, target in forward]
        low = lax.ppermute(
            lax.slice_in_dim(block, block.shape[dim] - width, None, axis=dim), axis, forward
        )
        high = lax.ppermute(lax.slice_in_dim(block, 0, width, axis=dim), axis, backward)
        block = jnp.concatenate([low, block, high], axis=dim)
    return block


def lookup(region_ids, region_cond):
    summed = jnp.zeros(region_ids.shape, jnp.float32)
    for region in range(region_cond.shape[0]):
        summed = summed + jnp.where(region_ids == region, region_cond[region], jnp.float32(0.0))
    return summed


def conduction(field_in, cond_ext):
    centre = field_in[:, 1:-1]
    cond_mid = cond_ext[1:-1]
    summed = 0.5 * (cond_mid + cond_ext[2:]) * (centre - field_in[:, 2:])
    summed = summed + 0.5 * (cond_mid + cond_ext[:-2]) * (centre - field_in[:, :-2])
    cond_y = jnp.pad(cond_mid, ((0, 0), (1, 1), (0, 0)))
    field_y = jnp.pad(centre, ((0, 0), (0, 0), (1, 1), (0, 0)))
    summed = summed + 0.5 * (cond_mid + cond_y[:, 2:]) * (centre - field_y[:, :, 2:])
    summed = summed + 0.5 * (cond_mid + cond_y[:, :-2]) * (centre - field_y[:, :, :-2])
    cond_z = jnp.pad(cond_mid, ((0, 0), (0, 0), (1, 1)))
    field_z = jnp.pad(centre, ((0, 0), (0, 0), (0, 0), (1, 1)))
    summed = summed + 0.5 * (cond_mid + cond_z[:, :, 2:]) * (centre - field_z[:, :, :, 2:])
    summed = summed + 0.5 * (cond_mid + cond_z[:, :, :-2]) * (centre - field_z[:, :, :, :-2])
    return summed


def bounds(shift_val, cond_max):
    high_eig = shift_val + 12.0 * cond_max
    mid_eig = 0.5 * (high_eig + shift_val)
    half_span = 0.5 * (high_eig - shift_val)
    return (mid_eig, half_span, mid_eig / half_span)


def solve_slabs(right_side, shift_val, cond_max, cond_ext):
    mid_eig, half_span, ratio_eig = bounds(shift_val, cond_max)
    rho_now = 1.0 / ratio_eig
    solution = jnp.zeros_like(right_side)
    residual = right_side
    direction = right_side / mid_eig
    for sweep_idx in range(STEPS - 1):
        solution = solution + direction
        padded = extended(direction, (("slab", 1),), 1)
        applied = conduction(padded, cond_ext) + shift_val * direction
        residual = residual - applied
        rho_next = 1.0 / (2.0 * ratio_eig - rho_now)
        direction = rho_next * rho_now * direction + 2.0 * rho_next / half_span * residual
        rho_now = rho_next
    return solution + direction


def run_segments(stacked, shifts, solver):
    factors = []
    current = stacked
    for segment_idx in range(ADI):
        shift_val = shifts[segment_idx]
        if segment_idx == 0:
            current = solver(stacked, shift_val)
        else:
            current = current - (shifts[segment_idx - 1] + shift_val) * solver(current, shift_val)
        factors.append(jnp.sqrt(2.0 * shift_val) * current)
    return jnp.stack(factors)


def body(input_map, output_map, region_ids, region_cond, shift_ids):
    col_local = input_map.shape[0]
    local_x = input_map.shape[1]
    cond_cells = lookup(region_ids, region_cond)
    cond_max = jnp.max(region_cond)
    shifts = 0.25 * jnp.exp2(shift_ids.astype(jnp.float32))
    total_x = local_x * lax.axis_size("slab")
    stacked = jnp.concatenate([input_map, output_map], 0)
    cond_ext = extended(cond_cells, (("slab", 0),), 1)
    factor_stack = run_segments(
        stacked, shifts, lambda rhs, shift_val: solve_slabs(rhs, shift_val, cond_max, cond_ext)
    )
    ctrl_local = factor_stack[:, :col_local]
    obsv_local = factor_stack[:, col_local:]
    ctrl_cols, obsv_cols = (
        lax.all_to_all(ctrl_local, "col", split_axis=3, concat_axis=1, tiled=True),
        lax.all_to_all(obsv_local, "col", split_axis=3, concat_axis=1, tiled=True),
    )
    row_count = ctrl_cols.shape[0] * ctrl_cols.shape[1]
    ctrl_flat = ctrl_cols.reshape(row_count, -1)
    obsv_flat = obsv_cols.reshape(row_count, -1)
    partial_value = lax.dot_general(
        ctrl_flat,
        obsv_flat,
        (((1,), (1,)), ((), ())),
        precision=lax.Precision.HIGHEST,
        preferred_element_type=jnp.float32,
    )
    cells_total = total_x * region_ids.shape[1] * region_ids.shape[2]
    norm_scale = 1.0 / math.sqrt(cells_total)
    slab_count = lax.axis_size("slab")
    col_count = lax.axis_size("col")
    tile_rows = row_count // slab_count
    tile_cols = row_count // col_count
    tiles = partial_value.reshape(slab_count, tile_rows, col_count, tile_cols)
    tiles = tiles.transpose(0, 2, 1, 3).reshape(slab_count * col_count, tile_rows, tile_cols)
    received = lax.all_to_all(tiles, ("slab", "col"), 0, 0, tiled=True)
    own_tile = jnp.sum(received, axis=0)
    return (ctrl_cols, obsv_cols, own_tile * norm_scale)


def solution(mesh):
    placed = (
        P("col", "slab", None, None),
        P("col", "slab", None, None),
        P("slab", None, None),
        P(),
        P(),
    )
    return jax.shard_map(
        body,
        mesh=mesh,
        in_specs=placed,
        out_specs=(
            P(None, None, "slab", "col", None),
            P(None, None, "slab", "col", None),
            P("slab", "col"),
        ),
        check_vma=False,
    )
```

```python
import math

import jax
import jax.numpy as jnp
from jax import lax
from jax.sharding import PartitionSpec as P

ADI = 2
STEPS = 3


def extended(block, sides, width):
    for axis, dim in sides:
        count = lax.axis_size(axis)
        forward = [(i, i + 1) for i in range(count - 1)]
        backward = [(target, source) for source, target in forward]
        low = lax.ppermute(
            lax.slice_in_dim(block, block.shape[dim] - width, None, axis=dim), axis, forward
        )
        high = lax.ppermute(lax.slice_in_dim(block, 0, width, axis=dim), axis, backward)
        block = jnp.concatenate([low, block, high], axis=dim)
    return block


def lookup(region_ids, region_cond):
    summed = jnp.zeros(region_ids.shape, jnp.float32)
    for region in range(region_cond.shape[0]):
        summed = summed + jnp.where(region_ids == region, region_cond[region], jnp.float32(0.0))
    return summed


def conduction(field_in, cond_ext):
    centre = field_in[:, 1:-1]
    cond_mid = cond_ext[1:-1]
    summed = 0.5 * (cond_mid + cond_ext[2:]) * (centre - field_in[:, 2:])
    summed = summed + 0.5 * (cond_mid + cond_ext[:-2]) * (centre - field_in[:, :-2])
    cond_y = jnp.pad(cond_mid, ((0, 0), (1, 1), (0, 0)))
    field_y = jnp.pad(centre, ((0, 0), (0, 0), (1, 1), (0, 0)))
    summed = summed + 0.5 * (cond_mid + cond_y[:, 2:]) * (centre - field_y[:, :, 2:])
    summed = summed + 0.5 * (cond_mid + cond_y[:, :-2]) * (centre - field_y[:, :, :-2])
    cond_z = jnp.pad(cond_mid, ((0, 0), (0, 0), (1, 1)))
    field_z = jnp.pad(centre, ((0, 0), (0, 0), (0, 0), (1, 1)))
    summed = summed + 0.5 * (cond_mid + cond_z[:, :, 2:]) * (centre - field_z[:, :, :, 2:])
    summed = summed + 0.5 * (cond_mid + cond_z[:, :, :-2]) * (centre - field_z[:, :, :, :-2])
    return summed


def bounds(shift_val, cond_max):
    high_eig = shift_val + 12.0 * cond_max
    mid_eig = 0.5 * (high_eig + shift_val)
    half_span = 0.5 * (high_eig - shift_val)
    return (mid_eig, half_span, mid_eig / half_span)


def solve_slabs(right_side, shift_val, cond_max, cond_ext):
    mid_eig, half_span, ratio_eig = bounds(shift_val, cond_max)
    rho_now = 1.0 / ratio_eig
    solution = jnp.zeros_like(right_side)
    residual = right_side
    direction = right_side / mid_eig
    for sweep_idx in range(STEPS - 1):
        solution = solution + direction
        padded = extended(direction, (("slab", 1),), 1)
        applied = conduction(padded, cond_ext) + shift_val * direction
        residual = residual - applied
        rho_next = 1.0 / (2.0 * ratio_eig - rho_now)
        direction = rho_next * rho_now * direction + 2.0 * rho_next / half_span * residual
        rho_now = rho_next
    return solution + direction


def run_segments(stacked, shifts, solver):
    factors = []
    current = stacked
    for segment_idx in range(ADI):
        shift_val = shifts[segment_idx]
        if segment_idx == 0:
            current = solver(stacked, shift_val)
        else:
            current = current - (shifts[segment_idx - 1] + shift_val) * solver(current, shift_val)
        factors.append(jnp.sqrt(2.0 * shift_val) * current)
    return jnp.stack(factors)


def body(input_map, output_map, region_ids, region_cond, shift_ids):
    col_local = input_map.shape[0]
    local_x = input_map.shape[1]
    cond_cells = lookup(region_ids, region_cond)
    cond_max = jnp.max(region_cond)
    shifts = 0.25 * jnp.exp2(shift_ids.astype(jnp.float32))
    total_x = local_x * lax.axis_size("slab")
    stacked = jnp.concatenate([input_map, output_map], 0)
    cond_ext = extended(cond_cells, (("slab", 0),), 1)
    factor_stack = run_segments(
        stacked, shifts, lambda rhs, shift_val: solve_slabs(rhs, shift_val, cond_max, cond_ext)
    )
    ctrl_local = factor_stack[:, :col_local]
    obsv_local = factor_stack[:, col_local:]
    ctrl_cols, obsv_cols = (
        lax.all_to_all(ctrl_local, "col", split_axis=3, concat_axis=1, tiled=True),
        lax.all_to_all(obsv_local, "col", split_axis=3, concat_axis=1, tiled=True),
    )
    row_count = ctrl_cols.shape[0] * ctrl_cols.shape[1]
    ctrl_flat = ctrl_cols.reshape(row_count, -1)
    obsv_flat = obsv_cols.reshape(row_count, -1)
    partial_value = lax.dot_general(
        ctrl_flat,
        obsv_flat,
        (((1,), (1,)), ((), ())),
        precision=lax.Precision.HIGHEST,
        preferred_element_type=jnp.float32,
    )
    cells_total = total_x * region_ids.shape[1] * region_ids.shape[2]
    norm_scale = 1.0 / math.sqrt(cells_total)
    slab_count = lax.axis_size("slab")
    col_count = lax.axis_size("col")
    tile_rows = row_count // slab_count
    tile_cols = row_count // col_count
    col_parts = partial_value.reshape(row_count, col_count, tile_cols).transpose(1, 0, 2)
    col_sum = jnp.sum(lax.all_to_all(col_parts, "col", 0, 0, tiled=True), axis=0)
    row_parts = col_sum.reshape(slab_count, tile_rows, tile_cols)
    own_tile = jnp.sum(lax.all_to_all(row_parts, "slab", 0, 0, tiled=True), axis=0)
    return (ctrl_cols, obsv_cols, own_tile * norm_scale)


def solution(mesh):
    placed = (
        P("col", "slab", None, None),
        P("col", "slab", None, None),
        P("slab", None, None),
        P(),
        P(),
    )
    return jax.shard_map(
        body,
        mesh=mesh,
        in_specs=placed,
        out_specs=(
            P(None, None, "slab", "col", None),
            P(None, None, "slab", "col", None),
            P("slab", "col"),
        ),
        check_vma=False,
    )
```

```python
import math

import jax
import jax.numpy as jnp
from jax import lax
from jax.experimental import pallas as pl
from jax.experimental.pallas import tpu as pltpu
from jax.sharding import PartitionSpec as P

ADI = 2
STEPS = 3


def extended(block, sides, width):
    for axis, dim in sides:
        count = lax.axis_size(axis)
        forward = [(i, i + 1) for i in range(count - 1)]
        backward = [(target, source) for source, target in forward]
        low = lax.ppermute(
            lax.slice_in_dim(block, block.shape[dim] - width, None, axis=dim), axis, forward
        )
        high = lax.ppermute(lax.slice_in_dim(block, 0, width, axis=dim), axis, backward)
        block = jnp.concatenate([low, block, high], axis=dim)
    return block


def scatter_sum_kernel(tiles_ref, out_ref, recv, send_sem, recv_sem):
    count = tiles_ref.shape[0]
    me = lax.axis_index("slab")
    col = lax.axis_index("col")
    recv[pl.ds(me, 1)] = tiles_ref[pl.ds(me, 1)]
    barrier = pltpu.get_barrier_semaphore()

    def greet(k, carry):
        peer = lax.rem(me + k, count)
        pl.semaphore_signal(barrier, inc=1, device_id=(peer, col), device_id_type=pl.DeviceIdType.MESH)
        return carry

    lax.fori_loop(1, count, greet, 0)
    pl.semaphore_wait(barrier, count - 1)

    def copy_to(k):
        peer = lax.rem(me + k, count)
        return pltpu.make_async_remote_copy(
            src_ref=tiles_ref.at[pl.ds(peer, 1)],
            dst_ref=recv.at[pl.ds(me, 1)],
            send_sem=send_sem.at[peer],
            recv_sem=recv_sem.at[me],
            device_id=(peer, col),
            device_id_type=pl.DeviceIdType.MESH,
        )

    def send(k, carry):
        copy_to(k).start()
        return carry

    lax.fori_loop(1, count, send, 0)

    def finish(k, carry):
        peer = lax.rem(me + k, count)
        copy_to(k).wait_send()
        pltpu.make_async_remote_copy(
            src_ref=tiles_ref.at[pl.ds(me, 1)],
            dst_ref=recv.at[pl.ds(peer, 1)],
            send_sem=send_sem.at[me],
            recv_sem=recv_sem.at[peer],
            device_id=(peer, col),
            device_id_type=pl.DeviceIdType.MESH,
        ).wait_recv()
        return carry

    lax.fori_loop(1, count, finish, 0)
    out_ref[...] = jnp.sum(recv[...], axis=0, keepdims=True)


def scatter_sum(tiles):
    count, rows, lanes = tiles.shape
    return pl.pallas_call(
        scatter_sum_kernel,
        out_shape=jax.ShapeDtypeStruct((1, rows, lanes), jnp.float32),
        in_specs=[pl.BlockSpec(memory_space=pltpu.VMEM)],
        out_specs=pl.BlockSpec(memory_space=pltpu.VMEM),
        scratch_shapes=[
            pltpu.VMEM((count, rows, lanes), jnp.float32),
            pltpu.SemaphoreType.DMA((count,)),
            pltpu.SemaphoreType.DMA((count,)),
        ],
        compiler_params=pltpu.CompilerParams(collective_id=0, has_side_effects=True),
    )(tiles)


def lookup(region_ids, region_cond):
    summed = jnp.zeros(region_ids.shape, jnp.float32)
    for region in range(region_cond.shape[0]):
        summed = summed + jnp.where(region_ids == region, region_cond[region], jnp.float32(0.0))
    return summed


def conduction(field_in, cond_ext):
    centre = field_in[:, 1:-1]
    cond_mid = cond_ext[1:-1]
    summed = 0.5 * (cond_mid + cond_ext[2:]) * (centre - field_in[:, 2:])
    summed = summed + 0.5 * (cond_mid + cond_ext[:-2]) * (centre - field_in[:, :-2])
    cond_y = jnp.pad(cond_mid, ((0, 0), (1, 1), (0, 0)))
    field_y = jnp.pad(centre, ((0, 0), (0, 0), (1, 1), (0, 0)))
    summed = summed + 0.5 * (cond_mid + cond_y[:, 2:]) * (centre - field_y[:, :, 2:])
    summed = summed + 0.5 * (cond_mid + cond_y[:, :-2]) * (centre - field_y[:, :, :-2])
    cond_z = jnp.pad(cond_mid, ((0, 0), (0, 0), (1, 1)))
    field_z = jnp.pad(centre, ((0, 0), (0, 0), (0, 0), (1, 1)))
    summed = summed + 0.5 * (cond_mid + cond_z[:, :, 2:]) * (centre - field_z[:, :, :, 2:])
    summed = summed + 0.5 * (cond_mid + cond_z[:, :, :-2]) * (centre - field_z[:, :, :, :-2])
    return summed


def bounds(shift_val, cond_max):
    high_eig = shift_val + 12.0 * cond_max
    mid_eig = 0.5 * (high_eig + shift_val)
    half_span = 0.5 * (high_eig - shift_val)
    return (mid_eig, half_span, mid_eig / half_span)


def solve_slabs(right_side, shift_val, cond_max, cond_ext):
    mid_eig, half_span, ratio_eig = bounds(shift_val, cond_max)
    rho_now = 1.0 / ratio_eig
    solution = jnp.zeros_like(right_side)
    residual = right_side
    direction = right_side / mid_eig
    for sweep_idx in range(STEPS - 1):
        solution = solution + direction
        padded = extended(direction, (("slab", 1),), 1)
        applied = conduction(padded, cond_ext) + shift_val * direction
        residual = residual - applied
        rho_next = 1.0 / (2.0 * ratio_eig - rho_now)
        direction = rho_next * rho_now * direction + 2.0 * rho_next / half_span * residual
        rho_now = rho_next
    return solution + direction


def run_segments(stacked, shifts, solver):
    factors = []
    current = stacked
    for segment_idx in range(ADI):
        shift_val = shifts[segment_idx]
        if segment_idx == 0:
            current = solver(stacked, shift_val)
        else:
            current = current - (shifts[segment_idx - 1] + shift_val) * solver(current, shift_val)
        factors.append(jnp.sqrt(2.0 * shift_val) * current)
    return jnp.stack(factors)


def body(input_map, output_map, region_ids, region_cond, shift_ids):
    col_local = input_map.shape[0]
    local_x = input_map.shape[1]
    cond_cells = lookup(region_ids, region_cond)
    cond_max = jnp.max(region_cond)
    shifts = 0.25 * jnp.exp2(shift_ids.astype(jnp.float32))
    total_x = local_x * lax.axis_size("slab")
    stacked = jnp.concatenate([input_map, output_map], 0)
    cond_ext = extended(cond_cells, (("slab", 0),), 1)
    factor_stack = run_segments(
        stacked, shifts, lambda rhs, shift_val: solve_slabs(rhs, shift_val, cond_max, cond_ext)
    )
    ctrl_local = factor_stack[:, :col_local]
    obsv_local = factor_stack[:, col_local:]
    ctrl_cols, obsv_cols = (
        lax.all_to_all(ctrl_local, "col", split_axis=3, concat_axis=1, tiled=True),
        lax.all_to_all(obsv_local, "col", split_axis=3, concat_axis=1, tiled=True),
    )
    row_count = ctrl_cols.shape[0] * ctrl_cols.shape[1]
    ctrl_flat = ctrl_cols.reshape(row_count, -1)
    obsv_flat = obsv_cols.reshape(row_count, -1)
    partial_value = lax.dot_general(
        ctrl_flat,
        obsv_flat,
        (((1,), (1,)), ((), ())),
        precision=lax.Precision.HIGHEST,
        preferred_element_type=jnp.float32,
    )
    cells_total = total_x * region_ids.shape[1] * region_ids.shape[2]
    norm_scale = 1.0 / math.sqrt(cells_total)
    slab_count = lax.axis_size("slab")
    col_count = lax.axis_size("col")
    tile_rows = row_count // slab_count
    tile_cols = row_count // col_count
    col_parts = partial_value.reshape(row_count, col_count, tile_cols).transpose(1, 0, 2)
    col_sum = jnp.sum(lax.all_to_all(col_parts, "col", 0, 0, tiled=True), axis=0)
    row_parts = col_sum.reshape(slab_count, 1, tile_rows * tile_cols)
    own_tile = scatter_sum(row_parts).reshape(tile_rows, tile_cols)
    return (ctrl_cols, obsv_cols, own_tile * norm_scale)


def solution(mesh):
    placed = (
        P("col", "slab", None, None),
        P("col", "slab", None, None),
        P("slab", None, None),
        P(),
        P(),
    )
    return jax.shard_map(
        body,
        mesh=mesh,
        in_specs=placed,
        out_specs=(
            P(None, None, "slab", "col", None),
            P(None, None, "slab", "col", None),
            P("slab", "col"),
        ),
        check_vma=False,
    )
```

```python
import math

import jax
import jax.numpy as jnp
from jax import lax
from jax.experimental import pallas as pl
from jax.experimental.pallas import tpu as pltpu
from jax.sharding import PartitionSpec as P

ADI = 2
STEPS = 3


def extended(block, sides, width):
    for axis, dim in sides:
        count = lax.axis_size(axis)
        forward = [(i, i + 1) for i in range(count - 1)]
        backward = [(target, source) for source, target in forward]
        low = lax.ppermute(
            lax.slice_in_dim(block, block.shape[dim] - width, None, axis=dim), axis, forward
        )
        high = lax.ppermute(lax.slice_in_dim(block, 0, width, axis=dim), axis, backward)
        block = jnp.concatenate([low, block, high], axis=dim)
    return block


def scatter_sum_kernel(tiles_ref, out_ref, recv, send_sem, recv_sem):
    count = tiles_ref.shape[0]
    me = lax.axis_index("slab")
    col = lax.axis_index("col")
    recv[pl.ds(me, 1)] = tiles_ref[pl.ds(me, 1)]
    barrier = pltpu.get_barrier_semaphore()

    def greet(k, carry):
        peer = lax.rem(me + k, count)
        pl.semaphore_signal(barrier, inc=1, device_id=(peer, col), device_id_type=pl.DeviceIdType.MESH)
        return carry

    lax.fori_loop(1, count, greet, 0)
    pl.semaphore_wait(barrier, count - 1)

    def copy_to(k):
        peer = lax.rem(me + k, count)
        return pltpu.make_async_remote_copy(
            src_ref=tiles_ref.at[pl.ds(peer, 1)],
            dst_ref=recv.at[pl.ds(me, 1)],
            send_sem=send_sem.at[peer],
            recv_sem=recv_sem.at[me],
            device_id=(peer, col),
            device_id_type=pl.DeviceIdType.MESH,
        )

    def send(k, carry):
        copy_to(k).start()
        return carry

    lax.fori_loop(1, count, send, 0)

    def finish(k, carry):
        peer = lax.rem(me + k, count)
        copy_to(k).wait_send()
        pltpu.make_async_remote_copy(
            src_ref=tiles_ref.at[pl.ds(me, 1)],
            dst_ref=recv.at[pl.ds(peer, 1)],
            send_sem=send_sem.at[me],
            recv_sem=recv_sem.at[peer],
            device_id=(peer, col),
            device_id_type=pl.DeviceIdType.MESH,
        ).wait_recv()
        return carry

    lax.fori_loop(1, count, finish, 0)
    out_ref[...] = jnp.sum(recv[...], axis=0, keepdims=True)


def scatter_sum(tiles):
    count, rows, lanes = tiles.shape
    return pl.pallas_call(
        scatter_sum_kernel,
        out_shape=jax.ShapeDtypeStruct((1, rows, lanes), jnp.float32),
        in_specs=[pl.BlockSpec(memory_space=pltpu.VMEM)],
        out_specs=pl.BlockSpec(memory_space=pltpu.VMEM),
        scratch_shapes=[
            pltpu.VMEM((count, rows, lanes), jnp.float32),
            pltpu.SemaphoreType.DMA((count,)),
            pltpu.SemaphoreType.DMA((count,)),
        ],
        compiler_params=pltpu.CompilerParams(collective_id=0, has_side_effects=True),
    )(tiles)


def lookup(region_ids, region_cond):
    summed = jnp.zeros(region_ids.shape, jnp.float32)
    for region in range(region_cond.shape[0]):
        summed = summed + jnp.where(region_ids == region, region_cond[region], jnp.float32(0.0))
    return summed


def halo_pair(block, axis, dim):
    count = lax.axis_size(axis)
    forward = [(i, i + 1) for i in range(count - 1)]
    backward = [(target, source) for source, target in forward]
    size = block.shape[dim]
    low = lax.ppermute(lax.slice_in_dim(block, size - 1, None, axis=dim), axis, forward)
    high = lax.ppermute(lax.slice_in_dim(block, 0, 1, axis=dim), axis, backward)
    return low, high


def shifted(block, low, high, dim):
    size = block.shape[dim]
    ahead = jnp.concatenate([lax.slice_in_dim(block, 1, None, axis=dim), high], axis=dim)
    behind = jnp.concatenate([low, lax.slice_in_dim(block, 0, size - 1, axis=dim)], axis=dim)
    return ahead, behind


def coefficients(cond_xy):
    cond_mid = cond_xy[1:-1, 1:-1]
    kxp = 0.5 * (cond_mid + cond_xy[2:, 1:-1])
    kxm = 0.5 * (cond_mid + cond_xy[:-2, 1:-1])
    kyp = 0.5 * (cond_mid + cond_xy[1:-1, 2:])
    kym = 0.5 * (cond_mid + cond_xy[1:-1, :-2])
    cond_z = jnp.pad(cond_mid, ((0, 0), (0, 0), (1, 1)))
    kzp = 0.5 * (cond_mid + cond_z[:, :, 2:])
    kzm = 0.5 * (cond_mid + cond_z[:, :, :-2])
    return (kxp, kxm, kyp, kym, kzp, kzm)


def conduction(field, coeffs):
    kxp, kxm, kyp, kym, kzp, kzm = coeffs
    xlo, xhi = halo_pair(field, "slab", 1)
    ylo, yhi = halo_pair(field, "col", 2)
    nxp, nxm = shifted(field, xlo, xhi, 1)
    nyp, nym = shifted(field, ylo, yhi, 2)
    field_z = jnp.pad(field, ((0, 0), (0, 0), (0, 0), (1, 1)))
    summed = kxp * (field - nxp)
    summed = summed + kxm * (field - nxm)
    summed = summed + kyp * (field - nyp)
    summed = summed + kym * (field - nym)
    summed = summed + kzp * (field - field_z[..., 2:])
    summed = summed + kzm * (field - field_z[..., :-2])
    return summed


def bounds(shift_val, cond_max):
    high_eig = shift_val + 12.0 * cond_max
    mid_eig = 0.5 * (high_eig + shift_val)
    half_span = 0.5 * (high_eig - shift_val)
    return (mid_eig, half_span, mid_eig / half_span)


def solve_slabs(right_side, shift_val, cond_max, coeffs):
    mid_eig, half_span, ratio_eig = bounds(shift_val, cond_max)
    rho_now = 1.0 / ratio_eig
    solution = jnp.zeros_like(right_side)
    residual = right_side
    direction = right_side / mid_eig
    for sweep_idx in range(STEPS - 1):
        solution = solution + direction
        applied = conduction(direction, coeffs) + shift_val * direction
        residual = residual - applied
        rho_next = 1.0 / (2.0 * ratio_eig - rho_now)
        direction = rho_next * rho_now * direction + 2.0 * rho_next / half_span * residual
        rho_now = rho_next
    return solution + direction


def run_segments(stacked, shifts, solver):
    factors = []
    current = stacked
    for segment_idx in range(ADI):
        shift_val = shifts[segment_idx]
        if segment_idx == 0:
            current = solver(stacked, shift_val)
        else:
            current = current - (shifts[segment_idx - 1] + shift_val) * solver(current, shift_val)
        factors.append(jnp.sqrt(2.0 * shift_val) * current)
    return jnp.stack(factors)


def body(input_map, output_map, region_ids, region_cond, shift_ids):
    ctrl_in = lax.all_to_all(input_map, "col", 2, 0, tiled=True)
    obsv_in = lax.all_to_all(output_map, "col", 2, 0, tiled=True)
    col_local = ctrl_in.shape[0]
    rows = ctrl_in.shape[2]
    local_x = input_map.shape[1]
    cond_cells = lookup(region_ids, region_cond)
    cond_max = jnp.max(region_cond)
    shifts = 0.25 * jnp.exp2(shift_ids.astype(jnp.float32))
    total_x = local_x * lax.axis_size("slab")
    stacked = jnp.concatenate([ctrl_in, obsv_in], 0)
    cond_ypad = jnp.pad(cond_cells, ((0, 0), (1, 1), (0, 0)))
    cond_y = lax.dynamic_slice_in_dim(cond_ypad, lax.axis_index("col") * rows, rows + 2, axis=1)
    cond_xy = extended(cond_y, (("slab", 0),), 1)
    coeffs = coefficients(cond_xy)
    factor_stack = run_segments(
        stacked, shifts, lambda rhs, shift_val: solve_slabs(rhs, shift_val, cond_max, coeffs)
    )
    ctrl_cols = factor_stack[:, :col_local]
    obsv_cols = factor_stack[:, col_local:]
    row_count = ctrl_cols.shape[0] * ctrl_cols.shape[1]
    ctrl_flat = ctrl_cols.reshape(row_count, -1)
    obsv_flat = obsv_cols.reshape(row_count, -1)
    partial_value = lax.dot_general(
        ctrl_flat,
        obsv_flat,
        (((1,), (1,)), ((), ())),
        precision=lax.Precision.HIGHEST,
        preferred_element_type=jnp.float32,
    )
    cells_total = total_x * region_ids.shape[1] * region_ids.shape[2]
    norm_scale = 1.0 / math.sqrt(cells_total)
    slab_count = lax.axis_size("slab")
    col_count = lax.axis_size("col")
    tile_rows = row_count // slab_count
    tile_cols = row_count // col_count
    col_parts = partial_value.reshape(row_count, col_count, tile_cols).transpose(1, 0, 2)
    col_sum = jnp.sum(lax.all_to_all(col_parts, "col", 0, 0, tiled=True), axis=0)
    row_parts = col_sum.reshape(slab_count, 1, tile_rows * tile_cols)
    own_tile = scatter_sum(row_parts).reshape(tile_rows, tile_cols)
    return (ctrl_cols, obsv_cols, own_tile * norm_scale)


def solution(mesh):
    placed = (
        P("col", "slab", None, None),
        P("col", "slab", None, None),
        P("slab", None, None),
        P(),
        P(),
    )
    return jax.shard_map(
        body,
        mesh=mesh,
        in_specs=placed,
        out_specs=(
            P(None, None, "slab", "col", None),
            P(None, None, "slab", "col", None),
            P("slab", "col"),
        ),
        check_vma=False,
    )
```

```python
import math

import jax
import jax.numpy as jnp
from jax import lax
from jax.experimental import pallas as pl
from jax.experimental.pallas import tpu as pltpu
from jax.sharding import PartitionSpec as P

ADI = 2
STEPS = 3


def extended(block, sides, width):
    for axis, dim in sides:
        count = lax.axis_size(axis)
        forward = [(i, i + 1) for i in range(count - 1)]
        backward = [(target, source) for source, target in forward]
        low = lax.ppermute(
            lax.slice_in_dim(block, block.shape[dim] - width, None, axis=dim), axis, forward
        )
        high = lax.ppermute(lax.slice_in_dim(block, 0, width, axis=dim), axis, backward)
        block = jnp.concatenate([low, block, high], axis=dim)
    return block


def scatter_sum_kernel(tiles_ref, out_ref, recv, send_sem, recv_sem):
    count = tiles_ref.shape[0]
    me = lax.axis_index("slab")
    col = lax.axis_index("col")
    recv[pl.ds(me, 1)] = tiles_ref[pl.ds(me, 1)]
    barrier = pltpu.get_barrier_semaphore()

    def greet(k, carry):
        peer = lax.rem(me + k, count)
        pl.semaphore_signal(barrier, inc=1, device_id=(peer, col), device_id_type=pl.DeviceIdType.MESH)
        return carry

    lax.fori_loop(1, count, greet, 0)
    pl.semaphore_wait(barrier, count - 1)

    def copy_to(k):
        peer = lax.rem(me + k, count)
        return pltpu.make_async_remote_copy(
            src_ref=tiles_ref.at[pl.ds(peer, 1)],
            dst_ref=recv.at[pl.ds(me, 1)],
            send_sem=send_sem.at[peer],
            recv_sem=recv_sem.at[me],
            device_id=(peer, col),
            device_id_type=pl.DeviceIdType.MESH,
        )

    def send(k, carry):
        copy_to(k).start()
        return carry

    lax.fori_loop(1, count, send, 0)

    def finish(k, carry):
        peer = lax.rem(me + k, count)
        copy_to(k).wait_send()
        pltpu.make_async_remote_copy(
            src_ref=tiles_ref.at[pl.ds(me, 1)],
            dst_ref=recv.at[pl.ds(peer, 1)],
            send_sem=send_sem.at[me],
            recv_sem=recv_sem.at[peer],
            device_id=(peer, col),
            device_id_type=pl.DeviceIdType.MESH,
        ).wait_recv()
        return carry

    lax.fori_loop(1, count, finish, 0)
    out_ref[...] = jnp.sum(recv[...], axis=0, keepdims=True)


def scatter_sum(tiles):
    count, rows, lanes = tiles.shape
    return pl.pallas_call(
        scatter_sum_kernel,
        out_shape=jax.ShapeDtypeStruct((1, rows, lanes), jnp.float32),
        in_specs=[pl.BlockSpec(memory_space=pltpu.VMEM)],
        out_specs=pl.BlockSpec(memory_space=pltpu.VMEM),
        scratch_shapes=[
            pltpu.VMEM((count, rows, lanes), jnp.float32),
            pltpu.SemaphoreType.DMA((count,)),
            pltpu.SemaphoreType.DMA((count,)),
        ],
        compiler_params=pltpu.CompilerParams(collective_id=0, has_side_effects=True),
    )(tiles)


def lookup(region_ids, region_cond):
    summed = jnp.zeros(region_ids.shape, jnp.float32)
    for region in range(region_cond.shape[0]):
        summed = summed + jnp.where(region_ids == region, region_cond[region], jnp.float32(0.0))
    return summed


def halo_pair(block, axis, dim):
    count = lax.axis_size(axis)
    forward = [(i, i + 1) for i in range(count - 1)]
    backward = [(target, source) for source, target in forward]
    size = block.shape[dim]
    low = lax.ppermute(lax.slice_in_dim(block, size - 1, None, axis=dim), axis, forward)
    high = lax.ppermute(lax.slice_in_dim(block, 0, 1, axis=dim), axis, backward)
    return low, high


def shifted(block, low, high, dim):
    size = block.shape[dim]
    ahead = jnp.concatenate([lax.slice_in_dim(block, 1, None, axis=dim), high], axis=dim)
    behind = jnp.concatenate([low, lax.slice_in_dim(block, 0, size - 1, axis=dim)], axis=dim)
    return ahead, behind


def coefficients(cond_xy):
    cond_mid = cond_xy[1:-1, 1:-1]
    kxp = 0.5 * (cond_mid + cond_xy[2:, 1:-1])
    kxm = 0.5 * (cond_mid + cond_xy[:-2, 1:-1])
    kyp = 0.5 * (cond_mid + cond_xy[1:-1, 2:])
    kym = 0.5 * (cond_mid + cond_xy[1:-1, :-2])
    cond_z = jnp.pad(cond_mid, ((0, 0), (0, 0), (1, 1)))
    kzp = 0.5 * (cond_mid + cond_z[:, :, 2:])
    kzm = 0.5 * (cond_mid + cond_z[:, :, :-2])
    return (kxp, kxm, kyp, kym, kzp, kzm)


def conduction(field, coeffs):
    kxp, kxm, kyp, kym, kzp, kzm = coeffs
    xlo, xhi = halo_pair(field, "slab", 1)
    ylo, yhi = halo_pair(field, "col", 2)
    nxp, nxm = shifted(field, xlo, xhi, 1)
    nyp, nym = shifted(field, ylo, yhi, 2)
    field_z = jnp.pad(field, ((0, 0), (0, 0), (0, 0), (1, 1)))
    summed = kxp * (field - nxp)
    summed = summed + kxm * (field - nxm)
    summed = summed + kyp * (field - nyp)
    summed = summed + kym * (field - nym)
    summed = summed + kzp * (field - field_z[..., 2:])
    summed = summed + kzm * (field - field_z[..., :-2])
    return summed


def bounds(shift_val, cond_max):
    high_eig = shift_val + 12.0 * cond_max
    mid_eig = 0.5 * (high_eig + shift_val)
    half_span = 0.5 * (high_eig - shift_val)
    return (mid_eig, half_span, mid_eig / half_span)


def solve_slabs(right_side, shift_val, cond_max, coeffs):
    mid_eig, half_span, ratio_eig = bounds(shift_val, cond_max)
    rho_now = 1.0 / ratio_eig
    solution = jnp.zeros_like(right_side)
    residual = right_side
    direction = right_side / mid_eig
    for sweep_idx in range(STEPS - 1):
        solution = solution + direction
        applied = conduction(direction, coeffs) + shift_val * direction
        residual = residual - applied
        rho_next = 1.0 / (2.0 * ratio_eig - rho_now)
        direction = rho_next * rho_now * direction + 2.0 * rho_next / half_span * residual
        rho_now = rho_next
    return solution + direction


def run_segments(stacked, shifts, solver):
    factors = []
    current = stacked
    for segment_idx in range(ADI):
        shift_val = shifts[segment_idx]
        if segment_idx == 0:
            current = solver(stacked, shift_val)
        else:
            current = current - (shifts[segment_idx - 1] + shift_val) * solver(current, shift_val)
        factors.append(jnp.sqrt(2.0 * shift_val) * current)
    return jnp.stack(factors)


def body(input_map, output_map, region_ids, region_cond, shift_ids):
    ctrl_in = lax.all_to_all(input_map, "col", 2, 0, tiled=True)
    obsv_in = lax.all_to_all(output_map, "col", 2, 0, tiled=True)
    col_local = ctrl_in.shape[0]
    rows = ctrl_in.shape[2]
    local_x = input_map.shape[1]
    cond_cells = lookup(region_ids, region_cond)
    cond_max = jnp.max(region_cond)
    shifts = 0.25 * jnp.exp2(shift_ids.astype(jnp.float32))
    total_x = local_x * lax.axis_size("slab")
    cond_ypad = jnp.pad(cond_cells, ((0, 0), (1, 1), (0, 0)))
    cond_y = lax.dynamic_slice_in_dim(cond_ypad, lax.axis_index("col") * rows, rows + 2, axis=1)
    cond_xy = extended(cond_y, (("slab", 0),), 1)
    coeffs = coefficients(cond_xy)
    solver = lambda rhs, shift_val: solve_slabs(rhs, shift_val, cond_max, coeffs)
    ctrl_cols = run_segments(ctrl_in, shifts, solver)
    obsv_cols = run_segments(obsv_in, shifts, solver)
    row_count = ctrl_cols.shape[0] * ctrl_cols.shape[1]
    ctrl_flat = ctrl_cols.reshape(row_count, -1)
    obsv_flat = obsv_cols.reshape(row_count, -1)
    partial_value = lax.dot_general(
        ctrl_flat,
        obsv_flat,
        (((1,), (1,)), ((), ())),
        precision=lax.Precision.HIGHEST,
        preferred_element_type=jnp.float32,
    )
    cells_total = total_x * region_ids.shape[1] * region_ids.shape[2]
    norm_scale = 1.0 / math.sqrt(cells_total)
    slab_count = lax.axis_size("slab")
    col_count = lax.axis_size("col")
    tile_rows = row_count // slab_count
    tile_cols = row_count // col_count
    col_parts = partial_value.reshape(row_count, col_count, tile_cols).transpose(1, 0, 2)
    col_sum = jnp.sum(lax.all_to_all(col_parts, "col", 0, 0, tiled=True), axis=0)
    row_parts = col_sum.reshape(slab_count, 1, tile_rows * tile_cols)
    own_tile = scatter_sum(row_parts).reshape(tile_rows, tile_cols)
    return (ctrl_cols, obsv_cols, own_tile * norm_scale)


def solution(mesh):
    placed = (
        P("col", "slab", None, None),
        P("col", "slab", None, None),
        P("slab", None, None),
        P(),
        P(),
    )
    return jax.shard_map(
        body,
        mesh=mesh,
        in_specs=placed,
        out_specs=(
            P(None, None, "slab", "col", None),
            P(None, None, "slab", "col", None),
            P("slab", "col"),
        ),
        check_vma=False,
    )
```

```python
import functools
import math

import jax
import jax.numpy as jnp
from jax import lax
from jax.experimental import pallas as pl
from jax.experimental.pallas import tpu as pltpu
from jax.sharding import PartitionSpec as P

ADI = 2
STEPS = 3


def extended(block, sides, width):
    for axis, dim in sides:
        count = lax.axis_size(axis)
        forward = [(i, i + 1) for i in range(count - 1)]
        backward = [(target, source) for source, target in forward]
        low = lax.ppermute(
            lax.slice_in_dim(block, block.shape[dim] - width, None, axis=dim), axis, forward
        )
        high = lax.ppermute(lax.slice_in_dim(block, 0, width, axis=dim), axis, backward)
        block = jnp.concatenate([low, block, high], axis=dim)
    return block


def scatter_sum_kernel(tiles_ref, out_ref, recv, send_sem, recv_sem):
    count = tiles_ref.shape[0]
    me = lax.axis_index("slab")
    col = lax.axis_index("col")
    recv[pl.ds(me, 1)] = tiles_ref[pl.ds(me, 1)]
    barrier = pltpu.get_barrier_semaphore()

    def greet(k, carry):
        peer = lax.rem(me + k, count)
        pl.semaphore_signal(barrier, inc=1, device_id=(peer, col), device_id_type=pl.DeviceIdType.MESH)
        return carry

    lax.fori_loop(1, count, greet, 0)
    pl.semaphore_wait(barrier, count - 1)

    def copy_to(k):
        peer = lax.rem(me + k, count)
        return pltpu.make_async_remote_copy(
            src_ref=tiles_ref.at[pl.ds(peer, 1)],
            dst_ref=recv.at[pl.ds(me, 1)],
            send_sem=send_sem.at[peer],
            recv_sem=recv_sem.at[me],
            device_id=(peer, col),
            device_id_type=pl.DeviceIdType.MESH,
        )

    def send(k, carry):
        copy_to(k).start()
        return carry

    lax.fori_loop(1, count, send, 0)

    def finish(k, carry):
        peer = lax.rem(me + k, count)
        copy_to(k).wait_send()
        pltpu.make_async_remote_copy(
            src_ref=tiles_ref.at[pl.ds(me, 1)],
            dst_ref=recv.at[pl.ds(peer, 1)],
            send_sem=send_sem.at[me],
            recv_sem=recv_sem.at[peer],
            device_id=(peer, col),
            device_id_type=pl.DeviceIdType.MESH,
        ).wait_recv()
        return carry

    lax.fori_loop(1, count, finish, 0)
    out_ref[...] = jnp.sum(recv[...], axis=0, keepdims=True)


def scatter_sum(tiles):
    count, rows, lanes = tiles.shape
    return pl.pallas_call(
        scatter_sum_kernel,
        out_shape=jax.ShapeDtypeStruct((1, rows, lanes), jnp.float32),
        in_specs=[pl.BlockSpec(memory_space=pltpu.VMEM)],
        out_specs=pl.BlockSpec(memory_space=pltpu.VMEM),
        scratch_shapes=[
            pltpu.VMEM((count, rows, lanes), jnp.float32),
            pltpu.SemaphoreType.DMA((count,)),
            pltpu.SemaphoreType.DMA((count,)),
        ],
        compiler_params=pltpu.CompilerParams(collective_id=0, has_side_effects=True),
    )(tiles)


def lookup(region_ids, region_cond):
    summed = jnp.zeros(region_ids.shape, jnp.float32)
    for region in range(region_cond.shape[0]):
        summed = summed + jnp.where(region_ids == region, region_cond[region], jnp.float32(0.0))
    return summed


def sweep_kernel(first, scal_ref, *refs):
    if first:
        d_ref, r_ref, xlo_ref, xhi_ref, ylo_ref, yhi_ref, k_ref = refs[:7]
        s_ref = None
        outs = refs[7:]
    else:
        s_ref, d_ref, r_ref, xlo_ref, xhi_ref, ylo_ref, yhi_ref, k_ref = refs[:8]
        outs = refs[8:]
    so_ref, ro_ref, do_ref, bx0_ref, bx1_ref, by0_ref, by1_ref = outs
    shift_val = scal_ref[0]
    keep = scal_ref[1]
    gain = scal_ref[2]
    rows = d_ref.shape[2]
    lanes = d_ref.shape[3]
    for layer in range(2):
        d = d_ref[:, layer]
        nxm = xlo_ref[:, 0] if layer == 0 else d_ref[:, 0]
        nxp = d_ref[:, 1] if layer == 0 else xhi_ref[:, 0]
        row_id = lax.broadcasted_iota(jnp.int32, d.shape, 1)
        lane_id = lax.broadcasted_iota(jnp.int32, d.shape, 2)
        nyp = jnp.where(row_id == rows - 1, yhi_ref[:, layer], pltpu.roll(d, rows - 1, 1))
        nym = jnp.where(row_id == 0, ylo_ref[:, layer], pltpu.roll(d, 1, 1))
        nzp = jnp.where(lane_id == lanes - 1, 0.0, pltpu.roll(d, lanes - 1, 2))
        nzm = jnp.where(lane_id == 0, 0.0, pltpu.roll(d, 1, 2))
        summed = k_ref[0, layer] * (d - nxp)
        summed = summed + k_ref[1, layer] * (d - nxm)
        summed = summed + k_ref[2, layer] * (d - nyp)
        summed = summed + k_ref[3, layer] * (d - nym)
        summed = summed + k_ref[4, layer] * (d - nzp)
        summed = summed + k_ref[5, layer] * (d - nzm)
        applied = summed + shift_val * d
        r_new = r_ref[:, layer] - applied
        d_new = keep * d + gain * r_new
        so_ref[:, layer] = d if s_ref is None else s_ref[:, layer] + d
        ro_ref[:, layer] = r_new
        do_ref[:, layer] = d_new
        by0_ref[:, layer] = d_new[:, 0:1]
        by1_ref[:, layer] = d_new[:, rows - 1:rows]
        if layer == 0:
            bx0_ref[:, 0] = d_new
        else:
            bx1_ref[:, 0] = d_new


def sweep(scalars, solution, direction, residual, xlo, xhi, ylo, yhi, coeffs, block=8):
    cols, depth, rows, lanes = direction.shape
    first = solution is None
    full = pl.BlockSpec((block, depth, rows, lanes), lambda i: (i, 0, 0, 0))
    xface = pl.BlockSpec((block, 1, rows, lanes), lambda i: (i, 0, 0, 0))
    yface = pl.BlockSpec((block, depth, 1, lanes), lambda i: (i, 0, 0, 0))
    kspec = pl.BlockSpec(coeffs.shape, lambda i: (0, 0, 0, 0))
    sspec = pl.BlockSpec(memory_space=pltpu.SMEM)
    operands = [direction, residual, xlo, xhi, ylo, yhi, coeffs]
    specs = [full, full, xface, xface, yface, yface, kspec]
    if not first:
        operands = [solution] + operands
        specs = [full] + specs
    big = jax.ShapeDtypeStruct(direction.shape, jnp.float32)
    xs = jax.ShapeDtypeStruct((cols, 1, rows, lanes), jnp.float32)
    ys = jax.ShapeDtypeStruct((cols, depth, 1, lanes), jnp.float32)
    cells = direction.size
    return pl.pallas_call(
        functools.partial(sweep_kernel, first),
        grid=(cols // block,),
        in_specs=[sspec] + specs,
        out_specs=[full, full, full, xface, xface, yface, yface],
        out_shape=[big, big, big, xs, xs, ys, ys],
        cost_estimate=pl.CostEstimate(flops=30 * cells, bytes_accessed=28 * cells, transcendentals=0),
    )(scalars, *operands)


def coefficients(cond_xy):
    cond_mid = cond_xy[1:-1, 1:-1]
    kxp = 0.5 * (cond_mid + cond_xy[2:, 1:-1])
    kxm = 0.5 * (cond_mid + cond_xy[:-2, 1:-1])
    kyp = 0.5 * (cond_mid + cond_xy[1:-1, 2:])
    kym = 0.5 * (cond_mid + cond_xy[1:-1, :-2])
    cond_z = jnp.pad(cond_mid, ((0, 0), (0, 0), (1, 1)))
    kzp = 0.5 * (cond_mid + cond_z[:, :, 2:])
    kzm = 0.5 * (cond_mid + cond_z[:, :, :-2])
    return jnp.stack([kxp, kxm, kyp, kym, kzp, kzm])


def neighbour_faces(faces):
    bx0, bx1, by0, by1 = faces
    pairs = {}
    for axis in ("slab", "col"):
        forward = [(i, i + 1) for i in range(lax.axis_size(axis) - 1)]
        pairs[axis] = (forward, [(target, source) for source, target in forward])
    xlo = lax.ppermute(bx1, "slab", pairs["slab"][0])
    xhi = lax.ppermute(bx0, "slab", pairs["slab"][1])
    ylo = lax.ppermute(by1, "col", pairs["col"][0])
    yhi = lax.ppermute(by0, "col", pairs["col"][1])
    return xlo, xhi, ylo, yhi


def bounds(shift_val, cond_max):
    high_eig = shift_val + 12.0 * cond_max
    mid_eig = 0.5 * (high_eig + shift_val)
    half_span = 0.5 * (high_eig - shift_val)
    return (mid_eig, half_span, mid_eig / half_span)


def solve_slabs(right_side, shift_val, cond_max, coeffs):
    mid_eig, half_span, ratio_eig = bounds(shift_val, cond_max)
    rho_now = 1.0 / ratio_eig
    solution = None
    residual = right_side
    direction = right_side / mid_eig
    faces = (direction[:, :1], direction[:, 1:], direction[:, :, :1], direction[:, :, -1:])
    for sweep_idx in range(STEPS - 1):
        rho_next = 1.0 / (2.0 * ratio_eig - rho_now)
        scalars = jnp.stack([shift_val, rho_next * rho_now, 2.0 * rho_next / half_span]).astype(jnp.float32)
        halos = neighbour_faces(faces)
        solution, residual, direction, *faces = sweep(
            scalars, solution, direction, residual, *halos, coeffs
        )
        rho_now = rho_next
    return solution + direction


def run_segments(stacked, shifts, solver):
    factors = []
    current = stacked
    for segment_idx in range(ADI):
        shift_val = shifts[segment_idx]
        if segment_idx == 0:
            current = solver(stacked, shift_val)
        else:
            current = current - (shifts[segment_idx - 1] + shift_val) * solver(current, shift_val)
        factors.append(jnp.sqrt(2.0 * shift_val) * current)
    return jnp.stack(factors)


def body(input_map, output_map, region_ids, region_cond, shift_ids):
    ctrl_in = lax.all_to_all(input_map, "col", 2, 0, tiled=True)
    obsv_in = lax.all_to_all(output_map, "col", 2, 0, tiled=True)
    col_local = ctrl_in.shape[0]
    rows = ctrl_in.shape[2]
    local_x = input_map.shape[1]
    cond_cells = lookup(region_ids, region_cond)
    cond_max = jnp.max(region_cond)
    shifts = 0.25 * jnp.exp2(shift_ids.astype(jnp.float32))
    total_x = local_x * lax.axis_size("slab")
    cond_ypad = jnp.pad(cond_cells, ((0, 0), (1, 1), (0, 0)))
    cond_y = lax.dynamic_slice_in_dim(cond_ypad, lax.axis_index("col") * rows, rows + 2, axis=1)
    cond_xy = extended(cond_y, (("slab", 0),), 1)
    coeffs = coefficients(cond_xy)
    solver = lambda rhs, shift_val: solve_slabs(rhs, shift_val, cond_max, coeffs)
    ctrl_cols = run_segments(ctrl_in, shifts, solver)
    obsv_cols = run_segments(obsv_in, shifts, solver)
    row_count = ctrl_cols.shape[0] * ctrl_cols.shape[1]
    ctrl_flat = ctrl_cols.reshape(row_count, -1)
    obsv_flat = obsv_cols.reshape(row_count, -1)
    partial_value = lax.dot_general(
        ctrl_flat,
        obsv_flat,
        (((1,), (1,)), ((), ())),
        precision=lax.Precision.HIGHEST,
        preferred_element_type=jnp.float32,
    )
    cells_total = total_x * region_ids.shape[1] * region_ids.shape[2]
    norm_scale = 1.0 / math.sqrt(cells_total)
    slab_count = lax.axis_size("slab")
    col_count = lax.axis_size("col")
    tile_rows = row_count // slab_count
    tile_cols = row_count // col_count
    col_parts = partial_value.reshape(row_count, col_count, tile_cols).transpose(1, 0, 2)
    col_sum = jnp.sum(lax.all_to_all(col_parts, "col", 0, 0, tiled=True), axis=0)
    row_parts = col_sum.reshape(slab_count, 1, tile_rows * tile_cols)
    own_tile = scatter_sum(row_parts).reshape(tile_rows, tile_cols)
    return (ctrl_cols, obsv_cols, own_tile * norm_scale)


def solution(mesh):
    placed = (
        P("col", "slab", None, None),
        P("col", "slab", None, None),
        P("slab", None, None),
        P(),
        P(),
    )
    return jax.shard_map(
        body,
        mesh=mesh,
        in_specs=placed,
        out_specs=(
            P(None, None, "slab", "col", None),
            P(None, None, "slab", "col", None),
            P("slab", "col"),
        ),
        check_vma=False,
    )
```

```python
import math

import jax
import jax.numpy as jnp
from jax import lax
from jax.experimental import pallas as pl
from jax.experimental.pallas import tpu as pltpu
from jax.sharding import PartitionSpec as P

ADI = 2
STEPS = 3


def extended(block, sides, width):
    for axis, dim in sides:
        count = lax.axis_size(axis)
        forward = [(i, i + 1) for i in range(count - 1)]
        backward = [(target, source) for source, target in forward]
        low = lax.ppermute(
            lax.slice_in_dim(block, block.shape[dim] - width, None, axis=dim), axis, forward
        )
        high = lax.ppermute(lax.slice_in_dim(block, 0, width, axis=dim), axis, backward)
        block = jnp.concatenate([low, block, high], axis=dim)
    return block


def scatter_sum_kernel(tiles_ref, out_ref, recv, send_sem, recv_sem):
    count = tiles_ref.shape[0]
    me = lax.axis_index("slab")
    col = lax.axis_index("col")
    recv[pl.ds(me, 1)] = tiles_ref[pl.ds(me, 1)]
    barrier = pltpu.get_barrier_semaphore()

    def greet(k, carry):
        peer = lax.rem(me + k, count)
        pl.semaphore_signal(barrier, inc=1, device_id=(peer, col), device_id_type=pl.DeviceIdType.MESH)
        return carry

    lax.fori_loop(1, count, greet, 0)
    pl.semaphore_wait(barrier, count - 1)

    def copy_to(k):
        peer = lax.rem(me + k, count)
        return pltpu.make_async_remote_copy(
            src_ref=tiles_ref.at[pl.ds(peer, 1)],
            dst_ref=recv.at[pl.ds(me, 1)],
            send_sem=send_sem.at[peer],
            recv_sem=recv_sem.at[me],
            device_id=(peer, col),
            device_id_type=pl.DeviceIdType.MESH,
        )

    def send(k, carry):
        copy_to(k).start()
        return carry

    lax.fori_loop(1, count, send, 0)

    def finish(k, carry):
        peer = lax.rem(me + k, count)
        copy_to(k).wait_send()
        pltpu.make_async_remote_copy(
            src_ref=tiles_ref.at[pl.ds(me, 1)],
            dst_ref=recv.at[pl.ds(peer, 1)],
            send_sem=send_sem.at[me],
            recv_sem=recv_sem.at[peer],
            device_id=(peer, col),
            device_id_type=pl.DeviceIdType.MESH,
        ).wait_recv()
        return carry

    lax.fori_loop(1, count, finish, 0)
    out_ref[...] = jnp.sum(recv[...], axis=0, keepdims=True)


def scatter_sum(tiles):
    count, rows, lanes = tiles.shape
    return pl.pallas_call(
        scatter_sum_kernel,
        out_shape=jax.ShapeDtypeStruct((1, rows, lanes), jnp.float32),
        in_specs=[pl.BlockSpec(memory_space=pltpu.VMEM)],
        out_specs=pl.BlockSpec(memory_space=pltpu.VMEM),
        scratch_shapes=[
            pltpu.VMEM((count, rows, lanes), jnp.float32),
            pltpu.SemaphoreType.DMA((count,)),
            pltpu.SemaphoreType.DMA((count,)),
        ],
        compiler_params=pltpu.CompilerParams(collective_id=0, has_side_effects=True),
    )(tiles)


def lookup(region_ids, region_cond):
    summed = jnp.zeros(region_ids.shape, jnp.float32)
    for region in range(region_cond.shape[0]):
        summed = summed + jnp.where(region_ids == region, region_cond[region], jnp.float32(0.0))
    return summed


def halo_pair(block, axis, dim):
    count = lax.axis_size(axis)
    forward = [(i, i + 1) for i in range(count - 1)]
    backward = [(target, source) for source, target in forward]
    size = block.shape[dim]
    low = lax.ppermute(lax.slice_in_dim(block, size - 1, None, axis=dim), axis, forward)
    high = lax.ppermute(lax.slice_in_dim(block, 0, 1, axis=dim), axis, backward)
    return low, high


def shifted(block, low, high, dim):
    size = block.shape[dim]
    ahead = jnp.concatenate([lax.slice_in_dim(block, 1, None, axis=dim), high], axis=dim)
    behind = jnp.concatenate([low, lax.slice_in_dim(block, 0, size - 1, axis=dim)], axis=dim)
    return ahead, behind


def coefficients(cond_xy, valid):
    cond_mid = cond_xy[1:-1, 1:-1]
    kxp = 0.5 * (cond_mid + cond_xy[2:, 1:-1])
    kxm = 0.5 * (cond_mid + cond_xy[:-2, 1:-1])
    kyp = 0.5 * (cond_mid + cond_xy[1:-1, 2:])
    kym = 0.5 * (cond_mid + cond_xy[1:-1, :-2])
    cond_z = jnp.pad(cond_mid, ((0, 0), (0, 0), (1, 1)))
    kzp = 0.5 * (cond_mid + cond_z[:, :, 2:])
    kzm = 0.5 * (cond_mid + cond_z[:, :, :-2])
    return tuple(jnp.where(valid, k, 0.0) for k in (kxp, kxm, kyp, kym, kzp, kzm))


def windows(block, rows, margin, count):
    padded = jnp.pad(block, ((0, 0), (0, 0), (margin, margin), (0, 0)))
    parts = [lax.slice_in_dim(padded, c * rows, c * rows + rows + 2 * margin, axis=2) for c in range(count)]
    received = lax.all_to_all(jnp.stack(parts), "col", 0, 0, tiled=True)
    return received.reshape((-1,) + received.shape[2:])


def conduction(field, coeffs):
    kxp, kxm, kyp, kym, kzp, kzm = coeffs
    xlo, xhi = halo_pair(field, "slab", 1)
    nxp, nxm = shifted(field, xlo, xhi, 1)
    field_y = jnp.pad(field, ((0, 0), (0, 0), (1, 1), (0, 0)))
    field_z = jnp.pad(field, ((0, 0), (0, 0), (0, 0), (1, 1)))
    summed = kxp * (field - nxp)
    summed = summed + kxm * (field - nxm)
    summed = summed + kyp * (field - field_y[:, :, 2:])
    summed = summed + kym * (field - field_y[:, :, :-2])
    summed = summed + kzp * (field - field_z[..., 2:])
    summed = summed + kzm * (field - field_z[..., :-2])
    return summed


def bounds(shift_val, cond_max):
    high_eig = shift_val + 12.0 * cond_max
    mid_eig = 0.5 * (high_eig + shift_val)
    half_span = 0.5 * (high_eig - shift_val)
    return (mid_eig, half_span, mid_eig / half_span)


def solve_slabs(right_side, shift_val, cond_max, coeffs):
    mid_eig, half_span, ratio_eig = bounds(shift_val, cond_max)
    rho_now = 1.0 / ratio_eig
    solution = jnp.zeros_like(right_side)
    residual = right_side
    direction = right_side / mid_eig
    for sweep_idx in range(STEPS - 1):
        solution = solution + direction
        applied = conduction(direction, coeffs) + shift_val * direction
        residual = residual - applied
        rho_next = 1.0 / (2.0 * ratio_eig - rho_now)
        direction = rho_next * rho_now * direction + 2.0 * rho_next / half_span * residual
        rho_now = rho_next
    return solution + direction


def run_segments(stacked, shifts, solver, margin):
    factors = []
    current = stacked
    for segment_idx in range(ADI):
        shift_val = shifts[segment_idx]
        if segment_idx == 0:
            current = solver(stacked, shift_val)
        else:
            current = current - (shifts[segment_idx - 1] + shift_val) * solver(current, shift_val)
        factors.append(lax.slice_in_dim(jnp.sqrt(2.0 * shift_val) * current, margin, -margin, axis=2))
    return jnp.stack(factors)


def body(input_map, output_map, region_ids, region_cond, shift_ids):
    col_count = lax.axis_size("col")
    rows = input_map.shape[2] // col_count
    margin = ADI * (STEPS - 1)
    ctrl_in = windows(input_map, rows, margin, col_count)
    obsv_in = windows(output_map, rows, margin, col_count)
    local_x = input_map.shape[1]
    cond_cells = lookup(region_ids, region_cond)
    cond_max = jnp.max(region_cond)
    shifts = 0.25 * jnp.exp2(shift_ids.astype(jnp.float32))
    total_x = local_x * lax.axis_size("slab")
    span = rows + 2 * margin
    cond_pad = jnp.pad(cond_cells, ((0, 0), (margin + 1, margin + 1), (0, 0)))
    row_start = lax.axis_index("col") * rows
    cond_y = lax.dynamic_slice_in_dim(cond_pad, row_start, span + 2, axis=1)
    cond_xy = extended(cond_y, (("slab", 0),), 1)
    global_row = row_start - margin + lax.broadcasted_iota(jnp.int32, (1, span, 1), 1)
    valid = (global_row >= 0) & (global_row < input_map.shape[2])
    coeffs = coefficients(cond_xy, valid)
    solver = lambda rhs, shift_val: solve_slabs(rhs, shift_val, cond_max, coeffs)
    ctrl_cols = run_segments(ctrl_in, shifts, solver, margin)
    obsv_cols = run_segments(obsv_in, shifts, solver, margin)
    row_count = ctrl_cols.shape[0] * ctrl_cols.shape[1]
    ctrl_flat = ctrl_cols.reshape(row_count, -1)
    obsv_flat = obsv_cols.reshape(row_count, -1)
    partial_value = lax.dot_general(
        ctrl_flat,
        obsv_flat,
        (((1,), (1,)), ((), ())),
        precision=lax.Precision.HIGHEST,
        preferred_element_type=jnp.float32,
    )
    cells_total = total_x * region_ids.shape[1] * region_ids.shape[2]
    norm_scale = 1.0 / math.sqrt(cells_total)
    slab_count = lax.axis_size("slab")
    col_count = lax.axis_size("col")
    tile_rows = row_count // slab_count
    tile_cols = row_count // col_count
    col_parts = partial_value.reshape(row_count, col_count, tile_cols).transpose(1, 0, 2)
    col_sum = jnp.sum(lax.all_to_all(col_parts, "col", 0, 0, tiled=True), axis=0)
    row_parts = col_sum.reshape(slab_count, 1, tile_rows * tile_cols)
    own_tile = scatter_sum(row_parts).reshape(tile_rows, tile_cols)
    return (ctrl_cols, obsv_cols, own_tile * norm_scale)


def solution(mesh):
    placed = (
        P("col", "slab", None, None),
        P("col", "slab", None, None),
        P("slab", None, None),
        P(),
        P(),
    )
    return jax.shard_map(
        body,
        mesh=mesh,
        in_specs=placed,
        out_specs=(
            P(None, None, "slab", "col", None),
            P(None, None, "slab", "col", None),
            P("slab", "col"),
        ),
        check_vma=False,
    )
```

```python
import math

import jax
import jax.numpy as jnp
from jax import lax
from jax.experimental import pallas as pl
from jax.experimental.pallas import tpu as pltpu
from jax.sharding import PartitionSpec as P

ADI = 2
STEPS = 3


def extended(block, sides, width):
    for axis, dim in sides:
        count = lax.axis_size(axis)
        forward = [(i, i + 1) for i in range(count - 1)]
        backward = [(target, source) for source, target in forward]
        low = lax.ppermute(
            lax.slice_in_dim(block, block.shape[dim] - width, None, axis=dim), axis, forward
        )
        high = lax.ppermute(lax.slice_in_dim(block, 0, width, axis=dim), axis, backward)
        block = jnp.concatenate([low, block, high], axis=dim)
    return block


def scatter_sum_kernel(tiles_ref, out_ref, recv, send_sem, recv_sem):
    count = tiles_ref.shape[0]
    me = lax.axis_index("slab")
    col = lax.axis_index("col")
    recv[pl.ds(me, 1)] = tiles_ref[pl.ds(me, 1)]
    barrier = pltpu.get_barrier_semaphore()

    def greet(k, carry):
        peer = lax.rem(me + k, count)
        pl.semaphore_signal(barrier, inc=1, device_id=(peer, col), device_id_type=pl.DeviceIdType.MESH)
        return carry

    lax.fori_loop(1, count, greet, 0)
    pl.semaphore_wait(barrier, count - 1)

    def copy_to(k):
        peer = lax.rem(me + k, count)
        return pltpu.make_async_remote_copy(
            src_ref=tiles_ref.at[pl.ds(peer, 1)],
            dst_ref=recv.at[pl.ds(me, 1)],
            send_sem=send_sem.at[peer],
            recv_sem=recv_sem.at[me],
            device_id=(peer, col),
            device_id_type=pl.DeviceIdType.MESH,
        )

    def send(k, carry):
        copy_to(k).start()
        return carry

    lax.fori_loop(1, count, send, 0)

    def finish(k, carry):
        peer = lax.rem(me + k, count)
        copy_to(k).wait_send()
        pltpu.make_async_remote_copy(
            src_ref=tiles_ref.at[pl.ds(me, 1)],
            dst_ref=recv.at[pl.ds(peer, 1)],
            send_sem=send_sem.at[me],
            recv_sem=recv_sem.at[peer],
            device_id=(peer, col),
            device_id_type=pl.DeviceIdType.MESH,
        ).wait_recv()
        return carry

    lax.fori_loop(1, count, finish, 0)
    out_ref[...] = jnp.sum(recv[...], axis=0, keepdims=True)


def scatter_sum(tiles):
    count, rows, lanes = tiles.shape
    return pl.pallas_call(
        scatter_sum_kernel,
        out_shape=jax.ShapeDtypeStruct((1, rows, lanes), jnp.float32),
        in_specs=[pl.BlockSpec(memory_space=pltpu.VMEM)],
        out_specs=pl.BlockSpec(memory_space=pltpu.VMEM),
        scratch_shapes=[
            pltpu.VMEM((count, rows, lanes), jnp.float32),
            pltpu.SemaphoreType.DMA((count,)),
            pltpu.SemaphoreType.DMA((count,)),
        ],
        compiler_params=pltpu.CompilerParams(collective_id=0, has_side_effects=True),
    )(tiles)


def lookup(region_ids, region_cond):
    summed = jnp.zeros(region_ids.shape, jnp.float32)
    for region in range(region_cond.shape[0]):
        summed = summed + jnp.where(region_ids == region, region_cond[region], jnp.float32(0.0))
    return summed


def halo_pair(block, axis, dim):
    count = lax.axis_size(axis)
    forward = [(i, i + 1) for i in range(count - 1)]
    backward = [(target, source) for source, target in forward]
    size = block.shape[dim]
    low = lax.ppermute(lax.slice_in_dim(block, size - 1, None, axis=dim), axis, forward)
    high = lax.ppermute(lax.slice_in_dim(block, 0, 1, axis=dim), axis, backward)
    return low, high


def shifted(block, low, high, dim):
    size = block.shape[dim]
    ahead = jnp.concatenate([lax.slice_in_dim(block, 1, None, axis=dim), high], axis=dim)
    behind = jnp.concatenate([low, lax.slice_in_dim(block, 0, size - 1, axis=dim)], axis=dim)
    return ahead, behind


def coefficients(cond_xy):
    cond_mid = cond_xy[1:-1, 1:-1]
    kxp = 0.5 * (cond_mid + cond_xy[2:, 1:-1])
    kxm = 0.5 * (cond_mid + cond_xy[:-2, 1:-1])
    kyp = 0.5 * (cond_mid + cond_xy[1:-1, 2:])
    kym = 0.5 * (cond_mid + cond_xy[1:-1, :-2])
    cond_z = jnp.pad(cond_mid, ((0, 0), (0, 0), (1, 1)))
    kzp = 0.5 * (cond_mid + cond_z[:, :, 2:])
    kzm = 0.5 * (cond_mid + cond_z[:, :, :-2])
    return (kxp, kxm, kyp, kym, kzp, kzm)


def windows(block, rows, count):
    parts = [lax.slice_in_dim(block, c * rows, (c + 1) * rows, axis=2) for c in range(count)]
    received = lax.all_to_all(jnp.stack(parts), "col", 0, 0, tiled=True)
    return received.reshape((-1,) + received.shape[2:])


def conduction(field, coeffs):
    kxp, kxm, kyp, kym, kzp, kzm = coeffs
    xlo, xhi = halo_pair(field, "slab", 1)
    ylo, yhi = halo_pair(field, "col", 2)
    nxp, nxm = shifted(field, xlo, xhi, 1)
    nyp, nym = shifted(field, ylo, yhi, 2)
    field_z = jnp.pad(field, ((0, 0), (0, 0), (0, 0), (1, 1)))
    summed = kxp * (field - nxp)
    summed = summed + kxm * (field - nxm)
    summed = summed + kyp * (field - nyp)
    summed = summed + kym * (field - nym)
    summed = summed + kzp * (field - field_z[..., 2:])
    summed = summed + kzm * (field - field_z[..., :-2])
    return summed


def bounds(shift_val, cond_max):
    high_eig = shift_val + 12.0 * cond_max
    mid_eig = 0.5 * (high_eig + shift_val)
    half_span = 0.5 * (high_eig - shift_val)
    return (mid_eig, half_span, mid_eig / half_span)


def solve_slabs(right_side, shift_val, cond_max, coeffs):
    mid_eig, half_span, ratio_eig = bounds(shift_val, cond_max)
    rho_now = 1.0 / ratio_eig
    solution = jnp.zeros_like(right_side)
    residual = right_side
    direction = right_side / mid_eig
    for sweep_idx in range(STEPS - 1):
        solution = solution + direction
        applied = conduction(direction, coeffs) + shift_val * direction
        residual = residual - applied
        rho_next = 1.0 / (2.0 * ratio_eig - rho_now)
        direction = rho_next * rho_now * direction + 2.0 * rho_next / half_span * residual
        rho_now = rho_next
    return solution + direction


def run_segments(stacked, shifts, solver):
    factors = []
    current = stacked
    for segment_idx in range(ADI):
        shift_val = shifts[segment_idx]
        if segment_idx == 0:
            current = solver(stacked, shift_val)
        else:
            current = current - (shifts[segment_idx - 1] + shift_val) * solver(current, shift_val)
        factors.append(jnp.sqrt(2.0 * shift_val) * current)
    return jnp.stack(factors)


def body(input_map, output_map, region_ids, region_cond, shift_ids):
    col_count = lax.axis_size("col")
    ctrl_in = windows(input_map, input_map.shape[2] // col_count, col_count)
    obsv_in = windows(output_map, output_map.shape[2] // col_count, col_count)
    col_local = ctrl_in.shape[0]
    rows = ctrl_in.shape[2]
    local_x = input_map.shape[1]
    cond_cells = lookup(region_ids, region_cond)
    cond_max = jnp.max(region_cond)
    shifts = 0.25 * jnp.exp2(shift_ids.astype(jnp.float32))
    total_x = local_x * lax.axis_size("slab")
    cond_ypad = jnp.pad(cond_cells, ((0, 0), (1, 1), (0, 0)))
    cond_y = lax.dynamic_slice_in_dim(cond_ypad, lax.axis_index("col") * rows, rows + 2, axis=1)
    cond_xy = extended(cond_y, (("slab", 0),), 1)
    coeffs = coefficients(cond_xy)
    solver = lambda rhs, shift_val: solve_slabs(rhs, shift_val, cond_max, coeffs)
    ctrl_cols = run_segments(ctrl_in, shifts, solver)
    obsv_cols = run_segments(obsv_in, shifts, solver)
    row_count = ctrl_cols.shape[0] * ctrl_cols.shape[1]
    ctrl_flat = ctrl_cols.reshape(row_count, -1)
    obsv_flat = obsv_cols.reshape(row_count, -1)
    partial_value = lax.dot_general(
        ctrl_flat,
        obsv_flat,
        (((1,), (1,)), ((), ())),
        precision=lax.Precision.HIGHEST,
        preferred_element_type=jnp.float32,
    )
    cells_total = total_x * region_ids.shape[1] * region_ids.shape[2]
    norm_scale = 1.0 / math.sqrt(cells_total)
    slab_count = lax.axis_size("slab")
    col_count = lax.axis_size("col")
    tile_rows = row_count // slab_count
    tile_cols = row_count // col_count
    col_parts = partial_value.reshape(row_count, col_count, tile_cols).transpose(1, 0, 2)
    col_sum = jnp.sum(lax.all_to_all(col_parts, "col", 0, 0, tiled=True), axis=0)
    row_parts = col_sum.reshape(slab_count, 1, tile_rows * tile_cols)
    own_tile = scatter_sum(row_parts).reshape(tile_rows, tile_cols)
    return (ctrl_cols, obsv_cols, own_tile * norm_scale)


def solution(mesh):
    placed = (
        P("col", "slab", None, None),
        P("col", "slab", None, None),
        P("slab", None, None),
        P(),
        P(),
    )
    return jax.shard_map(
        body,
        mesh=mesh,
        in_specs=placed,
        out_specs=(
            P(None, None, "slab", "col", None),
            P(None, None, "slab", "col", None),
            P("slab", "col"),
        ),
        check_vma=False,
    )
```

```python
import math

import jax
import jax.numpy as jnp
from jax import lax
from jax.experimental import pallas as pl
from jax.experimental.pallas import tpu as pltpu
from jax.sharding import PartitionSpec as P

ADI = 2
STEPS = 3


def extended(block, sides, width):
    for axis, dim in sides:
        count = lax.axis_size(axis)
        forward = [(i, i + 1) for i in range(count - 1)]
        backward = [(target, source) for source, target in forward]
        low = lax.ppermute(
            lax.slice_in_dim(block, block.shape[dim] - width, None, axis=dim), axis, forward
        )
        high = lax.ppermute(lax.slice_in_dim(block, 0, width, axis=dim), axis, backward)
        block = jnp.concatenate([low, block, high], axis=dim)
    return block


def scatter_sum_kernel(tiles_ref, out_ref, recv, send_sem, recv_sem):
    count = tiles_ref.shape[0]
    me = lax.axis_index("slab")
    col = lax.axis_index("col")
    recv[pl.ds(me, 1)] = tiles_ref[pl.ds(me, 1)]
    barrier = pltpu.get_barrier_semaphore()

    def greet(k, carry):
        peer = lax.rem(me + k, count)
        pl.semaphore_signal(barrier, inc=1, device_id=(peer, col), device_id_type=pl.DeviceIdType.MESH)
        return carry

    lax.fori_loop(1, count, greet, 0)
    pl.semaphore_wait(barrier, count - 1)

    def copy_to(k):
        peer = lax.rem(me + k, count)
        return pltpu.make_async_remote_copy(
            src_ref=tiles_ref.at[pl.ds(peer, 1)],
            dst_ref=recv.at[pl.ds(me, 1)],
            send_sem=send_sem.at[peer],
            recv_sem=recv_sem.at[me],
            device_id=(peer, col),
            device_id_type=pl.DeviceIdType.MESH,
        )

    def send(k, carry):
        copy_to(k).start()
        return carry

    lax.fori_loop(1, count, send, 0)

    def finish(k, carry):
        peer = lax.rem(me + k, count)
        copy_to(k).wait_send()
        pltpu.make_async_remote_copy(
            src_ref=tiles_ref.at[pl.ds(me, 1)],
            dst_ref=recv.at[pl.ds(peer, 1)],
            send_sem=send_sem.at[me],
            recv_sem=recv_sem.at[peer],
            device_id=(peer, col),
            device_id_type=pl.DeviceIdType.MESH,
        ).wait_recv()
        return carry

    lax.fori_loop(1, count, finish, 0)
    out_ref[...] = jnp.sum(recv[...], axis=0, keepdims=True)


def scatter_sum(tiles):
    count, rows, lanes = tiles.shape
    return pl.pallas_call(
        scatter_sum_kernel,
        out_shape=jax.ShapeDtypeStruct((1, rows, lanes), jnp.float32),
        in_specs=[pl.BlockSpec(memory_space=pltpu.VMEM)],
        out_specs=pl.BlockSpec(memory_space=pltpu.VMEM),
        scratch_shapes=[
            pltpu.VMEM((count, rows, lanes), jnp.float32),
            pltpu.SemaphoreType.DMA((count,)),
            pltpu.SemaphoreType.DMA((count,)),
        ],
        compiler_params=pltpu.CompilerParams(collective_id=0, has_side_effects=True),
    )(tiles)


def gram_kernel(a_ref, b_ref, out_ref):
    @pl.when((pl.program_id(0) == 0) & (pl.program_id(1) == 0))
    def _():
        out_ref[...] = jnp.zeros_like(out_ref)

    total = out_ref[...]
    for row in range(a_ref.shape[2]):
        total = total + lax.dot_general(
            a_ref[:, 0, row, :],
            b_ref[:, 0, row, :],
            (((1,), (1,)), ((), ())),
            precision=lax.Precision.HIGHEST,
            preferred_element_type=jnp.float32,
        )
    out_ref[...] = total


def gram(a, b, rows_per_step=8):
    count, depth, rows, lanes = a.shape
    spec = pl.BlockSpec((count, 1, rows_per_step, lanes), lambda i, j: (0, i, j, 0))
    return pl.pallas_call(
        gram_kernel,
        grid=(depth, rows // rows_per_step),
        in_specs=[spec, spec],
        out_specs=pl.BlockSpec((count, count), lambda i, j: (0, 0)),
        out_shape=jax.ShapeDtypeStruct((count, count), jnp.float32),
        cost_estimate=pl.CostEstimate(
            flops=2 * count * count * a.size // count, bytes_accessed=8 * a.size, transcendentals=0
        ),
    )(a, b)


def lookup(region_ids, region_cond):
    summed = jnp.zeros(region_ids.shape, jnp.float32)
    for region in range(region_cond.shape[0]):
        summed = summed + jnp.where(region_ids == region, region_cond[region], jnp.float32(0.0))
    return summed


def halo_pair(block, axis, dim):
    count = lax.axis_size(axis)
    forward = [(i, i + 1) for i in range(count - 1)]
    backward = [(target, source) for source, target in forward]
    size = block.shape[dim]
    low = lax.ppermute(lax.slice_in_dim(block, size - 1, None, axis=dim), axis, forward)
    high = lax.ppermute(lax.slice_in_dim(block, 0, 1, axis=dim), axis, backward)
    return low, high


def shifted(block, low, high, dim):
    size = block.shape[dim]
    ahead = jnp.concatenate([lax.slice_in_dim(block, 1, None, axis=dim), high], axis=dim)
    behind = jnp.concatenate([low, lax.slice_in_dim(block, 0, size - 1, axis=dim)], axis=dim)
    return ahead, behind


def coefficients(cond_xy):
    cond_mid = cond_xy[1:-1, 1:-1]
    kxp = 0.5 * (cond_mid + cond_xy[2:, 1:-1])
    kxm = 0.5 * (cond_mid + cond_xy[:-2, 1:-1])
    kyp = 0.5 * (cond_mid + cond_xy[1:-1, 2:])
    kym = 0.5 * (cond_mid + cond_xy[1:-1, :-2])
    cond_z = jnp.pad(cond_mid, ((0, 0), (0, 0), (1, 1)))
    kzp = 0.5 * (cond_mid + cond_z[:, :, 2:])
    kzm = 0.5 * (cond_mid + cond_z[:, :, :-2])
    return (kxp, kxm, kyp, kym, kzp, kzm)


def windows(block, rows, count):
    parts = [lax.slice_in_dim(block, c * rows, (c + 1) * rows, axis=2) for c in range(count)]
    received = lax.all_to_all(jnp.stack(parts), "col", 0, 0, tiled=True)
    return received.reshape((-1,) + received.shape[2:])


def conduction(field, coeffs):
    kxp, kxm, kyp, kym, kzp, kzm = coeffs
    xlo, xhi = halo_pair(field, "slab", 1)
    ylo, yhi = halo_pair(field, "col", 2)
    nxp, nxm = shifted(field, xlo, xhi, 1)
    nyp, nym = shifted(field, ylo, yhi, 2)
    field_z = jnp.pad(field, ((0, 0), (0, 0), (0, 0), (1, 1)))
    summed = kxp * (field - nxp)
    summed = summed + kxm * (field - nxm)
    summed = summed + kyp * (field - nyp)
    summed = summed + kym * (field - nym)
    summed = summed + kzp * (field - field_z[..., 2:])
    summed = summed + kzm * (field - field_z[..., :-2])
    return summed


def bounds(shift_val, cond_max):
    high_eig = shift_val + 12.0 * cond_max
    mid_eig = 0.5 * (high_eig + shift_val)
    half_span = 0.5 * (high_eig - shift_val)
    return (mid_eig, half_span, mid_eig / half_span)


def solve_slabs(right_side, shift_val, cond_max, coeffs):
    mid_eig, half_span, ratio_eig = bounds(shift_val, cond_max)
    rho_now = 1.0 / ratio_eig
    solution = jnp.zeros_like(right_side)
    residual = right_side
    direction = right_side / mid_eig
    for sweep_idx in range(STEPS - 1):
        solution = solution + direction
        applied = conduction(direction, coeffs) + shift_val * direction
        residual = residual - applied
        rho_next = 1.0 / (2.0 * ratio_eig - rho_now)
        direction = rho_next * rho_now * direction + 2.0 * rho_next / half_span * residual
        rho_now = rho_next
    return solution + direction


def run_segments(stacked, shifts, solver):
    factors = []
    current = stacked
    for segment_idx in range(ADI):
        shift_val = shifts[segment_idx]
        if segment_idx == 0:
            current = solver(stacked, shift_val)
        else:
            current = current - (shifts[segment_idx - 1] + shift_val) * solver(current, shift_val)
        factors.append(jnp.sqrt(2.0 * shift_val) * current)
    return jnp.stack(factors)


def body(input_map, output_map, region_ids, region_cond, shift_ids):
    col_count = lax.axis_size("col")
    ctrl_in = windows(input_map, input_map.shape[2] // col_count, col_count)
    obsv_in = windows(output_map, output_map.shape[2] // col_count, col_count)
    col_local = ctrl_in.shape[0]
    rows = ctrl_in.shape[2]
    local_x = input_map.shape[1]
    cond_cells = lookup(region_ids, region_cond)
    cond_max = jnp.max(region_cond)
    shifts = 0.25 * jnp.exp2(shift_ids.astype(jnp.float32))
    total_x = local_x * lax.axis_size("slab")
    cond_ypad = jnp.pad(cond_cells, ((0, 0), (1, 1), (0, 0)))
    cond_y = lax.dynamic_slice_in_dim(cond_ypad, lax.axis_index("col") * rows, rows + 2, axis=1)
    cond_xy = extended(cond_y, (("slab", 0),), 1)
    coeffs = coefficients(cond_xy)
    solver = lambda rhs, shift_val: solve_slabs(rhs, shift_val, cond_max, coeffs)
    ctrl_cols = run_segments(ctrl_in, shifts, solver)
    obsv_cols = run_segments(obsv_in, shifts, solver)
    row_count = ctrl_cols.shape[0] * ctrl_cols.shape[1]
    partial_value = gram(
        ctrl_cols.reshape((row_count,) + ctrl_cols.shape[2:]),
        obsv_cols.reshape((row_count,) + obsv_cols.shape[2:]),
    )
    cells_total = total_x * region_ids.shape[1] * region_ids.shape[2]
    norm_scale = 1.0 / math.sqrt(cells_total)
    slab_count = lax.axis_size("slab")
    col_count = lax.axis_size("col")
    tile_rows = row_count // slab_count
    tile_cols = row_count // col_count
    col_parts = partial_value.reshape(row_count, col_count, tile_cols).transpose(1, 0, 2)
    col_sum = jnp.sum(lax.all_to_all(col_parts, "col", 0, 0, tiled=True), axis=0)
    row_parts = col_sum.reshape(slab_count, 1, tile_rows * tile_cols)
    own_tile = scatter_sum(row_parts).reshape(tile_rows, tile_cols)
    return (ctrl_cols, obsv_cols, own_tile * norm_scale)


def solution(mesh):
    placed = (
        P("col", "slab", None, None),
        P("col", "slab", None, None),
        P("slab", None, None),
        P(),
        P(),
    )
    return jax.shard_map(
        body,
        mesh=mesh,
        in_specs=placed,
        out_specs=(
            P(None, None, "slab", "col", None),
            P(None, None, "slab", "col", None),
            P("slab", "col"),
        ),
        check_vma=False,
    )
```

```python
import math

import jax
import jax.numpy as jnp
from jax import lax
from jax.experimental import pallas as pl
from jax.experimental.pallas import tpu as pltpu
from jax.sharding import PartitionSpec as P

ADI = 2
STEPS = 3


def extended(block, sides, width):
    for axis, dim in sides:
        count = lax.axis_size(axis)
        forward = [(i, i + 1) for i in range(count - 1)]
        backward = [(target, source) for source, target in forward]
        low = lax.ppermute(
            lax.slice_in_dim(block, block.shape[dim] - width, None, axis=dim), axis, forward
        )
        high = lax.ppermute(lax.slice_in_dim(block, 0, width, axis=dim), axis, backward)
        block = jnp.concatenate([low, block, high], axis=dim)
    return block


def scatter_sum_kernel(tiles_ref, out_ref, recv, send_sem, recv_sem):
    count = tiles_ref.shape[0]
    me = lax.axis_index("slab")
    col = lax.axis_index("col")
    recv[pl.ds(me, 1)] = tiles_ref[pl.ds(me, 1)]
    barrier = pltpu.get_barrier_semaphore()

    def greet(k, carry):
        peer = lax.rem(me + k, count)
        pl.semaphore_signal(barrier, inc=1, device_id=(peer, col), device_id_type=pl.DeviceIdType.MESH)
        return carry

    lax.fori_loop(1, count, greet, 0)
    pl.semaphore_wait(barrier, count - 1)

    def copy_to(k):
        peer = lax.rem(me + k, count)
        return pltpu.make_async_remote_copy(
            src_ref=tiles_ref.at[pl.ds(peer, 1)],
            dst_ref=recv.at[pl.ds(me, 1)],
            send_sem=send_sem.at[peer],
            recv_sem=recv_sem.at[me],
            device_id=(peer, col),
            device_id_type=pl.DeviceIdType.MESH,
        )

    def send(k, carry):
        copy_to(k).start()
        return carry

    lax.fori_loop(1, count, send, 0)

    def finish(k, carry):
        peer = lax.rem(me + k, count)
        copy_to(k).wait_send()
        pltpu.make_async_remote_copy(
            src_ref=tiles_ref.at[pl.ds(me, 1)],
            dst_ref=recv.at[pl.ds(peer, 1)],
            send_sem=send_sem.at[me],
            recv_sem=recv_sem.at[peer],
            device_id=(peer, col),
            device_id_type=pl.DeviceIdType.MESH,
        ).wait_recv()
        return carry

    lax.fori_loop(1, count, finish, 0)
    out_ref[...] = jnp.sum(recv[...], axis=0, keepdims=True)


def scatter_sum(tiles):
    count, rows, lanes = tiles.shape
    return pl.pallas_call(
        scatter_sum_kernel,
        out_shape=jax.ShapeDtypeStruct((1, rows, lanes), jnp.float32),
        in_specs=[pl.BlockSpec(memory_space=pltpu.VMEM)],
        out_specs=pl.BlockSpec(memory_space=pltpu.VMEM),
        scratch_shapes=[
            pltpu.VMEM((count, rows, lanes), jnp.float32),
            pltpu.SemaphoreType.DMA((count,)),
            pltpu.SemaphoreType.DMA((count,)),
        ],
        compiler_params=pltpu.CompilerParams(collective_id=0, has_side_effects=True),
    )(tiles)


def gram_kernel(a_ref, b_ref, out_ref):
    @pl.when((pl.program_id(0) == 0) & (pl.program_id(1) == 0))
    def _():
        out_ref[...] = jnp.zeros_like(out_ref)

    rows = a_ref.shape[2]
    left = jnp.concatenate([a_ref[:, 0, row, :] for row in range(rows)], axis=1)
    right = jnp.concatenate([b_ref[:, 0, row, :] for row in range(rows)], axis=1)
    out_ref[...] += lax.dot_general(
        left,
        right,
        (((1,), (1,)), ((), ())),
        precision=lax.Precision.HIGHEST,
        preferred_element_type=jnp.float32,
    )


def gram(a, b, rows_per_step=16):
    count, depth, rows, lanes = a.shape
    spec = pl.BlockSpec((count, 1, rows_per_step, lanes), lambda i, j: (0, i, j, 0))
    return pl.pallas_call(
        gram_kernel,
        grid=(depth, rows // rows_per_step),
        in_specs=[spec, spec],
        out_specs=pl.BlockSpec((count, count), lambda i, j: (0, 0)),
        out_shape=jax.ShapeDtypeStruct((count, count), jnp.float32),
        cost_estimate=pl.CostEstimate(
            flops=2 * count * count * a.size // count, bytes_accessed=8 * a.size, transcendentals=0
        ),
    )(a, b)


def lookup(region_ids, region_cond):
    summed = jnp.zeros(region_ids.shape, jnp.float32)
    for region in range(region_cond.shape[0]):
        summed = summed + jnp.where(region_ids == region, region_cond[region], jnp.float32(0.0))
    return summed


def halo_pair(block, axis, dim):
    count = lax.axis_size(axis)
    forward = [(i, i + 1) for i in range(count - 1)]
    backward = [(target, source) for source, target in forward]
    size = block.shape[dim]
    low = lax.ppermute(lax.slice_in_dim(block, size - 1, None, axis=dim), axis, forward)
    high = lax.ppermute(lax.slice_in_dim(block, 0, 1, axis=dim), axis, backward)
    return low, high


def shifted(block, low, high, dim):
    size = block.shape[dim]
    ahead = jnp.concatenate([lax.slice_in_dim(block, 1, None, axis=dim), high], axis=dim)
    behind = jnp.concatenate([low, lax.slice_in_dim(block, 0, size - 1, axis=dim)], axis=dim)
    return ahead, behind


def coefficients(cond_xy):
    cond_mid = cond_xy[1:-1, 1:-1]
    kxp = 0.5 * (cond_mid + cond_xy[2:, 1:-1])
    kxm = 0.5 * (cond_mid + cond_xy[:-2, 1:-1])
    kyp = 0.5 * (cond_mid + cond_xy[1:-1, 2:])
    kym = 0.5 * (cond_mid + cond_xy[1:-1, :-2])
    cond_z = jnp.pad(cond_mid, ((0, 0), (0, 0), (1, 1)))
    kzp = 0.5 * (cond_mid + cond_z[:, :, 2:])
    kzm = 0.5 * (cond_mid + cond_z[:, :, :-2])
    return (kxp, kxm, kyp, kym, kzp, kzm)


def windows(block, rows, count):
    parts = [lax.slice_in_dim(block, c * rows, (c + 1) * rows, axis=2) for c in range(count)]
    received = lax.all_to_all(jnp.stack(parts), "col", 0, 0, tiled=True)
    return received.reshape((-1,) + received.shape[2:])


def conduction(field, coeffs):
    kxp, kxm, kyp, kym, kzp, kzm = coeffs
    xlo, xhi = halo_pair(field, "slab", 1)
    ylo, yhi = halo_pair(field, "col", 2)
    nxp, nxm = shifted(field, xlo, xhi, 1)
    nyp, nym = shifted(field, ylo, yhi, 2)
    field_z = jnp.pad(field, ((0, 0), (0, 0), (0, 0), (1, 1)))
    summed = kxp * (field - nxp)
    summed = summed + kxm * (field - nxm)
    summed = summed + kyp * (field - nyp)
    summed = summed + kym * (field - nym)
    summed = summed + kzp * (field - field_z[..., 2:])
    summed = summed + kzm * (field - field_z[..., :-2])
    return summed


def bounds(shift_val, cond_max):
    high_eig = shift_val + 12.0 * cond_max
    mid_eig = 0.5 * (high_eig + shift_val)
    half_span = 0.5 * (high_eig - shift_val)
    return (mid_eig, half_span, mid_eig / half_span)


def solve_slabs(right_side, shift_val, cond_max, coeffs):
    mid_eig, half_span, ratio_eig = bounds(shift_val, cond_max)
    rho_now = 1.0 / ratio_eig
    solution = jnp.zeros_like(right_side)
    residual = right_side
    direction = right_side / mid_eig
    for sweep_idx in range(STEPS - 1):
        solution = solution + direction
        applied = conduction(direction, coeffs) + shift_val * direction
        residual = residual - applied
        rho_next = 1.0 / (2.0 * ratio_eig - rho_now)
        direction = rho_next * rho_now * direction + 2.0 * rho_next / half_span * residual
        rho_now = rho_next
    return solution + direction


def run_segments(stacked, shifts, solver):
    factors = []
    current = stacked
    for segment_idx in range(ADI):
        shift_val = shifts[segment_idx]
        if segment_idx == 0:
            current = solver(stacked, shift_val)
        else:
            current = current - (shifts[segment_idx - 1] + shift_val) * solver(current, shift_val)
        factors.append(jnp.sqrt(2.0 * shift_val) * current)
    return jnp.stack(factors)


def body(input_map, output_map, region_ids, region_cond, shift_ids):
    col_count = lax.axis_size("col")
    ctrl_in = windows(input_map, input_map.shape[2] // col_count, col_count)
    obsv_in = windows(output_map, output_map.shape[2] // col_count, col_count)
    col_local = ctrl_in.shape[0]
    rows = ctrl_in.shape[2]
    local_x = input_map.shape[1]
    cond_cells = lookup(region_ids, region_cond)
    cond_max = jnp.max(region_cond)
    shifts = 0.25 * jnp.exp2(shift_ids.astype(jnp.float32))
    total_x = local_x * lax.axis_size("slab")
    cond_ypad = jnp.pad(cond_cells, ((0, 0), (1, 1), (0, 0)))
    cond_y = lax.dynamic_slice_in_dim(cond_ypad, lax.axis_index("col") * rows, rows + 2, axis=1)
    cond_xy = extended(cond_y, (("slab", 0),), 1)
    coeffs = coefficients(cond_xy)
    solver = lambda rhs, shift_val: solve_slabs(rhs, shift_val, cond_max, coeffs)
    ctrl_cols = run_segments(ctrl_in, shifts, solver)
    obsv_cols = run_segments(obsv_in, shifts, solver)
    row_count = ctrl_cols.shape[0] * ctrl_cols.shape[1]
    partial_value = gram(
        ctrl_cols.reshape((row_count,) + ctrl_cols.shape[2:]),
        obsv_cols.reshape((row_count,) + obsv_cols.shape[2:]),
    )
    cells_total = total_x * region_ids.shape[1] * region_ids.shape[2]
    norm_scale = 1.0 / math.sqrt(cells_total)
    slab_count = lax.axis_size("slab")
    col_count = lax.axis_size("col")
    tile_rows = row_count // slab_count
    tile_cols = row_count // col_count
    col_parts = partial_value.reshape(row_count, col_count, tile_cols).transpose(1, 0, 2)
    col_sum = jnp.sum(lax.all_to_all(col_parts, "col", 0, 0, tiled=True), axis=0)
    row_parts = col_sum.reshape(slab_count, 1, tile_rows * tile_cols)
    own_tile = scatter_sum(row_parts).reshape(tile_rows, tile_cols)
    return (ctrl_cols, obsv_cols, own_tile * norm_scale)


def solution(mesh):
    placed = (
        P("col", "slab", None, None),
        P("col", "slab", None, None),
        P("slab", None, None),
        P(),
        P(),
    )
    return jax.shard_map(
        body,
        mesh=mesh,
        in_specs=placed,
        out_specs=(
            P(None, None, "slab", "col", None),
            P(None, None, "slab", "col", None),
            P("slab", "col"),
        ),
        check_vma=False,
    )
```

```python
import math

import jax
import jax.numpy as jnp
from jax import lax
from jax.experimental import pallas as pl
from jax.experimental.pallas import tpu as pltpu
from jax.sharding import PartitionSpec as P

ADI = 2
STEPS = 3


def extended(block, sides, width):
    for axis, dim in sides:
        count = lax.axis_size(axis)
        forward = [(i, i + 1) for i in range(count - 1)]
        backward = [(target, source) for source, target in forward]
        low = lax.ppermute(
            lax.slice_in_dim(block, block.shape[dim] - width, None, axis=dim), axis, forward
        )
        high = lax.ppermute(lax.slice_in_dim(block, 0, width, axis=dim), axis, backward)
        block = jnp.concatenate([low, block, high], axis=dim)
    return block


def reduce_kernel(tiles_ref, out_ref, recv1, stage, recv2, send1, rsem1, send2, rsem2):
    ncol = tiles_ref.shape[0]
    nslab = recv2.shape[0]
    my_slab = lax.axis_index("slab")
    my_col = lax.axis_index("col")
    mesh = pl.DeviceIdType.MESH
    recv1[pl.ds(my_col, 1)] = tiles_ref[pl.ds(my_col, 1)]
    barrier = pltpu.get_barrier_semaphore()
    for k in range(1, ncol):
        peer = lax.rem(my_col + k, ncol)
        pl.semaphore_signal(barrier, inc=1, device_id=(my_slab, peer), device_id_type=mesh)

    def greet(k, carry):
        peer = lax.rem(my_slab + k, nslab)
        pl.semaphore_signal(barrier, inc=1, device_id=(peer, my_col), device_id_type=mesh)
        return carry

    lax.fori_loop(1, nslab, greet, 0)
    pl.semaphore_wait(barrier, ncol - 1 + nslab - 1)

    def col_copy(peer, src, dst):
        return pltpu.make_async_remote_copy(
            src_ref=tiles_ref.at[pl.ds(src, 1)],
            dst_ref=recv1.at[pl.ds(dst, 1)],
            send_sem=send1.at[src],
            recv_sem=rsem1.at[dst],
            device_id=(my_slab, peer),
            device_id_type=mesh,
        )

    for k in range(1, ncol):
        peer = lax.rem(my_col + k, ncol)
        col_copy(peer, peer, my_col).start()
    for k in range(1, ncol):
        peer = lax.rem(my_col + k, ncol)
        col_copy(peer, peer, my_col).wait_send()
        col_copy(peer, my_col, peer).wait_recv()
    summed = jnp.sum(recv1[...], axis=0)
    for k in range(nslab):
        stage[k] = summed[k:k + 1]
    recv2[pl.ds(my_slab, 1)] = stage[pl.ds(my_slab, 1)]

    def slab_copy(peer, src, dst):
        return pltpu.make_async_remote_copy(
            src_ref=stage.at[pl.ds(src, 1)],
            dst_ref=recv2.at[pl.ds(dst, 1)],
            send_sem=send2.at[src],
            recv_sem=rsem2.at[dst],
            device_id=(peer, my_col),
            device_id_type=mesh,
        )

    def send(k, carry):
        peer = lax.rem(my_slab + k, nslab)
        slab_copy(peer, peer, my_slab).start()
        return carry

    lax.fori_loop(1, nslab, send, 0)

    def finish(k, carry):
        peer = lax.rem(my_slab + k, nslab)
        slab_copy(peer, peer, my_slab).wait_send()
        slab_copy(peer, my_slab, peer).wait_recv()
        return carry

    lax.fori_loop(1, nslab, finish, 0)
    out_ref[...] = jnp.sum(recv2[...], axis=0, keepdims=True)


def reduce_scatter(tiles, nslab):
    ncol, rows, lanes = tiles.shape
    return pl.pallas_call(
        reduce_kernel,
        out_shape=jax.ShapeDtypeStruct((1, 1, lanes), jnp.float32),
        in_specs=[pl.BlockSpec(memory_space=pltpu.VMEM)],
        out_specs=pl.BlockSpec(memory_space=pltpu.VMEM),
        scratch_shapes=[
            pltpu.VMEM((ncol, rows, lanes), jnp.float32),
            pltpu.VMEM((nslab, 1, lanes), jnp.float32),
            pltpu.VMEM((nslab, 1, lanes), jnp.float32),
            pltpu.SemaphoreType.DMA((ncol,)),
            pltpu.SemaphoreType.DMA((ncol,)),
            pltpu.SemaphoreType.DMA((nslab,)),
            pltpu.SemaphoreType.DMA((nslab,)),
        ],
        compiler_params=pltpu.CompilerParams(collective_id=0, has_side_effects=True),
    )(tiles)


def gram_kernel(a_ref, b_ref, out_ref):
    @pl.when((pl.program_id(0) == 0) & (pl.program_id(1) == 0))
    def _():
        out_ref[...] = jnp.zeros_like(out_ref)

    rows = a_ref.shape[2]
    left = jnp.concatenate([a_ref[:, 0, row, :] for row in range(rows)], axis=1)
    right = jnp.concatenate([b_ref[:, 0, row, :] for row in range(rows)], axis=1)
    out_ref[...] += lax.dot_general(
        left,
        right,
        (((1,), (1,)), ((), ())),
        precision=lax.Precision.HIGHEST,
        preferred_element_type=jnp.float32,
    )


def gram(a, b, rows_per_step=16):
    count, depth, rows, lanes = a.shape
    spec = pl.BlockSpec((count, 1, rows_per_step, lanes), lambda i, j: (0, i, j, 0))
    return pl.pallas_call(
        gram_kernel,
        grid=(depth, rows // rows_per_step),
        in_specs=[spec, spec],
        out_specs=pl.BlockSpec((count, count), lambda i, j: (0, 0)),
        out_shape=jax.ShapeDtypeStruct((count, count), jnp.float32),
        cost_estimate=pl.CostEstimate(
            flops=2 * count * count * a.size // count, bytes_accessed=8 * a.size, transcendentals=0
        ),
    )(a, b)


def lookup(region_ids, region_cond):
    summed = jnp.zeros(region_ids.shape, jnp.float32)
    for region in range(region_cond.shape[0]):
        summed = summed + jnp.where(region_ids == region, region_cond[region], jnp.float32(0.0))
    return summed


def halo_pair(block, axis, dim):
    count = lax.axis_size(axis)
    forward = [(i, i + 1) for i in range(count - 1)]
    backward = [(target, source) for source, target in forward]
    size = block.shape[dim]
    low = lax.ppermute(lax.slice_in_dim(block, size - 1, None, axis=dim), axis, forward)
    high = lax.ppermute(lax.slice_in_dim(block, 0, 1, axis=dim), axis, backward)
    return low, high


def shifted(block, low, high, dim):
    size = block.shape[dim]
    ahead = jnp.concatenate([lax.slice_in_dim(block, 1, None, axis=dim), high], axis=dim)
    behind = jnp.concatenate([low, lax.slice_in_dim(block, 0, size - 1, axis=dim)], axis=dim)
    return ahead, behind


def coefficients(cond_xy):
    cond_mid = cond_xy[1:-1, 1:-1]
    kxp = 0.5 * (cond_mid + cond_xy[2:, 1:-1])
    kxm = 0.5 * (cond_mid + cond_xy[:-2, 1:-1])
    kyp = 0.5 * (cond_mid + cond_xy[1:-1, 2:])
    kym = 0.5 * (cond_mid + cond_xy[1:-1, :-2])
    cond_z = jnp.pad(cond_mid, ((0, 0), (0, 0), (1, 1)))
    kzp = 0.5 * (cond_mid + cond_z[:, :, 2:])
    kzm = 0.5 * (cond_mid + cond_z[:, :, :-2])
    return (kxp, kxm, kyp, kym, kzp, kzm)


def windows(block, rows, count):
    parts = [lax.slice_in_dim(block, c * rows, (c + 1) * rows, axis=2) for c in range(count)]
    received = lax.all_to_all(jnp.stack(parts), "col", 0, 0, tiled=True)
    return received.reshape((-1,) + received.shape[2:])


def conduction(field, coeffs):
    kxp, kxm, kyp, kym, kzp, kzm = coeffs
    xlo, xhi = halo_pair(field, "slab", 1)
    ylo, yhi = halo_pair(field, "col", 2)
    nxp, nxm = shifted(field, xlo, xhi, 1)
    nyp, nym = shifted(field, ylo, yhi, 2)
    field_z = jnp.pad(field, ((0, 0), (0, 0), (0, 0), (1, 1)))
    summed = kxp * (field - nxp)
    summed = summed + kxm * (field - nxm)
    summed = summed + kyp * (field - nyp)
    summed = summed + kym * (field - nym)
    summed = summed + kzp * (field - field_z[..., 2:])
    summed = summed + kzm * (field - field_z[..., :-2])
    return summed


def bounds(shift_val, cond_max):
    high_eig = shift_val + 12.0 * cond_max
    mid_eig = 0.5 * (high_eig + shift_val)
    half_span = 0.5 * (high_eig - shift_val)
    return (mid_eig, half_span, mid_eig / half_span)


def solve_slabs(right_side, shift_val, cond_max, coeffs):
    mid_eig, half_span, ratio_eig = bounds(shift_val, cond_max)
    rho_now = 1.0 / ratio_eig
    solution = jnp.zeros_like(right_side)
    residual = right_side
    direction = right_side / mid_eig
    for sweep_idx in range(STEPS - 1):
        solution = solution + direction
        applied = conduction(direction, coeffs) + shift_val * direction
        residual = residual - applied
        rho_next = 1.0 / (2.0 * ratio_eig - rho_now)
        direction = rho_next * rho_now * direction + 2.0 * rho_next / half_span * residual
        rho_now = rho_next
    return solution + direction


def run_segments(stacked, shifts, solver):
    factors = []
    current = stacked
    for segment_idx in range(ADI):
        shift_val = shifts[segment_idx]
        if segment_idx == 0:
            current = solver(stacked, shift_val)
        else:
            current = current - (shifts[segment_idx - 1] + shift_val) * solver(current, shift_val)
        factors.append(jnp.sqrt(2.0 * shift_val) * current)
    return jnp.stack(factors)


def body(input_map, output_map, region_ids, region_cond, shift_ids):
    col_count = lax.axis_size("col")
    ctrl_in = windows(input_map, input_map.shape[2] // col_count, col_count)
    obsv_in = windows(output_map, output_map.shape[2] // col_count, col_count)
    col_local = ctrl_in.shape[0]
    rows = ctrl_in.shape[2]
    local_x = input_map.shape[1]
    cond_cells = lookup(region_ids, region_cond)
    cond_max = jnp.max(region_cond)
    shifts = 0.25 * jnp.exp2(shift_ids.astype(jnp.float32))
    total_x = local_x * lax.axis_size("slab")
    cond_ypad = jnp.pad(cond_cells, ((0, 0), (1, 1), (0, 0)))
    cond_y = lax.dynamic_slice_in_dim(cond_ypad, lax.axis_index("col") * rows, rows + 2, axis=1)
    cond_xy = extended(cond_y, (("slab", 0),), 1)
    coeffs = coefficients(cond_xy)
    solver = lambda rhs, shift_val: solve_slabs(rhs, shift_val, cond_max, coeffs)
    ctrl_cols = run_segments(ctrl_in, shifts, solver)
    obsv_cols = run_segments(obsv_in, shifts, solver)
    row_count = ctrl_cols.shape[0] * ctrl_cols.shape[1]
    partial_value = gram(
        ctrl_cols.reshape((row_count,) + ctrl_cols.shape[2:]),
        obsv_cols.reshape((row_count,) + obsv_cols.shape[2:]),
    )
    cells_total = total_x * region_ids.shape[1] * region_ids.shape[2]
    norm_scale = 1.0 / math.sqrt(cells_total)
    slab_count = lax.axis_size("slab")
    col_count = lax.axis_size("col")
    tile_rows = row_count // slab_count
    tile_cols = row_count // col_count
    tiles = partial_value.reshape(row_count, col_count, tile_cols).transpose(1, 0, 2)
    tiles = tiles.reshape(col_count, slab_count, tile_rows * tile_cols)
    own_tile = reduce_scatter(tiles, slab_count).reshape(tile_rows, tile_cols)
    return (ctrl_cols, obsv_cols, own_tile * norm_scale)


def solution(mesh):
    placed = (
        P("col", "slab", None, None),
        P("col", "slab", None, None),
        P("slab", None, None),
        P(),
        P(),
    )
    return jax.shard_map(
        body,
        mesh=mesh,
        in_specs=placed,
        out_specs=(
            P(None, None, "slab", "col", None),
            P(None, None, "slab", "col", None),
            P("slab", "col"),
        ),
        check_vma=False,
    )
```

```python
import math

import jax
import jax.numpy as jnp
from jax import lax
from jax.experimental import pallas as pl
from jax.experimental.pallas import tpu as pltpu
from jax.sharding import PartitionSpec as P

ADI = 2
STEPS = 3


def extended(block, sides, width):
    for axis, dim in sides:
        count = lax.axis_size(axis)
        forward = [(i, i + 1) for i in range(count - 1)]
        backward = [(target, source) for source, target in forward]
        low = lax.ppermute(
            lax.slice_in_dim(block, block.shape[dim] - width, None, axis=dim), axis, forward
        )
        high = lax.ppermute(lax.slice_in_dim(block, 0, width, axis=dim), axis, backward)
        block = jnp.concatenate([low, block, high], axis=dim)
    return block


def reduce_kernel(tiles_ref, out_ref, recv1, stage, recv2, send1, rsem1, send2, rsem2):
    ncol = tiles_ref.shape[0]
    nslab = recv2.shape[0]
    my_slab = lax.axis_index("slab")
    my_col = lax.axis_index("col")
    mesh = pl.DeviceIdType.MESH
    recv1[pl.ds(my_col, 1)] = tiles_ref[pl.ds(my_col, 1)]
    barrier = pltpu.get_barrier_semaphore()
    for k in range(1, ncol):
        peer = lax.rem(my_col + k, ncol)
        pl.semaphore_signal(barrier, inc=1, device_id=(my_slab, peer), device_id_type=mesh)

    def greet(k, carry):
        peer = lax.rem(my_slab + k, nslab)
        pl.semaphore_signal(barrier, inc=1, device_id=(peer, my_col), device_id_type=mesh)
        return carry

    lax.fori_loop(1, nslab, greet, 0)
    pl.semaphore_wait(barrier, ncol - 1 + nslab - 1)

    def col_copy(peer, src, dst):
        return pltpu.make_async_remote_copy(
            src_ref=tiles_ref.at[pl.ds(src, 1)],
            dst_ref=recv1.at[pl.ds(dst, 1)],
            send_sem=send1.at[src],
            recv_sem=rsem1.at[dst],
            device_id=(my_slab, peer),
            device_id_type=mesh,
        )

    for k in range(1, ncol):
        peer = lax.rem(my_col + k, ncol)
        col_copy(peer, peer, my_col).start()
    for k in range(1, ncol):
        peer = lax.rem(my_col + k, ncol)
        col_copy(peer, peer, my_col).wait_send()
        col_copy(peer, my_col, peer).wait_recv()
    summed = jnp.sum(recv1[...], axis=0)
    for k in range(nslab):
        stage[k] = summed[k:k + 1]
    recv2[pl.ds(my_slab, 1)] = stage[pl.ds(my_slab, 1)]

    def slab_copy(peer, src, dst):
        return pltpu.make_async_remote_copy(
            src_ref=stage.at[pl.ds(src, 1)],
            dst_ref=recv2.at[pl.ds(dst, 1)],
            send_sem=send2.at[src],
            recv_sem=rsem2.at[dst],
            device_id=(peer, my_col),
            device_id_type=mesh,
        )

    def send(k, carry):
        peer = lax.rem(my_slab + k, nslab)
        slab_copy(peer, peer, my_slab).start()
        return carry

    lax.fori_loop(1, nslab, send, 0)

    def finish(k, carry):
        peer = lax.rem(my_slab + k, nslab)
        slab_copy(peer, peer, my_slab).wait_send()
        slab_copy(peer, my_slab, peer).wait_recv()
        return carry

    lax.fori_loop(1, nslab, finish, 0)
    out_ref[...] = jnp.sum(recv2[...], axis=0, keepdims=True)


def reduce_scatter(tiles, nslab):
    ncol, rows, lanes = tiles.shape
    return pl.pallas_call(
        reduce_kernel,
        out_shape=jax.ShapeDtypeStruct((1, 1, lanes), jnp.float32),
        in_specs=[pl.BlockSpec(memory_space=pltpu.VMEM)],
        out_specs=pl.BlockSpec(memory_space=pltpu.VMEM),
        scratch_shapes=[
            pltpu.VMEM((ncol, rows, lanes), jnp.float32),
            pltpu.VMEM((nslab, 1, lanes), jnp.float32),
            pltpu.VMEM((nslab, 1, lanes), jnp.float32),
            pltpu.SemaphoreType.DMA((ncol,)),
            pltpu.SemaphoreType.DMA((ncol,)),
            pltpu.SemaphoreType.DMA((nslab,)),
            pltpu.SemaphoreType.DMA((nslab,)),
        ],
        compiler_params=pltpu.CompilerParams(collective_id=0, has_side_effects=True),
    )(tiles)


def gram_kernel(a_ref, b_ref, out_ref):
    @pl.when((pl.program_id(0) == 0) & (pl.program_id(1) == 0))
    def _():
        out_ref[...] = jnp.zeros_like(out_ref)

    rows = a_ref.shape[2]
    left = jnp.concatenate([a_ref[:, 0, row, :] for row in range(rows)], axis=1)
    right = jnp.concatenate([b_ref[:, 0, row, :] for row in range(rows)], axis=1)
    out_ref[...] += lax.dot_general(
        left,
        right,
        (((1,), (1,)), ((), ())),
        precision=lax.Precision.HIGH,
        preferred_element_type=jnp.float32,
    )


def gram(a, b, rows_per_step=16):
    count, depth, rows, lanes = a.shape
    spec = pl.BlockSpec((count, 1, rows_per_step, lanes), lambda i, j: (0, i, j, 0))
    return pl.pallas_call(
        gram_kernel,
        grid=(depth, rows // rows_per_step),
        in_specs=[spec, spec],
        out_specs=pl.BlockSpec((count, count), lambda i, j: (0, 0)),
        out_shape=jax.ShapeDtypeStruct((count, count), jnp.float32),
        cost_estimate=pl.CostEstimate(
            flops=2 * count * count * a.size // count, bytes_accessed=8 * a.size, transcendentals=0
        ),
    )(a, b)


def lookup(region_ids, region_cond):
    summed = jnp.zeros(region_ids.shape, jnp.float32)
    for region in range(region_cond.shape[0]):
        summed = summed + jnp.where(region_ids == region, region_cond[region], jnp.float32(0.0))
    return summed


def halo_pair(block, axis, dim):
    count = lax.axis_size(axis)
    forward = [(i, i + 1) for i in range(count - 1)]
    backward = [(target, source) for source, target in forward]
    size = block.shape[dim]
    low = lax.ppermute(lax.slice_in_dim(block, size - 1, None, axis=dim), axis, forward)
    high = lax.ppermute(lax.slice_in_dim(block, 0, 1, axis=dim), axis, backward)
    return low, high


def shifted(block, low, high, dim):
    size = block.shape[dim]
    ahead = jnp.concatenate([lax.slice_in_dim(block, 1, None, axis=dim), high], axis=dim)
    behind = jnp.concatenate([low, lax.slice_in_dim(block, 0, size - 1, axis=dim)], axis=dim)
    return ahead, behind


def coefficients(cond_xy):
    cond_mid = cond_xy[1:-1, 1:-1]
    kxp = 0.5 * (cond_mid + cond_xy[2:, 1:-1])
    kxm = 0.5 * (cond_mid + cond_xy[:-2, 1:-1])
    kyp = 0.5 * (cond_mid + cond_xy[1:-1, 2:])
    kym = 0.5 * (cond_mid + cond_xy[1:-1, :-2])
    cond_z = jnp.pad(cond_mid, ((0, 0), (0, 0), (1, 1)))
    kzp = 0.5 * (cond_mid + cond_z[:, :, 2:])
    kzm = 0.5 * (cond_mid + cond_z[:, :, :-2])
    return (kxp, kxm, kyp, kym, kzp, kzm)


def windows(block, rows, count):
    parts = [lax.slice_in_dim(block, c * rows, (c + 1) * rows, axis=2) for c in range(count)]
    received = lax.all_to_all(jnp.stack(parts), "col", 0, 0, tiled=True)
    return received.reshape((-1,) + received.shape[2:])


def conduction(field, coeffs):
    kxp, kxm, kyp, kym, kzp, kzm = coeffs
    xlo, xhi = halo_pair(field, "slab", 1)
    ylo, yhi = halo_pair(field, "col", 2)
    nxp, nxm = shifted(field, xlo, xhi, 1)
    nyp, nym = shifted(field, ylo, yhi, 2)
    field_z = jnp.pad(field, ((0, 0), (0, 0), (0, 0), (1, 1)))
    summed = kxp * (field - nxp)
    summed = summed + kxm * (field - nxm)
    summed = summed + kyp * (field - nyp)
    summed = summed + kym * (field - nym)
    summed = summed + kzp * (field - field_z[..., 2:])
    summed = summed + kzm * (field - field_z[..., :-2])
    return summed


def bounds(shift_val, cond_max):
    high_eig = shift_val + 12.0 * cond_max
    mid_eig = 0.5 * (high_eig + shift_val)
    half_span = 0.5 * (high_eig - shift_val)
    return (mid_eig, half_span, mid_eig / half_span)


def solve_slabs(right_side, shift_val, cond_max, coeffs):
    mid_eig, half_span, ratio_eig = bounds(shift_val, cond_max)
    rho_now = 1.0 / ratio_eig
    solution = jnp.zeros_like(right_side)
    residual = right_side
    direction = right_side / mid_eig
    for sweep_idx in range(STEPS - 1):
        solution = solution + direction
        applied = conduction(direction, coeffs) + shift_val * direction
        residual = residual - applied
        rho_next = 1.0 / (2.0 * ratio_eig - rho_now)
        direction = rho_next * rho_now * direction + 2.0 * rho_next / half_span * residual
        rho_now = rho_next
    return solution + direction


def run_segments(stacked, shifts, solver):
    factors = []
    current = stacked
    for segment_idx in range(ADI):
        shift_val = shifts[segment_idx]
        if segment_idx == 0:
            current = solver(stacked, shift_val)
        else:
            current = current - (shifts[segment_idx - 1] + shift_val) * solver(current, shift_val)
        factors.append(jnp.sqrt(2.0 * shift_val) * current)
    return jnp.stack(factors)


def body(input_map, output_map, region_ids, region_cond, shift_ids):
    col_count = lax.axis_size("col")
    ctrl_in = windows(input_map, input_map.shape[2] // col_count, col_count)
    obsv_in = windows(output_map, output_map.shape[2] // col_count, col_count)
    col_local = ctrl_in.shape[0]
    rows = ctrl_in.shape[2]
    local_x = input_map.shape[1]
    cond_cells = lookup(region_ids, region_cond)
    cond_max = jnp.max(region_cond)
    shifts = 0.25 * jnp.exp2(shift_ids.astype(jnp.float32))
    total_x = local_x * lax.axis_size("slab")
    cond_ypad = jnp.pad(cond_cells, ((0, 0), (1, 1), (0, 0)))
    cond_y = lax.dynamic_slice_in_dim(cond_ypad, lax.axis_index("col") * rows, rows + 2, axis=1)
    cond_xy = extended(cond_y, (("slab", 0),), 1)
    coeffs = coefficients(cond_xy)
    solver = lambda rhs, shift_val: solve_slabs(rhs, shift_val, cond_max, coeffs)
    ctrl_cols = run_segments(ctrl_in, shifts, solver)
    obsv_cols = run_segments(obsv_in, shifts, solver)
    row_count = ctrl_cols.shape[0] * ctrl_cols.shape[1]
    partial_value = gram(
        ctrl_cols.reshape((row_count,) + ctrl_cols.shape[2:]),
        obsv_cols.reshape((row_count,) + obsv_cols.shape[2:]),
    )
    cells_total = total_x * region_ids.shape[1] * region_ids.shape[2]
    norm_scale = 1.0 / math.sqrt(cells_total)
    slab_count = lax.axis_size("slab")
    col_count = lax.axis_size("col")
    tile_rows = row_count // slab_count
    tile_cols = row_count // col_count
    tiles = partial_value.reshape(row_count, col_count, tile_cols).transpose(1, 0, 2)
    tiles = tiles.reshape(col_count, slab_count, tile_rows * tile_cols)
    own_tile = reduce_scatter(tiles, slab_count).reshape(tile_rows, tile_cols)
    return (ctrl_cols, obsv_cols, own_tile * norm_scale)


def solution(mesh):
    placed = (
        P("col", "slab", None, None),
        P("col", "slab", None, None),
        P("slab", None, None),
        P(),
        P(),
    )
    return jax.shard_map(
        body,
        mesh=mesh,
        in_specs=placed,
        out_specs=(
            P(None, None, "slab", "col", None),
            P(None, None, "slab", "col", None),
            P("slab", "col"),
        ),
        check_vma=False,
    )
```

```python
import math

import jax
import jax.numpy as jnp
from jax import lax
from jax.experimental import pallas as pl
from jax.experimental.pallas import tpu as pltpu
from jax.sharding import PartitionSpec as P

ADI = 2
STEPS = 3


def extended(block, sides, width):
    for axis, dim in sides:
        count = lax.axis_size(axis)
        forward = [(i, i + 1) for i in range(count - 1)]
        backward = [(target, source) for source, target in forward]
        low = lax.ppermute(
            lax.slice_in_dim(block, block.shape[dim] - width, None, axis=dim), axis, forward
        )
        high = lax.ppermute(lax.slice_in_dim(block, 0, width, axis=dim), axis, backward)
        block = jnp.concatenate([low, block, high], axis=dim)
    return block


def reduce_kernel(tiles_ref, out_ref, recv1, stage, recv2, send1, rsem1, send2, rsem2):
    ncol = tiles_ref.shape[0]
    nslab = recv2.shape[0]
    my_slab = lax.axis_index("slab")
    my_col = lax.axis_index("col")
    mesh = pl.DeviceIdType.MESH
    recv1[pl.ds(my_col, 1)] = tiles_ref[pl.ds(my_col, 1)]
    barrier = pltpu.get_barrier_semaphore()
    for k in range(1, ncol):
        peer = lax.rem(my_col + k, ncol)
        pl.semaphore_signal(barrier, inc=1, device_id=(my_slab, peer), device_id_type=mesh)

    def greet(k, carry):
        peer = lax.rem(my_slab + k, nslab)
        pl.semaphore_signal(barrier, inc=1, device_id=(peer, my_col), device_id_type=mesh)
        return carry

    lax.fori_loop(1, nslab, greet, 0)
    pl.semaphore_wait(barrier, ncol - 1 + nslab - 1)

    def col_copy(peer, src, dst):
        return pltpu.make_async_remote_copy(
            src_ref=tiles_ref.at[pl.ds(src, 1)],
            dst_ref=recv1.at[pl.ds(dst, 1)],
            send_sem=send1.at[src],
            recv_sem=rsem1.at[dst],
            device_id=(my_slab, peer),
            device_id_type=mesh,
        )

    for k in range(1, ncol):
        peer = lax.rem(my_col + k, ncol)
        col_copy(peer, peer, my_col).start()
    for k in range(1, ncol):
        peer = lax.rem(my_col + k, ncol)
        col_copy(peer, peer, my_col).wait_send()
        col_copy(peer, my_col, peer).wait_recv()
    summed = jnp.sum(recv1[...], axis=0)
    for k in range(nslab):
        stage[k] = summed[k:k + 1]
    recv2[pl.ds(my_slab, 1)] = stage[pl.ds(my_slab, 1)]

    def slab_copy(peer, src, dst):
        return pltpu.make_async_remote_copy(
            src_ref=stage.at[pl.ds(src, 1)],
            dst_ref=recv2.at[pl.ds(dst, 1)],
            send_sem=send2.at[src],
            recv_sem=rsem2.at[dst],
            device_id=(peer, my_col),
            device_id_type=mesh,
        )

    def send(k, carry):
        peer = lax.rem(my_slab + k, nslab)
        slab_copy(peer, peer, my_slab).start()
        return carry

    lax.fori_loop(1, nslab, send, 0)

    def finish(k, carry):
        peer = lax.rem(my_slab + k, nslab)
        slab_copy(peer, peer, my_slab).wait_send()
        slab_copy(peer, my_slab, peer).wait_recv()
        return carry

    lax.fori_loop(1, nslab, finish, 0)
    out_ref[...] = jnp.sum(recv2[...], axis=0, keepdims=True)


def reduce_scatter(tiles, nslab):
    ncol, rows, lanes = tiles.shape
    return pl.pallas_call(
        reduce_kernel,
        out_shape=jax.ShapeDtypeStruct((1, 1, lanes), jnp.float32),
        in_specs=[pl.BlockSpec(memory_space=pltpu.VMEM)],
        out_specs=pl.BlockSpec(memory_space=pltpu.VMEM),
        scratch_shapes=[
            pltpu.VMEM((ncol, rows, lanes), jnp.float32),
            pltpu.VMEM((nslab, 1, lanes), jnp.float32),
            pltpu.VMEM((nslab, 1, lanes), jnp.float32),
            pltpu.SemaphoreType.DMA((ncol,)),
            pltpu.SemaphoreType.DMA((ncol,)),
            pltpu.SemaphoreType.DMA((nslab,)),
            pltpu.SemaphoreType.DMA((nslab,)),
        ],
        compiler_params=pltpu.CompilerParams(collective_id=0, has_side_effects=True),
    )(tiles)


def exchange_kernel(x_ref, o_ref, send_sem, recv_sem):
    ncol = o_ref.shape[0] // x_ref.shape[0]
    cols = x_ref.shape[0]
    rows = o_ref.shape[2]
    my_slab = lax.axis_index("slab")
    my_col = lax.axis_index("col")
    mesh = pl.DeviceIdType.MESH
    barrier = pltpu.get_barrier_semaphore()
    for k in range(1, ncol):
        peer = lax.rem(my_col + k, ncol)
        pl.semaphore_signal(barrier, inc=1, device_id=(my_slab, peer), device_id_type=mesh)
    pl.semaphore_wait(barrier, ncol - 1)

    def chunk_copy(peer, src, dst):
        return pltpu.make_async_remote_copy(
            src_ref=x_ref.at[:, :, pl.ds(pl.multiple_of(src * rows, 8), rows), :],
            dst_ref=o_ref.at[pl.ds(dst * cols, cols)],
            send_sem=send_sem.at[src],
            recv_sem=recv_sem.at[dst],
            device_id=(my_slab, peer),
            device_id_type=mesh,
        )

    for k in range(1, ncol):
        peer = lax.rem(my_col + k, ncol)
        chunk_copy(peer, peer, my_col).start()
    for k in range(1, ncol):
        peer = lax.rem(my_col + k, ncol)
        chunk_copy(peer, peer, my_col).wait_send()
        chunk_copy(peer, my_col, peer).wait_recv()


def exchange(block, ncol):
    cols, depth, rows, lanes = block.shape
    received = pl.pallas_call(
        exchange_kernel,
        out_shape=jax.ShapeDtypeStruct((cols * ncol, depth, rows // ncol, lanes), block.dtype),
        in_specs=[pl.BlockSpec(memory_space=pl.ANY)],
        out_specs=pl.BlockSpec(memory_space=pl.ANY),
        scratch_shapes=[pltpu.SemaphoreType.DMA((ncol,)), pltpu.SemaphoreType.DMA((ncol,))],
        compiler_params=pltpu.CompilerParams(collective_id=1, has_side_effects=True),
    )(block)
    me = lax.axis_index("col")
    own = lax.dynamic_slice_in_dim(block, me * (rows // ncol), rows // ncol, axis=2)
    return lax.dynamic_update_slice_in_dim(received, own, me * cols, axis=0)


def gram_kernel(a_ref, b_ref, out_ref):
    @pl.when((pl.program_id(0) == 0) & (pl.program_id(1) == 0))
    def _():
        out_ref[...] = jnp.zeros_like(out_ref)

    rows = a_ref.shape[2]
    left = jnp.concatenate([a_ref[:, 0, row, :] for row in range(rows)], axis=1)
    right = jnp.concatenate([b_ref[:, 0, row, :] for row in range(rows)], axis=1)
    out_ref[...] += lax.dot_general(
        left,
        right,
        (((1,), (1,)), ((), ())),
        precision=lax.Precision.HIGHEST,
        preferred_element_type=jnp.float32,
    )


def gram(a, b, rows_per_step=16):
    count, depth, rows, lanes = a.shape
    spec = pl.BlockSpec((count, 1, rows_per_step, lanes), lambda i, j: (0, i, j, 0))
    return pl.pallas_call(
        gram_kernel,
        grid=(depth, rows // rows_per_step),
        in_specs=[spec, spec],
        out_specs=pl.BlockSpec((count, count), lambda i, j: (0, 0)),
        out_shape=jax.ShapeDtypeStruct((count, count), jnp.float32),
        cost_estimate=pl.CostEstimate(
            flops=2 * count * count * a.size // count, bytes_accessed=8 * a.size, transcendentals=0
        ),
    )(a, b)


def lookup(region_ids, region_cond):
    summed = jnp.zeros(region_ids.shape, jnp.float32)
    for region in range(region_cond.shape[0]):
        summed = summed + jnp.where(region_ids == region, region_cond[region], jnp.float32(0.0))
    return summed


def halo_pair(block, axis, dim):
    count = lax.axis_size(axis)
    forward = [(i, i + 1) for i in range(count - 1)]
    backward = [(target, source) for source, target in forward]
    size = block.shape[dim]
    low = lax.ppermute(lax.slice_in_dim(block, size - 1, None, axis=dim), axis, forward)
    high = lax.ppermute(lax.slice_in_dim(block, 0, 1, axis=dim), axis, backward)
    return low, high


def shifted(block, low, high, dim):
    size = block.shape[dim]
    ahead = jnp.concatenate([lax.slice_in_dim(block, 1, None, axis=dim), high], axis=dim)
    behind = jnp.concatenate([low, lax.slice_in_dim(block, 0, size - 1, axis=dim)], axis=dim)
    return ahead, behind


def coefficients(cond_xy):
    cond_mid = cond_xy[1:-1, 1:-1]
    kxp = 0.5 * (cond_mid + cond_xy[2:, 1:-1])
    kxm = 0.5 * (cond_mid + cond_xy[:-2, 1:-1])
    kyp = 0.5 * (cond_mid + cond_xy[1:-1, 2:])
    kym = 0.5 * (cond_mid + cond_xy[1:-1, :-2])
    cond_z = jnp.pad(cond_mid, ((0, 0), (0, 0), (1, 1)))
    kzp = 0.5 * (cond_mid + cond_z[:, :, 2:])
    kzm = 0.5 * (cond_mid + cond_z[:, :, :-2])
    return (kxp, kxm, kyp, kym, kzp, kzm)


def windows(block, rows, count):
    parts = [lax.slice_in_dim(block, c * rows, (c + 1) * rows, axis=2) for c in range(count)]
    received = lax.all_to_all(jnp.stack(parts), "col", 0, 0, tiled=True)
    return received.reshape((-1,) + received.shape[2:])


def conduction(field, coeffs):
    kxp, kxm, kyp, kym, kzp, kzm = coeffs
    xlo, xhi = halo_pair(field, "slab", 1)
    ylo, yhi = halo_pair(field, "col", 2)
    nxp, nxm = shifted(field, xlo, xhi, 1)
    nyp, nym = shifted(field, ylo, yhi, 2)
    field_z = jnp.pad(field, ((0, 0), (0, 0), (0, 0), (1, 1)))
    summed = kxp * (field - nxp)
    summed = summed + kxm * (field - nxm)
    summed = summed + kyp * (field - nyp)
    summed = summed + kym * (field - nym)
    summed = summed + kzp * (field - field_z[..., 2:])
    summed = summed + kzm * (field - field_z[..., :-2])
    return summed


def bounds(shift_val, cond_max):
    high_eig = shift_val + 12.0 * cond_max
    mid_eig = 0.5 * (high_eig + shift_val)
    half_span = 0.5 * (high_eig - shift_val)
    return (mid_eig, half_span, mid_eig / half_span)


def solve_slabs(right_side, shift_val, cond_max, coeffs):
    mid_eig, half_span, ratio_eig = bounds(shift_val, cond_max)
    rho_now = 1.0 / ratio_eig
    solution = jnp.zeros_like(right_side)
    residual = right_side
    direction = right_side / mid_eig
    for sweep_idx in range(STEPS - 1):
        solution = solution + direction
        applied = conduction(direction, coeffs) + shift_val * direction
        residual = residual - applied
        rho_next = 1.0 / (2.0 * ratio_eig - rho_now)
        direction = rho_next * rho_now * direction + 2.0 * rho_next / half_span * residual
        rho_now = rho_next
    return solution + direction


def run_segments(stacked, shifts, solver):
    factors = []
    current = stacked
    for segment_idx in range(ADI):
        shift_val = shifts[segment_idx]
        if segment_idx == 0:
            current = solver(stacked, shift_val)
        else:
            current = current - (shifts[segment_idx - 1] + shift_val) * solver(current, shift_val)
        factors.append(jnp.sqrt(2.0 * shift_val) * current)
    return jnp.stack(factors)


def body(input_map, output_map, region_ids, region_cond, shift_ids):
    col_count = lax.axis_size("col")
    ctrl_in = exchange(input_map, col_count)
    obsv_in = windows(output_map, output_map.shape[2] // col_count, col_count)
    col_local = ctrl_in.shape[0]
    rows = ctrl_in.shape[2]
    local_x = input_map.shape[1]
    cond_cells = lookup(region_ids, region_cond)
    cond_max = jnp.max(region_cond)
    shifts = 0.25 * jnp.exp2(shift_ids.astype(jnp.float32))
    total_x = local_x * lax.axis_size("slab")
    cond_ypad = jnp.pad(cond_cells, ((0, 0), (1, 1), (0, 0)))
    cond_y = lax.dynamic_slice_in_dim(cond_ypad, lax.axis_index("col") * rows, rows + 2, axis=1)
    cond_xy = extended(cond_y, (("slab", 0),), 1)
    coeffs = coefficients(cond_xy)
    solver = lambda rhs, shift_val: solve_slabs(rhs, shift_val, cond_max, coeffs)
    ctrl_cols = run_segments(ctrl_in, shifts, solver)
    obsv_cols = run_segments(obsv_in, shifts, solver)
    row_count = ctrl_cols.shape[0] * ctrl_cols.shape[1]
    partial_value = gram(
        ctrl_cols.reshape((row_count,) + ctrl_cols.shape[2:]),
        obsv_cols.reshape((row_count,) + obsv_cols.shape[2:]),
    )
    cells_total = total_x * region_ids.shape[1] * region_ids.shape[2]
    norm_scale = 1.0 / math.sqrt(cells_total)
    slab_count = lax.axis_size("slab")
    col_count = lax.axis_size("col")
    tile_rows = row_count // slab_count
    tile_cols = row_count // col_count
    tiles = partial_value.reshape(row_count, col_count, tile_cols).transpose(1, 0, 2)
    tiles = tiles.reshape(col_count, slab_count, tile_rows * tile_cols)
    own_tile = reduce_scatter(tiles, slab_count).reshape(tile_rows, tile_cols)
    return (ctrl_cols, obsv_cols, own_tile * norm_scale)


def solution(mesh):
    placed = (
        P("col", "slab", None, None),
        P("col", "slab", None, None),
        P("slab", None, None),
        P(),
        P(),
    )
    return jax.shard_map(
        body,
        mesh=mesh,
        in_specs=placed,
        out_specs=(
            P(None, None, "slab", "col", None),
            P(None, None, "slab", "col", None),
            P("slab", "col"),
        ),
        check_vma=False,
    )
```

```python
import math

import jax
import jax.numpy as jnp
from jax import lax
from jax.experimental import pallas as pl
from jax.experimental.pallas import tpu as pltpu
from jax.sharding import PartitionSpec as P

ADI = 2
STEPS = 3


def extended(block, sides, width):
    for axis, dim in sides:
        count = lax.axis_size(axis)
        forward = [(i, i + 1) for i in range(count - 1)]
        backward = [(target, source) for source, target in forward]
        low = lax.ppermute(
            lax.slice_in_dim(block, block.shape[dim] - width, None, axis=dim), axis, forward
        )
        high = lax.ppermute(lax.slice_in_dim(block, 0, width, axis=dim), axis, backward)
        block = jnp.concatenate([low, block, high], axis=dim)
    return block


def reduce_kernel(tiles_ref, out_ref, recv1, stage, recv2, send1, rsem1, send2, rsem2):
    ncol = tiles_ref.shape[0]
    nslab = recv2.shape[0]
    my_slab = lax.axis_index("slab")
    my_col = lax.axis_index("col")
    mesh = pl.DeviceIdType.MESH
    recv1[pl.ds(my_col, 1)] = tiles_ref[pl.ds(my_col, 1)]
    barrier = pltpu.get_barrier_semaphore()
    for k in range(1, ncol):
        peer = lax.rem(my_col + k, ncol)
        pl.semaphore_signal(barrier, inc=1, device_id=(my_slab, peer), device_id_type=mesh)

    def greet(k, carry):
        peer = lax.rem(my_slab + k, nslab)
        pl.semaphore_signal(barrier, inc=1, device_id=(peer, my_col), device_id_type=mesh)
        return carry

    lax.fori_loop(1, nslab, greet, 0)
    pl.semaphore_wait(barrier, ncol - 1 + nslab - 1)

    def col_copy(peer, src, dst):
        return pltpu.make_async_remote_copy(
            src_ref=tiles_ref.at[pl.ds(src, 1)],
            dst_ref=recv1.at[pl.ds(dst, 1)],
            send_sem=send1.at[src],
            recv_sem=rsem1.at[dst],
            device_id=(my_slab, peer),
            device_id_type=mesh,
        )

    for k in range(1, ncol):
        peer = lax.rem(my_col + k, ncol)
        col_copy(peer, peer, my_col).start()
    for k in range(1, ncol):
        peer = lax.rem(my_col + k, ncol)
        col_copy(peer, peer, my_col).wait_send()
        col_copy(peer, my_col, peer).wait_recv()
    summed = jnp.sum(recv1[...], axis=0)
    for k in range(nslab):
        stage[k] = summed[k:k + 1]
    recv2[pl.ds(my_slab, 1)] = stage[pl.ds(my_slab, 1)]

    def slab_copy(peer, src, dst):
        return pltpu.make_async_remote_copy(
            src_ref=stage.at[pl.ds(src, 1)],
            dst_ref=recv2.at[pl.ds(dst, 1)],
            send_sem=send2.at[src],
            recv_sem=rsem2.at[dst],
            device_id=(peer, my_col),
            device_id_type=mesh,
        )

    def send(k, carry):
        peer = lax.rem(my_slab + k, nslab)
        slab_copy(peer, peer, my_slab).start()
        return carry

    lax.fori_loop(1, nslab, send, 0)

    def finish(k, carry):
        peer = lax.rem(my_slab + k, nslab)
        slab_copy(peer, peer, my_slab).wait_send()
        slab_copy(peer, my_slab, peer).wait_recv()
        return carry

    lax.fori_loop(1, nslab, finish, 0)
    out_ref[...] = jnp.sum(recv2[...], axis=0, keepdims=True)


def reduce_scatter(tiles, nslab):
    ncol, rows, lanes = tiles.shape
    return pl.pallas_call(
        reduce_kernel,
        out_shape=jax.ShapeDtypeStruct((1, 1, lanes), jnp.float32),
        in_specs=[pl.BlockSpec(memory_space=pltpu.VMEM)],
        out_specs=pl.BlockSpec(memory_space=pltpu.VMEM),
        scratch_shapes=[
            pltpu.VMEM((ncol, rows, lanes), jnp.float32),
            pltpu.VMEM((nslab, 1, lanes), jnp.float32),
            pltpu.VMEM((nslab, 1, lanes), jnp.float32),
            pltpu.SemaphoreType.DMA((ncol,)),
            pltpu.SemaphoreType.DMA((ncol,)),
            pltpu.SemaphoreType.DMA((nslab,)),
            pltpu.SemaphoreType.DMA((nslab,)),
        ],
        compiler_params=pltpu.CompilerParams(collective_id=0, has_side_effects=True),
    )(tiles)


def gram_kernel(a_ref, b_ref, out_ref):
    @pl.when((pl.program_id(0) == 0) & (pl.program_id(1) == 0))
    def _():
        out_ref[...] = jnp.zeros_like(out_ref)

    rows = a_ref.shape[2]
    left = jnp.concatenate([a_ref[:, 0, row, :] for row in range(rows)], axis=1)
    right = jnp.concatenate([b_ref[:, 0, row, :] for row in range(rows)], axis=1)
    out_ref[...] += lax.dot_general(
        left,
        right,
        (((1,), (1,)), ((), ())),
        precision=lax.Precision.HIGHEST,
        preferred_element_type=jnp.float32,
    )


def gram(a, b, rows_per_step=48):
    count, depth, rows, lanes = a.shape
    spec = pl.BlockSpec((count, 1, rows_per_step, lanes), lambda i, j: (0, i, j, 0))
    return pl.pallas_call(
        gram_kernel,
        grid=(depth, rows // rows_per_step),
        in_specs=[spec, spec],
        out_specs=pl.BlockSpec((count, count), lambda i, j: (0, 0)),
        out_shape=jax.ShapeDtypeStruct((count, count), jnp.float32),
        cost_estimate=pl.CostEstimate(
            flops=2 * count * count * a.size // count, bytes_accessed=8 * a.size, transcendentals=0
        ),
    )(a, b)


def lookup(region_ids, region_cond):
    summed = jnp.zeros(region_ids.shape, jnp.float32)
    for region in range(region_cond.shape[0]):
        summed = summed + jnp.where(region_ids == region, region_cond[region], jnp.float32(0.0))
    return summed


def halo_pair(block, axis, dim):
    count = lax.axis_size(axis)
    forward = [(i, i + 1) for i in range(count - 1)]
    backward = [(target, source) for source, target in forward]
    size = block.shape[dim]
    low = lax.ppermute(lax.slice_in_dim(block, size - 1, None, axis=dim), axis, forward)
    high = lax.ppermute(lax.slice_in_dim(block, 0, 1, axis=dim), axis, backward)
    return low, high


def shifted(block, low, high, dim):
    size = block.shape[dim]
    ahead = jnp.concatenate([lax.slice_in_dim(block, 1, None, axis=dim), high], axis=dim)
    behind = jnp.concatenate([low, lax.slice_in_dim(block, 0, size - 1, axis=dim)], axis=dim)
    return ahead, behind


def coefficients(cond_xy):
    cond_mid = cond_xy[1:-1, 1:-1]
    kxp = 0.5 * (cond_mid + cond_xy[2:, 1:-1])
    kxm = 0.5 * (cond_mid + cond_xy[:-2, 1:-1])
    kyp = 0.5 * (cond_mid + cond_xy[1:-1, 2:])
    kym = 0.5 * (cond_mid + cond_xy[1:-1, :-2])
    cond_z = jnp.pad(cond_mid, ((0, 0), (0, 0), (1, 1)))
    kzp = 0.5 * (cond_mid + cond_z[:, :, 2:])
    kzm = 0.5 * (cond_mid + cond_z[:, :, :-2])
    return (kxp, kxm, kyp, kym, kzp, kzm)


def windows(block, rows, count):
    parts = [lax.slice_in_dim(block, c * rows, (c + 1) * rows, axis=2) for c in range(count)]
    received = lax.all_to_all(jnp.stack(parts), "col", 0, 0, tiled=True)
    return received.reshape((-1,) + received.shape[2:])


def conduction(field, coeffs):
    kxp, kxm, kyp, kym, kzp, kzm = coeffs
    xlo, xhi = halo_pair(field, "slab", 1)
    ylo, yhi = halo_pair(field, "col", 2)
    nxp, nxm = shifted(field, xlo, xhi, 1)
    nyp, nym = shifted(field, ylo, yhi, 2)
    field_z = jnp.pad(field, ((0, 0), (0, 0), (0, 0), (1, 1)))
    summed = kxp * (field - nxp)
    summed = summed + kxm * (field - nxm)
    summed = summed + kyp * (field - nyp)
    summed = summed + kym * (field - nym)
    summed = summed + kzp * (field - field_z[..., 2:])
    summed = summed + kzm * (field - field_z[..., :-2])
    return summed


def bounds(shift_val, cond_max):
    high_eig = shift_val + 12.0 * cond_max
    mid_eig = 0.5 * (high_eig + shift_val)
    half_span = 0.5 * (high_eig - shift_val)
    return (mid_eig, half_span, mid_eig / half_span)


def solve_slabs(right_side, shift_val, cond_max, coeffs):
    mid_eig, half_span, ratio_eig = bounds(shift_val, cond_max)
    rho_now = 1.0 / ratio_eig
    solution = jnp.zeros_like(right_side)
    residual = right_side
    direction = right_side / mid_eig
    for sweep_idx in range(STEPS - 1):
        solution = solution + direction
        applied = conduction(direction, coeffs) + shift_val * direction
        residual = residual - applied
        rho_next = 1.0 / (2.0 * ratio_eig - rho_now)
        direction = rho_next * rho_now * direction + 2.0 * rho_next / half_span * residual
        rho_now = rho_next
    return solution + direction


def run_segments(stacked, shifts, solver):
    factors = []
    current = stacked
    for segment_idx in range(ADI):
        shift_val = shifts[segment_idx]
        if segment_idx == 0:
            current = solver(stacked, shift_val)
        else:
            current = current - (shifts[segment_idx - 1] + shift_val) * solver(current, shift_val)
        factors.append(jnp.sqrt(2.0 * shift_val) * current)
    return jnp.stack(factors)


def body(input_map, output_map, region_ids, region_cond, shift_ids):
    col_count = lax.axis_size("col")
    ctrl_in = windows(input_map, input_map.shape[2] // col_count, col_count)
    obsv_in = windows(output_map, output_map.shape[2] // col_count, col_count)
    col_local = ctrl_in.shape[0]
    rows = ctrl_in.shape[2]
    local_x = input_map.shape[1]
    cond_cells = lookup(region_ids, region_cond)
    cond_max = jnp.max(region_cond)
    shifts = 0.25 * jnp.exp2(shift_ids.astype(jnp.float32))
    total_x = local_x * lax.axis_size("slab")
    cond_ypad = jnp.pad(cond_cells, ((0, 0), (1, 1), (0, 0)))
    cond_y = lax.dynamic_slice_in_dim(cond_ypad, lax.axis_index("col") * rows, rows + 2, axis=1)
    cond_xy = extended(cond_y, (("slab", 0),), 1)
    coeffs = coefficients(cond_xy)
    solver = lambda rhs, shift_val: solve_slabs(rhs, shift_val, cond_max, coeffs)
    ctrl_cols = run_segments(ctrl_in, shifts, solver)
    obsv_cols = run_segments(obsv_in, shifts, solver)
    row_count = ctrl_cols.shape[0] * ctrl_cols.shape[1]
    partial_value = gram(
        ctrl_cols.reshape((row_count,) + ctrl_cols.shape[2:]),
        obsv_cols.reshape((row_count,) + obsv_cols.shape[2:]),
    )
    cells_total = total_x * region_ids.shape[1] * region_ids.shape[2]
    norm_scale = 1.0 / math.sqrt(cells_total)
    slab_count = lax.axis_size("slab")
    col_count = lax.axis_size("col")
    tile_rows = row_count // slab_count
    tile_cols = row_count // col_count
    tiles = partial_value.reshape(row_count, col_count, tile_cols).transpose(1, 0, 2)
    tiles = tiles.reshape(col_count, slab_count, tile_rows * tile_cols)
    own_tile = reduce_scatter(tiles, slab_count).reshape(tile_rows, tile_cols)
    return (ctrl_cols, obsv_cols, own_tile * norm_scale)


def solution(mesh):
    placed = (
        P("col", "slab", None, None),
        P("col", "slab", None, None),
        P("slab", None, None),
        P(),
        P(),
    )
    return jax.shard_map(
        body,
        mesh=mesh,
        in_specs=placed,
        out_specs=(
            P(None, None, "slab", "col", None),
            P(None, None, "slab", "col", None),
            P("slab", "col"),
        ),
        check_vma=False,
    )
```

```python
import math

import jax
import jax.numpy as jnp
from jax import lax
from jax.experimental import pallas as pl
from jax.experimental.pallas import tpu as pltpu
from jax.sharding import PartitionSpec as P

ADI = 2
STEPS = 3


def extended(block, sides, width):
    for axis, dim in sides:
        count = lax.axis_size(axis)
        forward = [(i, i + 1) for i in range(count - 1)]
        backward = [(target, source) for source, target in forward]
        low = lax.ppermute(
            lax.slice_in_dim(block, block.shape[dim] - width, None, axis=dim), axis, forward
        )
        high = lax.ppermute(lax.slice_in_dim(block, 0, width, axis=dim), axis, backward)
        block = jnp.concatenate([low, block, high], axis=dim)
    return block


def reduce_kernel(tiles_ref, out_ref, recv1, stage, recv2, send1, rsem1, send2, rsem2):
    ncol = tiles_ref.shape[0]
    nslab = recv2.shape[0]
    my_slab = lax.axis_index("slab")
    my_col = lax.axis_index("col")
    mesh = pl.DeviceIdType.MESH
    recv1[pl.ds(my_col, 1)] = tiles_ref[pl.ds(my_col, 1)]
    barrier = pltpu.get_barrier_semaphore()
    for k in range(1, ncol):
        peer = lax.rem(my_col + k, ncol)
        pl.semaphore_signal(barrier, inc=1, device_id=(my_slab, peer), device_id_type=mesh)

    def greet(k, carry):
        peer = lax.rem(my_slab + k, nslab)
        pl.semaphore_signal(barrier, inc=1, device_id=(peer, my_col), device_id_type=mesh)
        return carry

    lax.fori_loop(1, nslab, greet, 0)
    pl.semaphore_wait(barrier, ncol - 1 + nslab - 1)

    def col_copy(peer, src, dst):
        return pltpu.make_async_remote_copy(
            src_ref=tiles_ref.at[pl.ds(src, 1)],
            dst_ref=recv1.at[pl.ds(dst, 1)],
            send_sem=send1.at[src],
            recv_sem=rsem1.at[dst],
            device_id=(my_slab, peer),
            device_id_type=mesh,
        )

    for k in range(1, ncol):
        peer = lax.rem(my_col + k, ncol)
        col_copy(peer, peer, my_col).start()
    for k in range(1, ncol):
        peer = lax.rem(my_col + k, ncol)
        col_copy(peer, peer, my_col).wait_send()
        col_copy(peer, my_col, peer).wait_recv()
    summed = jnp.sum(recv1[...], axis=0)
    for k in range(nslab):
        stage[k] = summed[k:k + 1]
    recv2[pl.ds(my_slab, 1)] = stage[pl.ds(my_slab, 1)]

    def slab_copy(peer, src, dst):
        return pltpu.make_async_remote_copy(
            src_ref=stage.at[pl.ds(src, 1)],
            dst_ref=recv2.at[pl.ds(dst, 1)],
            send_sem=send2.at[src],
            recv_sem=rsem2.at[dst],
            device_id=(peer, my_col),
            device_id_type=mesh,
        )

    def send(k, carry):
        peer = lax.rem(my_slab + k, nslab)
        slab_copy(peer, peer, my_slab).start()
        return carry

    lax.fori_loop(1, nslab, send, 0)

    def finish(k, carry):
        peer = lax.rem(my_slab + k, nslab)
        slab_copy(peer, peer, my_slab).wait_send()
        slab_copy(peer, my_slab, peer).wait_recv()
        return carry

    lax.fori_loop(1, nslab, finish, 0)
    out_ref[...] = jnp.sum(recv2[...], axis=0, keepdims=True)


def reduce_scatter(tiles, nslab):
    ncol, rows, lanes = tiles.shape
    return pl.pallas_call(
        reduce_kernel,
        out_shape=jax.ShapeDtypeStruct((1, 1, lanes), jnp.float32),
        in_specs=[pl.BlockSpec(memory_space=pltpu.VMEM)],
        out_specs=pl.BlockSpec(memory_space=pltpu.VMEM),
        scratch_shapes=[
            pltpu.VMEM((ncol, rows, lanes), jnp.float32),
            pltpu.VMEM((nslab, 1, lanes), jnp.float32),
            pltpu.VMEM((nslab, 1, lanes), jnp.float32),
            pltpu.SemaphoreType.DMA((ncol,)),
            pltpu.SemaphoreType.DMA((ncol,)),
            pltpu.SemaphoreType.DMA((nslab,)),
            pltpu.SemaphoreType.DMA((nslab,)),
        ],
        compiler_params=pltpu.CompilerParams(collective_id=0, has_side_effects=True),
    )(tiles)


def gram_kernel(a_ref, b_ref, out_ref):
    @pl.when((pl.program_id(0) == 0) & (pl.program_id(1) == 0))
    def _():
        out_ref[...] = jnp.zeros_like(out_ref)

    rows = a_ref.shape[2]
    left = jnp.concatenate([a_ref[:, 0, row, :] for row in range(rows)], axis=1)
    right = jnp.concatenate([b_ref[:, 0, row, :] for row in range(rows)], axis=1)
    out_ref[...] += lax.dot_general(
        left,
        right,
        (((1,), (1,)), ((), ())),
        precision=lax.Precision.HIGHEST,
        preferred_element_type=jnp.float32,
    )


def gram(a, b, rows_per_step=16):
    count, depth, rows, lanes = a.shape
    spec = pl.BlockSpec((count, 1, rows_per_step, lanes), lambda i, j: (0, i, j, 0))
    return pl.pallas_call(
        gram_kernel,
        grid=(depth, rows // rows_per_step),
        in_specs=[spec, spec],
        out_specs=pl.BlockSpec((count, count), lambda i, j: (0, 0)),
        out_shape=jax.ShapeDtypeStruct((count, count), jnp.float32),
        cost_estimate=pl.CostEstimate(
            flops=2 * count * count * a.size // count, bytes_accessed=8 * a.size, transcendentals=0
        ),
    )(a, b)


def lookup(region_ids, region_cond):
    summed = jnp.zeros(region_ids.shape, jnp.float32)
    for region in range(region_cond.shape[0]):
        summed = summed + jnp.where(region_ids == region, region_cond[region], jnp.float32(0.0))
    return summed


def halo_pair(block, axis, dim):
    count = lax.axis_size(axis)
    forward = [(i, i + 1) for i in range(count - 1)]
    backward = [(target, source) for source, target in forward]
    size = block.shape[dim]
    last = lax.slice_in_dim(block, size - 1, None, axis=dim)
    first = lax.slice_in_dim(block, 0, 1, axis=dim)
    face_shape = last.shape
    flat = (-1, block.shape[-1])
    low = lax.ppermute(last.reshape(flat), axis, forward).reshape(face_shape)
    high = lax.ppermute(first.reshape(flat), axis, backward).reshape(face_shape)
    return low, high


def shifted(block, low, high, dim):
    size = block.shape[dim]
    ahead = jnp.concatenate([lax.slice_in_dim(block, 1, None, axis=dim), high], axis=dim)
    behind = jnp.concatenate([low, lax.slice_in_dim(block, 0, size - 1, axis=dim)], axis=dim)
    return ahead, behind


def coefficients(cond_xy):
    cond_mid = cond_xy[1:-1, 1:-1]
    kxp = 0.5 * (cond_mid + cond_xy[2:, 1:-1])
    kxm = 0.5 * (cond_mid + cond_xy[:-2, 1:-1])
    kyp = 0.5 * (cond_mid + cond_xy[1:-1, 2:])
    kym = 0.5 * (cond_mid + cond_xy[1:-1, :-2])
    cond_z = jnp.pad(cond_mid, ((0, 0), (0, 0), (1, 1)))
    kzp = 0.5 * (cond_mid + cond_z[:, :, 2:])
    kzm = 0.5 * (cond_mid + cond_z[:, :, :-2])
    return (kxp, kxm, kyp, kym, kzp, kzm)


def windows(block, rows, count):
    parts = [lax.slice_in_dim(block, c * rows, (c + 1) * rows, axis=2) for c in range(count)]
    received = lax.all_to_all(jnp.stack(parts), "col", 0, 0, tiled=True)
    return received.reshape((-1,) + received.shape[2:])


def conduction(field, coeffs):
    kxp, kxm, kyp, kym, kzp, kzm = coeffs
    xlo, xhi = halo_pair(field, "slab", 1)
    ylo, yhi = halo_pair(field, "col", 2)
    nxp, nxm = shifted(field, xlo, xhi, 1)
    nyp, nym = shifted(field, ylo, yhi, 2)
    field_z = jnp.pad(field, ((0, 0), (0, 0), (0, 0), (1, 1)))
    summed = kxp * (field - nxp)
    summed = summed + kxm * (field - nxm)
    summed = summed + kyp * (field - nyp)
    summed = summed + kym * (field - nym)
    summed = summed + kzp * (field - field_z[..., 2:])
    summed = summed + kzm * (field - field_z[..., :-2])
    return summed


def bounds(shift_val, cond_max):
    high_eig = shift_val + 12.0 * cond_max
    mid_eig = 0.5 * (high_eig + shift_val)
    half_span = 0.5 * (high_eig - shift_val)
    return (mid_eig, half_span, mid_eig / half_span)


def solve_slabs(right_side, shift_val, cond_max, coeffs):
    mid_eig, half_span, ratio_eig = bounds(shift_val, cond_max)
    rho_now = 1.0 / ratio_eig
    solution = jnp.zeros_like(right_side)
    residual = right_side
    direction = right_side / mid_eig
    for sweep_idx in range(STEPS - 1):
        solution = solution + direction
        applied = conduction(direction, coeffs) + shift_val * direction
        residual = residual - applied
        rho_next = 1.0 / (2.0 * ratio_eig - rho_now)
        direction = rho_next * rho_now * direction + 2.0 * rho_next / half_span * residual
        rho_now = rho_next
    return solution + direction


def run_segments(stacked, shifts, solver):
    factors = []
    current = stacked
    for segment_idx in range(ADI):
        shift_val = shifts[segment_idx]
        if segment_idx == 0:
            current = solver(stacked, shift_val)
        else:
            current = current - (shifts[segment_idx - 1] + shift_val) * solver(current, shift_val)
        factors.append(jnp.sqrt(2.0 * shift_val) * current)
    return jnp.stack(factors)


def body(input_map, output_map, region_ids, region_cond, shift_ids):
    col_count = lax.axis_size("col")
    ctrl_in = windows(input_map, input_map.shape[2] // col_count, col_count)
    obsv_in = windows(output_map, output_map.shape[2] // col_count, col_count)
    col_local = ctrl_in.shape[0]
    rows = ctrl_in.shape[2]
    local_x = input_map.shape[1]
    cond_cells = lookup(region_ids, region_cond)
    cond_max = jnp.max(region_cond)
    shifts = 0.25 * jnp.exp2(shift_ids.astype(jnp.float32))
    total_x = local_x * lax.axis_size("slab")
    cond_ypad = jnp.pad(cond_cells, ((0, 0), (1, 1), (0, 0)))
    cond_y = lax.dynamic_slice_in_dim(cond_ypad, lax.axis_index("col") * rows, rows + 2, axis=1)
    cond_xy = extended(cond_y, (("slab", 0),), 1)
    coeffs = coefficients(cond_xy)
    solver = lambda rhs, shift_val: solve_slabs(rhs, shift_val, cond_max, coeffs)
    ctrl_cols = run_segments(ctrl_in, shifts, solver)
    obsv_cols = run_segments(obsv_in, shifts, solver)
    row_count = ctrl_cols.shape[0] * ctrl_cols.shape[1]
    partial_value = gram(
        ctrl_cols.reshape((row_count,) + ctrl_cols.shape[2:]),
        obsv_cols.reshape((row_count,) + obsv_cols.shape[2:]),
    )
    cells_total = total_x * region_ids.shape[1] * region_ids.shape[2]
    norm_scale = 1.0 / math.sqrt(cells_total)
    slab_count = lax.axis_size("slab")
    col_count = lax.axis_size("col")
    tile_rows = row_count // slab_count
    tile_cols = row_count // col_count
    tiles = partial_value.reshape(row_count, col_count, tile_cols).transpose(1, 0, 2)
    tiles = tiles.reshape(col_count, slab_count, tile_rows * tile_cols)
    own_tile = reduce_scatter(tiles, slab_count).reshape(tile_rows, tile_cols)
    return (ctrl_cols, obsv_cols, own_tile * norm_scale)


def solution(mesh):
    placed = (
        P("col", "slab", None, None),
        P("col", "slab", None, None),
        P("slab", None, None),
        P(),
        P(),
    )
    return jax.shard_map(
        body,
        mesh=mesh,
        in_specs=placed,
        out_specs=(
            P(None, None, "slab", "col", None),
            P(None, None, "slab", "col", None),
            P("slab", "col"),
        ),
        check_vma=False,
    )
```

```python
import math

import jax
import jax.numpy as jnp
from jax import lax
from jax.experimental import pallas as pl
from jax.experimental.pallas import tpu as pltpu
from jax.sharding import PartitionSpec as P

ADI = 2
STEPS = 3


def extended(block, sides, width):
    for axis, dim in sides:
        count = lax.axis_size(axis)
        forward = [(i, i + 1) for i in range(count - 1)]
        backward = [(target, source) for source, target in forward]
        low = lax.ppermute(
            lax.slice_in_dim(block, block.shape[dim] - width, None, axis=dim), axis, forward
        )
        high = lax.ppermute(lax.slice_in_dim(block, 0, width, axis=dim), axis, backward)
        block = jnp.concatenate([low, block, high], axis=dim)
    return block


def reduce_kernel(tiles_ref, out_ref, recv1, stage, recv2, send1, rsem1, send2, rsem2):
    ncol = tiles_ref.shape[0]
    nslab = recv2.shape[0]
    my_slab = lax.axis_index("slab")
    my_col = lax.axis_index("col")
    mesh = pl.DeviceIdType.MESH
    recv1[pl.ds(my_col, 1)] = tiles_ref[pl.ds(my_col, 1)]
    barrier = pltpu.get_barrier_semaphore()
    for k in range(1, ncol):
        peer = lax.rem(my_col + k, ncol)
        pl.semaphore_signal(barrier, inc=1, device_id=(my_slab, peer), device_id_type=mesh)

    def greet(k, carry):
        peer = lax.rem(my_slab + k, nslab)
        pl.semaphore_signal(barrier, inc=1, device_id=(peer, my_col), device_id_type=mesh)
        return carry

    lax.fori_loop(1, nslab, greet, 0)
    pl.semaphore_wait(barrier, ncol - 1 + nslab - 1)

    def col_copy(peer, src, dst):
        return pltpu.make_async_remote_copy(
            src_ref=tiles_ref.at[pl.ds(src, 1)],
            dst_ref=recv1.at[pl.ds(dst, 1)],
            send_sem=send1.at[src],
            recv_sem=rsem1.at[dst],
            device_id=(my_slab, peer),
            device_id_type=mesh,
        )

    for k in range(1, ncol):
        peer = lax.rem(my_col + k, ncol)
        col_copy(peer, peer, my_col).start()
    for k in range(1, ncol):
        peer = lax.rem(my_col + k, ncol)
        col_copy(peer, peer, my_col).wait_send()
        col_copy(peer, my_col, peer).wait_recv()
    summed = jnp.sum(recv1[...], axis=0)
    for k in range(nslab):
        stage[k] = summed[k:k + 1]
    recv2[pl.ds(my_slab, 1)] = stage[pl.ds(my_slab, 1)]

    def slab_copy(peer, src, dst):
        return pltpu.make_async_remote_copy(
            src_ref=stage.at[pl.ds(src, 1)],
            dst_ref=recv2.at[pl.ds(dst, 1)],
            send_sem=send2.at[src],
            recv_sem=rsem2.at[dst],
            device_id=(peer, my_col),
            device_id_type=mesh,
        )

    def send(k, carry):
        peer = lax.rem(my_slab + k, nslab)
        slab_copy(peer, peer, my_slab).start()
        return carry

    lax.fori_loop(1, nslab, send, 0)

    def finish(k, carry):
        peer = lax.rem(my_slab + k, nslab)
        slab_copy(peer, peer, my_slab).wait_send()
        slab_copy(peer, my_slab, peer).wait_recv()
        return carry

    lax.fori_loop(1, nslab, finish, 0)
    out_ref[...] = jnp.sum(recv2[...], axis=0, keepdims=True)


def reduce_scatter(tiles, nslab):
    ncol, rows, lanes = tiles.shape
    return pl.pallas_call(
        reduce_kernel,
        out_shape=jax.ShapeDtypeStruct((1, 1, lanes), jnp.float32),
        in_specs=[pl.BlockSpec(memory_space=pltpu.VMEM)],
        out_specs=pl.BlockSpec(memory_space=pltpu.VMEM),
        scratch_shapes=[
            pltpu.VMEM((ncol, rows, lanes), jnp.float32),
            pltpu.VMEM((nslab, 1, lanes), jnp.float32),
            pltpu.VMEM((nslab, 1, lanes), jnp.float32),
            pltpu.SemaphoreType.DMA((ncol,)),
            pltpu.SemaphoreType.DMA((ncol,)),
            pltpu.SemaphoreType.DMA((nslab,)),
            pltpu.SemaphoreType.DMA((nslab,)),
        ],
        compiler_params=pltpu.CompilerParams(collective_id=0, has_side_effects=True),
    )(tiles)


def gram_kernel(c1_ref, c2_ref, o1_ref, o2_ref, out_ref, ctrl_ref, obsv_ref):
    @pl.when((pl.program_id(0) == 0) & (pl.program_id(1) == 0))
    def _():
        out_ref[...] = jnp.zeros_like(out_ref)

    ctrl_ref[0] = c1_ref[...]
    ctrl_ref[1] = c2_ref[...]
    obsv_ref[0] = o1_ref[...]
    obsv_ref[1] = o2_ref[...]
    rows = c1_ref.shape[2]

    def flat(first, second):
        stacked = [jnp.concatenate([first[:, 0, row, :], second[:, 0, row, :]], axis=0) for row in range(rows)]
        return jnp.concatenate(stacked, axis=1)

    out_ref[...] += lax.dot_general(
        flat(c1_ref, c2_ref),
        flat(o1_ref, o2_ref),
        (((1,), (1,)), ((), ())),
        precision=lax.Precision.HIGHEST,
        preferred_element_type=jnp.float32,
    )


def gram(ctrl_parts, obsv_parts, rows_per_step=16):
    count, depth, rows, lanes = ctrl_parts[0].shape
    spec = pl.BlockSpec((count, 1, rows_per_step, lanes), lambda i, j: (0, i, j, 0))
    stack_spec = pl.BlockSpec((2, count, 1, rows_per_step, lanes), lambda i, j: (0, 0, i, j, 0))
    stacked = jax.ShapeDtypeStruct((2,) + ctrl_parts[0].shape, jnp.float32)
    cells = 4 * ctrl_parts[0].size
    return pl.pallas_call(
        gram_kernel,
        grid=(depth, rows // rows_per_step),
        in_specs=[spec] * 4,
        out_specs=[pl.BlockSpec((2 * count, 2 * count), lambda i, j: (0, 0)), stack_spec, stack_spec],
        out_shape=[jax.ShapeDtypeStruct((2 * count, 2 * count), jnp.float32), stacked, stacked],
        cost_estimate=pl.CostEstimate(flops=2 * count * cells, bytes_accessed=8 * cells, transcendentals=0),
    )(*ctrl_parts, *obsv_parts)


def lookup(region_ids, region_cond):
    summed = jnp.zeros(region_ids.shape, jnp.float32)
    for region in range(region_cond.shape[0]):
        summed = summed + jnp.where(region_ids == region, region_cond[region], jnp.float32(0.0))
    return summed


def halo_pair(block, axis, dim):
    count = lax.axis_size(axis)
    forward = [(i, i + 1) for i in range(count - 1)]
    backward = [(target, source) for source, target in forward]
    size = block.shape[dim]
    low = lax.ppermute(lax.slice_in_dim(block, size - 1, None, axis=dim), axis, forward)
    high = lax.ppermute(lax.slice_in_dim(block, 0, 1, axis=dim), axis, backward)
    return low, high


def shifted(block, low, high, dim):
    size = block.shape[dim]
    ahead = jnp.concatenate([lax.slice_in_dim(block, 1, None, axis=dim), high], axis=dim)
    behind = jnp.concatenate([low, lax.slice_in_dim(block, 0, size - 1, axis=dim)], axis=dim)
    return ahead, behind


def coefficients(cond_xy):
    cond_mid = cond_xy[1:-1, 1:-1]
    kxp = 0.5 * (cond_mid + cond_xy[2:, 1:-1])
    kxm = 0.5 * (cond_mid + cond_xy[:-2, 1:-1])
    kyp = 0.5 * (cond_mid + cond_xy[1:-1, 2:])
    kym = 0.5 * (cond_mid + cond_xy[1:-1, :-2])
    cond_z = jnp.pad(cond_mid, ((0, 0), (0, 0), (1, 1)))
    kzp = 0.5 * (cond_mid + cond_z[:, :, 2:])
    kzm = 0.5 * (cond_mid + cond_z[:, :, :-2])
    return (kxp, kxm, kyp, kym, kzp, kzm)


def windows(block, rows, count):
    parts = [lax.slice_in_dim(block, c * rows, (c + 1) * rows, axis=2) for c in range(count)]
    received = lax.all_to_all(jnp.stack(parts), "col", 0, 0, tiled=True)
    return received.reshape((-1,) + received.shape[2:])


def conduction(field, coeffs):
    kxp, kxm, kyp, kym, kzp, kzm = coeffs
    xlo, xhi = halo_pair(field, "slab", 1)
    ylo, yhi = halo_pair(field, "col", 2)
    nxp, nxm = shifted(field, xlo, xhi, 1)
    nyp, nym = shifted(field, ylo, yhi, 2)
    field_z = jnp.pad(field, ((0, 0), (0, 0), (0, 0), (1, 1)))
    summed = kxp * (field - nxp)
    summed = summed + kxm * (field - nxm)
    summed = summed + kyp * (field - nyp)
    summed = summed + kym * (field - nym)
    summed = summed + kzp * (field - field_z[..., 2:])
    summed = summed + kzm * (field - field_z[..., :-2])
    return summed


def bounds(shift_val, cond_max):
    high_eig = shift_val + 12.0 * cond_max
    mid_eig = 0.5 * (high_eig + shift_val)
    half_span = 0.5 * (high_eig - shift_val)
    return (mid_eig, half_span, mid_eig / half_span)


def solve_slabs(right_side, shift_val, cond_max, coeffs):
    mid_eig, half_span, ratio_eig = bounds(shift_val, cond_max)
    rho_now = 1.0 / ratio_eig
    solution = jnp.zeros_like(right_side)
    residual = right_side
    direction = right_side / mid_eig
    for sweep_idx in range(STEPS - 1):
        solution = solution + direction
        applied = conduction(direction, coeffs) + shift_val * direction
        residual = residual - applied
        rho_next = 1.0 / (2.0 * ratio_eig - rho_now)
        direction = rho_next * rho_now * direction + 2.0 * rho_next / half_span * residual
        rho_now = rho_next
    return solution + direction


def run_segments(stacked, shifts, solver):
    factors = []
    current = stacked
    for segment_idx in range(ADI):
        shift_val = shifts[segment_idx]
        if segment_idx == 0:
            current = solver(stacked, shift_val)
        else:
            current = current - (shifts[segment_idx - 1] + shift_val) * solver(current, shift_val)
        factors.append(jnp.sqrt(2.0 * shift_val) * current)
    return factors


def body(input_map, output_map, region_ids, region_cond, shift_ids):
    col_count = lax.axis_size("col")
    ctrl_in = windows(input_map, input_map.shape[2] // col_count, col_count)
    obsv_in = windows(output_map, output_map.shape[2] // col_count, col_count)
    col_local = ctrl_in.shape[0]
    rows = ctrl_in.shape[2]
    local_x = input_map.shape[1]
    cond_cells = lookup(region_ids, region_cond)
    cond_max = jnp.max(region_cond)
    shifts = 0.25 * jnp.exp2(shift_ids.astype(jnp.float32))
    total_x = local_x * lax.axis_size("slab")
    cond_ypad = jnp.pad(cond_cells, ((0, 0), (1, 1), (0, 0)))
    cond_y = lax.dynamic_slice_in_dim(cond_ypad, lax.axis_index("col") * rows, rows + 2, axis=1)
    cond_xy = extended(cond_y, (("slab", 0),), 1)
    coeffs = coefficients(cond_xy)
    solver = lambda rhs, shift_val: solve_slabs(rhs, shift_val, cond_max, coeffs)
    ctrl_cols = run_segments(ctrl_in, shifts, solver)
    obsv_cols = run_segments(obsv_in, shifts, solver)
    partial_value, ctrl_cols, obsv_cols = gram(ctrl_cols, obsv_cols)
    row_count = partial_value.shape[0]
    cells_total = total_x * region_ids.shape[1] * region_ids.shape[2]
    norm_scale = 1.0 / math.sqrt(cells_total)
    slab_count = lax.axis_size("slab")
    col_count = lax.axis_size("col")
    tile_rows = row_count // slab_count
    tile_cols = row_count // col_count
    tiles = partial_value.reshape(row_count, col_count, tile_cols).transpose(1, 0, 2)
    tiles = tiles.reshape(col_count, slab_count, tile_rows * tile_cols)
    own_tile = reduce_scatter(tiles, slab_count).reshape(tile_rows, tile_cols)
    return (ctrl_cols, obsv_cols, own_tile * norm_scale)


def solution(mesh):
    placed = (
        P("col", "slab", None, None),
        P("col", "slab", None, None),
        P("slab", None, None),
        P(),
        P(),
    )
    return jax.shard_map(
        body,
        mesh=mesh,
        in_specs=placed,
        out_specs=(
            P(None, None, "slab", "col", None),
            P(None, None, "slab", "col", None),
            P("slab", "col"),
        ),
        check_vma=False,
    )
```

```python
import math

import jax
import jax.numpy as jnp
from jax import lax
from jax.experimental import pallas as pl
from jax.experimental.pallas import tpu as pltpu
from jax.sharding import PartitionSpec as P

ADI = 2
STEPS = 3


def extended(block, sides, width):
    for axis, dim in sides:
        count = lax.axis_size(axis)
        forward = [(i, i + 1) for i in range(count - 1)]
        backward = [(target, source) for source, target in forward]
        low = lax.ppermute(
            lax.slice_in_dim(block, block.shape[dim] - width, None, axis=dim), axis, forward
        )
        high = lax.ppermute(lax.slice_in_dim(block, 0, width, axis=dim), axis, backward)
        block = jnp.concatenate([low, block, high], axis=dim)
    return block


def reduce_kernel(tiles_ref, out_ref, recv1, stage, recv2, send1, rsem1, send2, rsem2):
    ncol = tiles_ref.shape[0]
    nslab = recv2.shape[0]
    my_slab = lax.axis_index("slab")
    my_col = lax.axis_index("col")
    mesh = pl.DeviceIdType.MESH
    recv1[pl.ds(my_col, 1)] = tiles_ref[pl.ds(my_col, 1)]
    barrier = pltpu.get_barrier_semaphore()
    for k in range(1, ncol):
        peer = lax.rem(my_col + k, ncol)
        pl.semaphore_signal(barrier, inc=1, device_id=(my_slab, peer), device_id_type=mesh)

    def greet(k, carry):
        peer = lax.rem(my_slab + k, nslab)
        pl.semaphore_signal(barrier, inc=1, device_id=(peer, my_col), device_id_type=mesh)
        return carry

    lax.fori_loop(1, nslab, greet, 0)
    pl.semaphore_wait(barrier, ncol - 1 + nslab - 1)

    def col_copy(peer, src, dst):
        return pltpu.make_async_remote_copy(
            src_ref=tiles_ref.at[pl.ds(src, 1)],
            dst_ref=recv1.at[pl.ds(dst, 1)],
            send_sem=send1.at[src],
            recv_sem=rsem1.at[dst],
            device_id=(my_slab, peer),
            device_id_type=mesh,
        )

    for k in range(1, ncol):
        peer = lax.rem(my_col + k, ncol)
        col_copy(peer, peer, my_col).start()
    for k in range(1, ncol):
        peer = lax.rem(my_col + k, ncol)
        col_copy(peer, peer, my_col).wait_send()
        col_copy(peer, my_col, peer).wait_recv()
    summed = jnp.sum(recv1[...], axis=0)
    for k in range(nslab):
        stage[k] = summed[k:k + 1]
    recv2[pl.ds(my_slab, 1)] = stage[pl.ds(my_slab, 1)]

    def slab_copy(peer, src, dst):
        return pltpu.make_async_remote_copy(
            src_ref=stage.at[pl.ds(src, 1)],
            dst_ref=recv2.at[pl.ds(dst, 1)],
            send_sem=send2.at[src],
            recv_sem=rsem2.at[dst],
            device_id=(peer, my_col),
            device_id_type=mesh,
        )

    def send(k, carry):
        peer = lax.rem(my_slab + k, nslab)
        slab_copy(peer, peer, my_slab).start()
        return carry

    lax.fori_loop(1, nslab, send, 0)

    def finish(k, carry):
        peer = lax.rem(my_slab + k, nslab)
        slab_copy(peer, peer, my_slab).wait_send()
        slab_copy(peer, my_slab, peer).wait_recv()
        return carry

    lax.fori_loop(1, nslab, finish, 0)
    out_ref[...] = jnp.sum(recv2[...], axis=0, keepdims=True)


def reduce_scatter(tiles, nslab):
    ncol, rows, lanes = tiles.shape
    return pl.pallas_call(
        reduce_kernel,
        out_shape=jax.ShapeDtypeStruct((1, 1, lanes), jnp.float32),
        in_specs=[pl.BlockSpec(memory_space=pltpu.VMEM)],
        out_specs=pl.BlockSpec(memory_space=pltpu.VMEM),
        scratch_shapes=[
            pltpu.VMEM((ncol, rows, lanes), jnp.float32),
            pltpu.VMEM((nslab, 1, lanes), jnp.float32),
            pltpu.VMEM((nslab, 1, lanes), jnp.float32),
            pltpu.SemaphoreType.DMA((ncol,)),
            pltpu.SemaphoreType.DMA((ncol,)),
            pltpu.SemaphoreType.DMA((nslab,)),
            pltpu.SemaphoreType.DMA((nslab,)),
        ],
        compiler_params=pltpu.CompilerParams(collective_id=0, has_side_effects=True),
    )(tiles)


def gram_kernel(a_ref, b_ref, out_ref):
    @pl.when((pl.program_id(0) == 0) & (pl.program_id(1) == 0))
    def _():
        out_ref[...] = jnp.zeros_like(out_ref)

    rows = a_ref.shape[2]
    left = jnp.concatenate([a_ref[:, 0, row, :] for row in range(rows)], axis=1)
    right = jnp.concatenate([b_ref[:, 0, row, :] for row in range(rows)], axis=1)
    out_ref[...] += lax.dot_general(
        left,
        right,
        (((1,), (1,)), ((), ())),
        precision=lax.Precision.HIGHEST,
        preferred_element_type=jnp.float32,
    )


def gram(a, b, rows_per_step=8):
    count, depth, rows, lanes = a.shape
    spec = pl.BlockSpec((count, 1, rows_per_step, lanes), lambda i, j: (0, i, j, 0))
    return pl.pallas_call(
        gram_kernel,
        grid=(depth, rows // rows_per_step),
        in_specs=[spec, spec],
        out_specs=pl.BlockSpec((count, count), lambda i, j: (0, 0)),
        out_shape=jax.ShapeDtypeStruct((count, count), jnp.float32),
        cost_estimate=pl.CostEstimate(
            flops=2 * count * count * a.size // count, bytes_accessed=8 * a.size, transcendentals=0
        ),
    )(a, b)


def lookup(region_ids, region_cond):
    summed = jnp.zeros(region_ids.shape, jnp.float32)
    for region in range(region_cond.shape[0]):
        summed = summed + jnp.where(region_ids == region, region_cond[region], jnp.float32(0.0))
    return summed


def halo_pair(block, axis, dim):
    count = lax.axis_size(axis)
    forward = [(i, i + 1) for i in range(count - 1)]
    backward = [(target, source) for source, target in forward]
    size = block.shape[dim]
    low = lax.ppermute(lax.slice_in_dim(block, size - 1, None, axis=dim), axis, forward)
    high = lax.ppermute(lax.slice_in_dim(block, 0, 1, axis=dim), axis, backward)
    return low, high


def shifted(block, low, high, dim):
    size = block.shape[dim]
    ahead = jnp.concatenate([lax.slice_in_dim(block, 1, None, axis=dim), high], axis=dim)
    behind = jnp.concatenate([low, lax.slice_in_dim(block, 0, size - 1, axis=dim)], axis=dim)
    return ahead, behind


def coefficients(cond_xy):
    cond_mid = cond_xy[1:-1, 1:-1]
    kxp = 0.5 * (cond_mid + cond_xy[2:, 1:-1])
    kxm = 0.5 * (cond_mid + cond_xy[:-2, 1:-1])
    kyp = 0.5 * (cond_mid + cond_xy[1:-1, 2:])
    kym = 0.5 * (cond_mid + cond_xy[1:-1, :-2])
    cond_z = jnp.pad(cond_mid, ((0, 0), (0, 0), (1, 1)))
    kzp = 0.5 * (cond_mid + cond_z[:, :, 2:])
    kzm = 0.5 * (cond_mid + cond_z[:, :, :-2])
    return (kxp, kxm, kyp, kym, kzp, kzm)


def windows(block, rows, count):
    parts = [lax.slice_in_dim(block, c * rows, (c + 1) * rows, axis=2) for c in range(count)]
    received = lax.all_to_all(jnp.stack(parts), "col", 0, 0, tiled=True)
    return received.reshape((-1,) + received.shape[2:])


def conduction(field, coeffs):
    kxp, kxm, kyp, kym, kzp, kzm = coeffs
    xlo, xhi = halo_pair(field, "slab", 1)
    ylo, yhi = halo_pair(field, "col", 2)
    nxp, nxm = shifted(field, xlo, xhi, 1)
    nyp, nym = shifted(field, ylo, yhi, 2)
    field_z = jnp.pad(field, ((0, 0), (0, 0), (0, 0), (1, 1)))
    summed = kxp * (field - nxp)
    summed = summed + kxm * (field - nxm)
    summed = summed + kyp * (field - nyp)
    summed = summed + kym * (field - nym)
    summed = summed + kzp * (field - field_z[..., 2:])
    summed = summed + kzm * (field - field_z[..., :-2])
    return summed


def bounds(shift_val, cond_max):
    high_eig = shift_val + 12.0 * cond_max
    mid_eig = 0.5 * (high_eig + shift_val)
    half_span = 0.5 * (high_eig - shift_val)
    return (mid_eig, half_span, mid_eig / half_span)


def solve_slabs(right_side, shift_val, cond_max, coeffs):
    mid_eig, half_span, ratio_eig = bounds(shift_val, cond_max)
    rho_now = 1.0 / ratio_eig
    solution = jnp.zeros_like(right_side)
    residual = right_side
    direction = right_side / mid_eig
    for sweep_idx in range(STEPS - 1):
        solution = solution + direction
        applied = conduction(direction, coeffs) + shift_val * direction
        residual = residual - applied
        rho_next = 1.0 / (2.0 * ratio_eig - rho_now)
        direction = rho_next * rho_now * direction + 2.0 * rho_next / half_span * residual
        rho_now = rho_next
    return solution + direction


def run_segments(stacked, shifts, solver):
    factors = []
    current = stacked
    for segment_idx in range(ADI):
        shift_val = shifts[segment_idx]
        if segment_idx == 0:
            current = solver(stacked, shift_val)
        else:
            current = current - (shifts[segment_idx - 1] + shift_val) * solver(current, shift_val)
        factors.append(jnp.sqrt(2.0 * shift_val) * current)
    return jnp.stack(factors)


def body(input_map, output_map, region_ids, region_cond, shift_ids):
    col_count = lax.axis_size("col")
    ctrl_in = windows(input_map, input_map.shape[2] // col_count, col_count)
    obsv_in = windows(output_map, output_map.shape[2] // col_count, col_count)
    col_local = ctrl_in.shape[0]
    rows = ctrl_in.shape[2]
    local_x = input_map.shape[1]
    cond_cells = lookup(region_ids, region_cond)
    cond_max = jnp.max(region_cond)
    shifts = 0.25 * jnp.exp2(shift_ids.astype(jnp.float32))
    total_x = local_x * lax.axis_size("slab")
    cond_ypad = jnp.pad(cond_cells, ((0, 0), (1, 1), (0, 0)))
    cond_y = lax.dynamic_slice_in_dim(cond_ypad, lax.axis_index("col") * rows, rows + 2, axis=1)
    cond_xy = extended(cond_y, (("slab", 0),), 1)
    coeffs = coefficients(cond_xy)
    solver = lambda rhs, shift_val: solve_slabs(rhs, shift_val, cond_max, coeffs)
    ctrl_cols = run_segments(ctrl_in, shifts, solver)
    obsv_cols = run_segments(obsv_in, shifts, solver)
    row_count = ctrl_cols.shape[0] * ctrl_cols.shape[1]
    partial_value = gram(
        ctrl_cols.reshape((row_count,) + ctrl_cols.shape[2:]),
        obsv_cols.reshape((row_count,) + obsv_cols.shape[2:]),
    )
    cells_total = total_x * region_ids.shape[1] * region_ids.shape[2]
    norm_scale = 1.0 / math.sqrt(cells_total)
    slab_count = lax.axis_size("slab")
    col_count = lax.axis_size("col")
    tile_rows = row_count // slab_count
    tile_cols = row_count // col_count
    tiles = partial_value.reshape(row_count, col_count, tile_cols).transpose(1, 0, 2)
    tiles = tiles.reshape(col_count, slab_count, tile_rows * tile_cols)
    own_tile = reduce_scatter(tiles, slab_count).reshape(tile_rows, tile_cols)
    return (ctrl_cols, obsv_cols, own_tile * norm_scale)


def solution(mesh):
    placed = (
        P("col", "slab", None, None),
        P("col", "slab", None, None),
        P("slab", None, None),
        P(),
        P(),
    )
    return jax.shard_map(
        body,
        mesh=mesh,
        in_specs=placed,
        out_specs=(
            P(None, None, "slab", "col", None),
            P(None, None, "slab", "col", None),
            P("slab", "col"),
        ),
        check_vma=False,
    )
```

```python
import math

import jax
import jax.numpy as jnp
from jax import lax
from jax.experimental import pallas as pl
from jax.experimental.pallas import tpu as pltpu
from jax.sharding import PartitionSpec as P

ADI = 2
STEPS = 3


def extended(block, sides, width):
    for axis, dim in sides:
        count = lax.axis_size(axis)
        forward = [(i, i + 1) for i in range(count - 1)]
        backward = [(target, source) for source, target in forward]
        low = lax.ppermute(
            lax.slice_in_dim(block, block.shape[dim] - width, None, axis=dim), axis, forward
        )
        high = lax.ppermute(lax.slice_in_dim(block, 0, width, axis=dim), axis, backward)
        block = jnp.concatenate([low, block, high], axis=dim)
    return block


def reduce_kernel(tiles_ref, out_ref, recv1, stage, recv2, send1, rsem1, send2, rsem2):
    ncol = tiles_ref.shape[0]
    nslab = recv2.shape[0]
    my_slab = lax.axis_index("slab")
    my_col = lax.axis_index("col")
    mesh = pl.DeviceIdType.MESH
    recv1[pl.ds(my_col, 1)] = tiles_ref[pl.ds(my_col, 1)]
    barrier = pltpu.get_barrier_semaphore()
    for k in range(1, ncol):
        peer = lax.rem(my_col + k, ncol)
        pl.semaphore_signal(barrier, inc=1, device_id=(my_slab, peer), device_id_type=mesh)

    def greet(k, carry):
        peer = lax.rem(my_slab + k, nslab)
        pl.semaphore_signal(barrier, inc=1, device_id=(peer, my_col), device_id_type=mesh)
        return carry

    lax.fori_loop(1, nslab, greet, 0)
    pl.semaphore_wait(barrier, ncol - 1 + nslab - 1)

    def col_copy(peer, src, dst):
        return pltpu.make_async_remote_copy(
            src_ref=tiles_ref.at[pl.ds(src, 1)],
            dst_ref=recv1.at[pl.ds(dst, 1)],
            send_sem=send1.at[src],
            recv_sem=rsem1.at[dst],
            device_id=(my_slab, peer),
            device_id_type=mesh,
        )

    for k in range(1, ncol):
        peer = lax.rem(my_col + k, ncol)
        col_copy(peer, peer, my_col).start()
    for k in range(1, ncol):
        peer = lax.rem(my_col + k, ncol)
        col_copy(peer, peer, my_col).wait_send()
        col_copy(peer, my_col, peer).wait_recv()
    summed = jnp.sum(recv1[...], axis=0)
    for k in range(nslab):
        stage[k] = summed[k:k + 1]
    recv2[pl.ds(my_slab, 1)] = stage[pl.ds(my_slab, 1)]

    def slab_copy(peer, src, dst):
        return pltpu.make_async_remote_copy(
            src_ref=stage.at[pl.ds(src, 1)],
            dst_ref=recv2.at[pl.ds(dst, 1)],
            send_sem=send2.at[src],
            recv_sem=rsem2.at[dst],
            device_id=(peer, my_col),
            device_id_type=mesh,
        )

    def send(k, carry):
        peer = lax.rem(my_slab + k, nslab)
        slab_copy(peer, peer, my_slab).start()
        return carry

    lax.fori_loop(1, nslab, send, 0)

    def finish(k, carry):
        peer = lax.rem(my_slab + k, nslab)
        slab_copy(peer, peer, my_slab).wait_send()
        slab_copy(peer, my_slab, peer).wait_recv()
        return carry

    lax.fori_loop(1, nslab, finish, 0)
    out_ref[...] = jnp.sum(recv2[...], axis=0, keepdims=True)


def reduce_scatter(tiles, nslab):
    ncol, rows, lanes = tiles.shape
    return pl.pallas_call(
        reduce_kernel,
        out_shape=jax.ShapeDtypeStruct((1, 1, lanes), jnp.float32),
        in_specs=[pl.BlockSpec(memory_space=pltpu.VMEM)],
        out_specs=pl.BlockSpec(memory_space=pltpu.VMEM),
        scratch_shapes=[
            pltpu.VMEM((ncol, rows, lanes), jnp.float32),
            pltpu.VMEM((nslab, 1, lanes), jnp.float32),
            pltpu.VMEM((nslab, 1, lanes), jnp.float32),
            pltpu.SemaphoreType.DMA((ncol,)),
            pltpu.SemaphoreType.DMA((ncol,)),
            pltpu.SemaphoreType.DMA((nslab,)),
            pltpu.SemaphoreType.DMA((nslab,)),
        ],
        compiler_params=pltpu.CompilerParams(collective_id=0, has_side_effects=True),
    )(tiles)


def exchange_kernel(x_ref, o_ref, send_sem, recv_sem):
    ncol = o_ref.shape[0] // x_ref.shape[0]
    cols = x_ref.shape[0]
    rows = o_ref.shape[2]
    my_slab = lax.axis_index("slab")
    my_col = lax.axis_index("col")
    mesh = pl.DeviceIdType.MESH
    barrier = pltpu.get_barrier_semaphore()
    for k in range(1, ncol):
        peer = lax.rem(my_col + k, ncol)
        pl.semaphore_signal(barrier, inc=1, device_id=(my_slab, peer), device_id_type=mesh)
    pl.semaphore_wait(barrier, ncol - 1)

    def chunk_copy(peer, src, dst):
        return pltpu.make_async_remote_copy(
            src_ref=x_ref.at[:, :, pl.ds(pl.multiple_of(src * rows, 8), rows), :],
            dst_ref=o_ref.at[pl.ds(dst * cols, cols)],
            send_sem=send_sem.at[src],
            recv_sem=recv_sem.at[dst],
            device_id=(my_slab, peer),
            device_id_type=mesh,
        )

    for k in range(1, ncol):
        peer = lax.rem(my_col + k, ncol)
        chunk_copy(peer, peer, my_col).start()
    for k in range(1, ncol):
        peer = lax.rem(my_col + k, ncol)
        chunk_copy(peer, peer, my_col).wait_send()
        chunk_copy(peer, my_col, peer).wait_recv()


def exchange(block, ncol):
    cols, depth, rows, lanes = block.shape
    received = pl.pallas_call(
        exchange_kernel,
        out_shape=jax.ShapeDtypeStruct((cols * ncol, depth, rows // ncol, lanes), block.dtype),
        in_specs=[pl.BlockSpec(memory_space=pl.ANY)],
        out_specs=pl.BlockSpec(memory_space=pl.ANY),
        scratch_shapes=[pltpu.SemaphoreType.DMA((ncol,)), pltpu.SemaphoreType.DMA((ncol,))],
        compiler_params=pltpu.CompilerParams(collective_id=1, has_side_effects=True),
    )(block)
    me = lax.axis_index("col")
    own = lax.dynamic_slice_in_dim(block, me * (rows // ncol), rows // ncol, axis=2)
    return lax.dynamic_update_slice_in_dim(received, own, me * cols, axis=0)


def gram_kernel(a_ref, b_ref, out_ref):
    @pl.when((pl.program_id(0) == 0) & (pl.program_id(1) == 0))
    def _():
        out_ref[...] = jnp.zeros_like(out_ref)

    rows = a_ref.shape[2]
    left = jnp.concatenate([a_ref[:, 0, row, :] for row in range(rows)], axis=1)
    right = jnp.concatenate([b_ref[:, 0, row, :] for row in range(rows)], axis=1)
    out_ref[...] += lax.dot_general(
        left,
        right,
        (((1,), (1,)), ((), ())),
        precision=lax.Precision.HIGHEST,
        preferred_element_type=jnp.float32,
    )


def gram(a, b, rows_per_step=16):
    count, depth, rows, lanes = a.shape
    spec = pl.BlockSpec((count, 1, rows_per_step, lanes), lambda i, j: (0, i, j, 0))
    return pl.pallas_call(
        gram_kernel,
        grid=(depth, rows // rows_per_step),
        in_specs=[spec, spec],
        out_specs=pl.BlockSpec((count, count), lambda i, j: (0, 0)),
        out_shape=jax.ShapeDtypeStruct((count, count), jnp.float32),
        cost_estimate=pl.CostEstimate(
            flops=2 * count * count * a.size // count, bytes_accessed=8 * a.size, transcendentals=0
        ),
    )(a, b)


def lookup(region_ids, region_cond):
    summed = jnp.zeros(region_ids.shape, jnp.float32)
    for region in range(region_cond.shape[0]):
        summed = summed + jnp.where(region_ids == region, region_cond[region], jnp.float32(0.0))
    return summed


def halo_pair(block, axis, dim):
    count = lax.axis_size(axis)
    forward = [(i, i + 1) for i in range(count - 1)]
    backward = [(target, source) for source, target in forward]
    size = block.shape[dim]
    low = lax.ppermute(lax.slice_in_dim(block, size - 1, None, axis=dim), axis, forward)
    high = lax.ppermute(lax.slice_in_dim(block, 0, 1, axis=dim), axis, backward)
    return low, high


def shifted(block, low, high, dim):
    size = block.shape[dim]
    ahead = jnp.concatenate([lax.slice_in_dim(block, 1, None, axis=dim), high], axis=dim)
    behind = jnp.concatenate([low, lax.slice_in_dim(block, 0, size - 1, axis=dim)], axis=dim)
    return ahead, behind


def coefficients(cond_xy):
    cond_mid = cond_xy[1:-1, 1:-1]
    kxp = 0.5 * (cond_mid + cond_xy[2:, 1:-1])
    kxm = 0.5 * (cond_mid + cond_xy[:-2, 1:-1])
    kyp = 0.5 * (cond_mid + cond_xy[1:-1, 2:])
    kym = 0.5 * (cond_mid + cond_xy[1:-1, :-2])
    cond_z = jnp.pad(cond_mid, ((0, 0), (0, 0), (1, 1)))
    kzp = 0.5 * (cond_mid + cond_z[:, :, 2:])
    kzm = 0.5 * (cond_mid + cond_z[:, :, :-2])
    return (kxp, kxm, kyp, kym, kzp, kzm)


def windows(block, rows, count):
    parts = [lax.slice_in_dim(block, c * rows, (c + 1) * rows, axis=2) for c in range(count)]
    received = lax.all_to_all(jnp.stack(parts), "col", 0, 0, tiled=True)
    return received.reshape((-1,) + received.shape[2:])


def conduction(field, coeffs):
    kxp, kxm, kyp, kym, kzp, kzm = coeffs
    xlo, xhi = halo_pair(field, "slab", 1)
    ylo, yhi = halo_pair(field, "col", 2)
    nxp, nxm = shifted(field, xlo, xhi, 1)
    nyp, nym = shifted(field, ylo, yhi, 2)
    field_z = jnp.pad(field, ((0, 0), (0, 0), (0, 0), (1, 1)))
    summed = kxp * (field - nxp)
    summed = summed + kxm * (field - nxm)
    summed = summed + kyp * (field - nyp)
    summed = summed + kym * (field - nym)
    summed = summed + kzp * (field - field_z[..., 2:])
    summed = summed + kzm * (field - field_z[..., :-2])
    return summed


def bounds(shift_val, cond_max):
    high_eig = shift_val + 12.0 * cond_max
    mid_eig = 0.5 * (high_eig + shift_val)
    half_span = 0.5 * (high_eig - shift_val)
    return (mid_eig, half_span, mid_eig / half_span)


def solve_slabs(right_side, shift_val, cond_max, coeffs):
    mid_eig, half_span, ratio_eig = bounds(shift_val, cond_max)
    rho_now = 1.0 / ratio_eig
    solution = jnp.zeros_like(right_side)
    residual = right_side
    direction = right_side / mid_eig
    for sweep_idx in range(STEPS - 1):
        solution = solution + direction
        applied = conduction(direction, coeffs) + shift_val * direction
        residual = residual - applied
        rho_next = 1.0 / (2.0 * ratio_eig - rho_now)
        direction = rho_next * rho_now * direction + 2.0 * rho_next / half_span * residual
        rho_now = rho_next
    return solution + direction


def run_segments(stacked, shifts, solver):
    factors = []
    current = stacked
    for segment_idx in range(ADI):
        shift_val = shifts[segment_idx]
        if segment_idx == 0:
            current = solver(stacked, shift_val)
        else:
            current = current - (shifts[segment_idx - 1] + shift_val) * solver(current, shift_val)
        factors.append(jnp.sqrt(2.0 * shift_val) * current)
    return jnp.stack(factors)


def body(input_map, output_map, region_ids, region_cond, shift_ids):
    col_count = lax.axis_size("col")
    ctrl_in = exchange(input_map, col_count)
    ctrl_in, output_map = lax.optimization_barrier((ctrl_in, output_map))
    obsv_in = windows(output_map, output_map.shape[2] // col_count, col_count)
    col_local = ctrl_in.shape[0]
    rows = ctrl_in.shape[2]
    local_x = input_map.shape[1]
    cond_cells = lookup(region_ids, region_cond)
    cond_max = jnp.max(region_cond)
    shifts = 0.25 * jnp.exp2(shift_ids.astype(jnp.float32))
    total_x = local_x * lax.axis_size("slab")
    cond_ypad = jnp.pad(cond_cells, ((0, 0), (1, 1), (0, 0)))
    cond_y = lax.dynamic_slice_in_dim(cond_ypad, lax.axis_index("col") * rows, rows + 2, axis=1)
    cond_xy = extended(cond_y, (("slab", 0),), 1)
    coeffs = coefficients(cond_xy)
    solver = lambda rhs, shift_val: solve_slabs(rhs, shift_val, cond_max, coeffs)
    ctrl_cols = run_segments(ctrl_in, shifts, solver)
    obsv_cols = run_segments(obsv_in, shifts, solver)
    row_count = ctrl_cols.shape[0] * ctrl_cols.shape[1]
    partial_value = gram(
        ctrl_cols.reshape((row_count,) + ctrl_cols.shape[2:]),
        obsv_cols.reshape((row_count,) + obsv_cols.shape[2:]),
    )
    cells_total = total_x * region_ids.shape[1] * region_ids.shape[2]
    norm_scale = 1.0 / math.sqrt(cells_total)
    slab_count = lax.axis_size("slab")
    col_count = lax.axis_size("col")
    tile_rows = row_count // slab_count
    tile_cols = row_count // col_count
    tiles = partial_value.reshape(row_count, col_count, tile_cols).transpose(1, 0, 2)
    tiles = tiles.reshape(col_count, slab_count, tile_rows * tile_cols)
    own_tile = reduce_scatter(tiles, slab_count).reshape(tile_rows, tile_cols)
    return (ctrl_cols, obsv_cols, own_tile * norm_scale)


def solution(mesh):
    placed = (
        P("col", "slab", None, None),
        P("col", "slab", None, None),
        P("slab", None, None),
        P(),
        P(),
    )
    return jax.shard_map(
        body,
        mesh=mesh,
        in_specs=placed,
        out_specs=(
            P(None, None, "slab", "col", None),
            P(None, None, "slab", "col", None),
            P("slab", "col"),
        ),
        check_vma=False,
    )
```

```python
import math

import jax
import jax.numpy as jnp
from jax import lax
from jax.experimental import pallas as pl
from jax.experimental.pallas import tpu as pltpu
from jax.sharding import PartitionSpec as P

ADI = 2
STEPS = 3


def extended(block, sides, width):
    for axis, dim in sides:
        count = lax.axis_size(axis)
        forward = [(i, i + 1) for i in range(count - 1)]
        backward = [(target, source) for source, target in forward]
        low = lax.ppermute(
            lax.slice_in_dim(block, block.shape[dim] - width, None, axis=dim), axis, forward
        )
        high = lax.ppermute(lax.slice_in_dim(block, 0, width, axis=dim), axis, backward)
        block = jnp.concatenate([low, block, high], axis=dim)
    return block


def reduce_kernel(tiles_ref, out_ref, recv1, stage, recv2, send1, rsem1, send2, rsem2):
    ncol = tiles_ref.shape[0]
    nslab = recv2.shape[0]
    my_slab = lax.axis_index("slab")
    my_col = lax.axis_index("col")
    mesh = pl.DeviceIdType.MESH
    recv1[pl.ds(my_col, 1)] = tiles_ref[pl.ds(my_col, 1)]
    barrier = pltpu.get_barrier_semaphore()
    for k in range(1, ncol):
        peer = lax.rem(my_col + k, ncol)
        pl.semaphore_signal(barrier, inc=1, device_id=(my_slab, peer), device_id_type=mesh)

    def greet(k, carry):
        peer = lax.rem(my_slab + k, nslab)
        pl.semaphore_signal(barrier, inc=1, device_id=(peer, my_col), device_id_type=mesh)
        return carry

    lax.fori_loop(1, nslab, greet, 0)
    pl.semaphore_wait(barrier, ncol - 1 + nslab - 1)

    def col_copy(peer, src, dst):
        return pltpu.make_async_remote_copy(
            src_ref=tiles_ref.at[pl.ds(src, 1)],
            dst_ref=recv1.at[pl.ds(dst, 1)],
            send_sem=send1.at[src],
            recv_sem=rsem1.at[dst],
            device_id=(my_slab, peer),
            device_id_type=mesh,
        )

    for k in range(1, ncol):
        peer = lax.rem(my_col + k, ncol)
        col_copy(peer, peer, my_col).start()
    for k in range(1, ncol):
        peer = lax.rem(my_col + k, ncol)
        col_copy(peer, peer, my_col).wait_send()
        col_copy(peer, my_col, peer).wait_recv()
    summed = jnp.sum(recv1[...], axis=0)
    for k in range(nslab):
        stage[k] = summed[k:k + 1]
    recv2[pl.ds(my_slab, 1)] = stage[pl.ds(my_slab, 1)]

    def slab_copy(peer, src, dst):
        return pltpu.make_async_remote_copy(
            src_ref=stage.at[pl.ds(src, 1)],
            dst_ref=recv2.at[pl.ds(dst, 1)],
            send_sem=send2.at[src],
            recv_sem=rsem2.at[dst],
            device_id=(peer, my_col),
            device_id_type=mesh,
        )

    def send(k, carry):
        peer = lax.rem(my_slab + k, nslab)
        slab_copy(peer, peer, my_slab).start()
        return carry

    lax.fori_loop(1, nslab, send, 0)

    def finish(k, carry):
        peer = lax.rem(my_slab + k, nslab)
        slab_copy(peer, peer, my_slab).wait_send()
        slab_copy(peer, my_slab, peer).wait_recv()
        return carry

    lax.fori_loop(1, nslab, finish, 0)
    out_ref[...] = jnp.sum(recv2[...], axis=0, keepdims=True)


def reduce_scatter(tiles, nslab):
    ncol, rows, lanes = tiles.shape
    return pl.pallas_call(
        reduce_kernel,
        out_shape=jax.ShapeDtypeStruct((1, 1, lanes), jnp.float32),
        in_specs=[pl.BlockSpec(memory_space=pltpu.VMEM)],
        out_specs=pl.BlockSpec(memory_space=pltpu.VMEM),
        scratch_shapes=[
            pltpu.VMEM((ncol, rows, lanes), jnp.float32),
            pltpu.VMEM((nslab, 1, lanes), jnp.float32),
            pltpu.VMEM((nslab, 1, lanes), jnp.float32),
            pltpu.SemaphoreType.DMA((ncol,)),
            pltpu.SemaphoreType.DMA((ncol,)),
            pltpu.SemaphoreType.DMA((nslab,)),
            pltpu.SemaphoreType.DMA((nslab,)),
        ],
        compiler_params=pltpu.CompilerParams(collective_id=0, has_side_effects=True),
    )(tiles)


def gram_kernel(a_ref, b_ref, out_ref):
    @pl.when((pl.program_id(0) == 0) & (pl.program_id(1) == 0))
    def _():
        out_ref[...] = jnp.zeros_like(out_ref)

    rows = a_ref.shape[2]
    left = jnp.concatenate([a_ref[:, 0, row, :] for row in range(rows)], axis=1)
    right = jnp.concatenate([b_ref[:, 0, row, :] for row in range(rows)], axis=1)
    out_ref[...] += lax.dot_general(
        left,
        right,
        (((1,), (1,)), ((), ())),
        precision=lax.Precision.HIGHEST,
        preferred_element_type=jnp.float32,
    )


def gram(a, b, rows_per_step=16):
    count, depth, rows, lanes = a.shape
    spec = pl.BlockSpec((count, 1, rows_per_step, lanes), lambda i, j: (0, i, j, 0))
    return pl.pallas_call(
        gram_kernel,
        grid=(depth, rows // rows_per_step),
        in_specs=[spec, spec],
        out_specs=pl.BlockSpec((count, count), lambda i, j: (0, 0)),
        out_shape=jax.ShapeDtypeStruct((count, count), jnp.float32),
        cost_estimate=pl.CostEstimate(
            flops=2 * count * count * a.size // count, bytes_accessed=8 * a.size, transcendentals=0
        ),
    )(a, b)


def lookup(region_ids, region_cond):
    summed = jnp.zeros(region_ids.shape, jnp.float32)
    for region in range(region_cond.shape[0]):
        summed = summed + jnp.where(region_ids == region, region_cond[region], jnp.float32(0.0))
    return summed


def halo_pair(block, axis, dim):
    count = lax.axis_size(axis)
    forward = [(i, i + 1) for i in range(count - 1)]
    backward = [(target, source) for source, target in forward]
    size = block.shape[dim]
    low = lax.ppermute(lax.slice_in_dim(block, size - 1, None, axis=dim), axis, forward)
    high = lax.ppermute(lax.slice_in_dim(block, 0, 1, axis=dim), axis, backward)
    return low, high


def shifted(block, low, high, dim):
    size = block.shape[dim]
    ahead = jnp.concatenate([lax.slice_in_dim(block, 1, None, axis=dim), high], axis=dim)
    behind = jnp.concatenate([low, lax.slice_in_dim(block, 0, size - 1, axis=dim)], axis=dim)
    return ahead, behind


def coefficients(cond_xy):
    cond_mid = cond_xy[1:-1, 1:-1]
    kxp = 0.5 * (cond_mid + cond_xy[2:, 1:-1])
    kxm = 0.5 * (cond_mid + cond_xy[:-2, 1:-1])
    kyp = 0.5 * (cond_mid + cond_xy[1:-1, 2:])
    kym = 0.5 * (cond_mid + cond_xy[1:-1, :-2])
    cond_z = jnp.pad(cond_mid, ((0, 0), (0, 0), (1, 1)))
    kzp = 0.5 * (cond_mid + cond_z[:, :, 2:])
    kzm = 0.5 * (cond_mid + cond_z[:, :, :-2])
    return (kxp, kxm, kyp, kym, kzp, kzm)


def windows(block, rows, count):
    parts = [lax.slice_in_dim(block, c * rows, (c + 1) * rows, axis=2) for c in range(count)]
    received = lax.all_to_all(jnp.stack(parts), "col", 0, 0, tiled=True)
    return received.reshape((-1,) + received.shape[2:])


def conduction(field, coeffs):
    kxp, kxm, kyp, kym, kzp, kzm = coeffs
    xlo, xhi = halo_pair(field, "slab", 1)
    ylo, yhi = halo_pair(field, "col", 2)
    nxp, nxm = shifted(field, xlo, xhi, 1)
    nyp, nym = shifted(field, ylo, yhi, 2)
    field_z = jnp.pad(field, ((0, 0), (0, 0), (0, 0), (1, 1)))
    summed = kxp * (field - nxp)
    summed = summed + kxm * (field - nxm)
    summed = summed + kyp * (field - nyp)
    summed = summed + kym * (field - nym)
    summed = summed + kzp * (field - field_z[..., 2:])
    summed = summed + kzm * (field - field_z[..., :-2])
    return summed


def bounds(shift_val, cond_max):
    high_eig = shift_val + 12.0 * cond_max
    mid_eig = 0.5 * (high_eig + shift_val)
    half_span = 0.5 * (high_eig - shift_val)
    return (mid_eig, half_span, mid_eig / half_span)


def solve_slabs(right_side, shift_val, cond_max, coeffs):
    mid_eig, half_span, ratio_eig = bounds(shift_val, cond_max)
    rho_now = 1.0 / ratio_eig
    solution = jnp.zeros_like(right_side)
    residual = right_side
    direction = right_side / mid_eig
    for sweep_idx in range(STEPS - 1):
        solution = solution + direction
        applied = conduction(direction, coeffs) + shift_val * direction
        residual = residual - applied
        rho_next = 1.0 / (2.0 * ratio_eig - rho_now)
        direction = rho_next * rho_now * direction + 2.0 * rho_next / half_span * residual
        rho_now = rho_next
    return solution + direction


def run_segments(stacked, shifts, solver):
    factors = []
    current = stacked
    for segment_idx in range(ADI):
        shift_val = shifts[segment_idx]
        if segment_idx == 0:
            current = solver(stacked, shift_val)
        else:
            current = current - (shifts[segment_idx - 1] + shift_val) * solver(current, shift_val)
        factors.append(jnp.sqrt(2.0 * shift_val) * current)
    return jnp.stack(factors)


def body(input_map, output_map, region_ids, region_cond, shift_ids):
    col_count = lax.axis_size("col")
    both = windows(jnp.concatenate([input_map, output_map], 0), input_map.shape[2] // col_count, col_count)
    both = both.reshape((col_count, 2, input_map.shape[0]) + both.shape[1:])
    ctrl_in = both[:, 0].reshape((-1,) + both.shape[3:])
    obsv_in = both[:, 1].reshape((-1,) + both.shape[3:])
    col_local = ctrl_in.shape[0]
    rows = ctrl_in.shape[2]
    local_x = input_map.shape[1]
    cond_cells = lookup(region_ids, region_cond)
    cond_max = jnp.max(region_cond)
    shifts = 0.25 * jnp.exp2(shift_ids.astype(jnp.float32))
    total_x = local_x * lax.axis_size("slab")
    cond_ypad = jnp.pad(cond_cells, ((0, 0), (1, 1), (0, 0)))
    cond_y = lax.dynamic_slice_in_dim(cond_ypad, lax.axis_index("col") * rows, rows + 2, axis=1)
    cond_xy = extended(cond_y, (("slab", 0),), 1)
    coeffs = coefficients(cond_xy)
    solver = lambda rhs, shift_val: solve_slabs(rhs, shift_val, cond_max, coeffs)
    ctrl_cols = run_segments(ctrl_in, shifts, solver)
    obsv_cols = run_segments(obsv_in, shifts, solver)
    row_count = ctrl_cols.shape[0] * ctrl_cols.shape[1]
    partial_value = gram(
        ctrl_cols.reshape((row_count,) + ctrl_cols.shape[2:]),
        obsv_cols.reshape((row_count,) + obsv_cols.shape[2:]),
    )
    cells_total = total_x * region_ids.shape[1] * region_ids.shape[2]
    norm_scale = 1.0 / math.sqrt(cells_total)
    slab_count = lax.axis_size("slab")
    col_count = lax.axis_size("col")
    tile_rows = row_count // slab_count
    tile_cols = row_count // col_count
    tiles = partial_value.reshape(row_count, col_count, tile_cols).transpose(1, 0, 2)
    tiles = tiles.reshape(col_count, slab_count, tile_rows * tile_cols)
    own_tile = reduce_scatter(tiles, slab_count).reshape(tile_rows, tile_cols)
    return (ctrl_cols, obsv_cols, own_tile * norm_scale)


def solution(mesh):
    placed = (
        P("col", "slab", None, None),
        P("col", "slab", None, None),
        P("slab", None, None),
        P(),
        P(),
    )
    return jax.shard_map(
        body,
        mesh=mesh,
        in_specs=placed,
        out_specs=(
            P(None, None, "slab", "col", None),
            P(None, None, "slab", "col", None),
            P("slab", "col"),
        ),
        check_vma=False,
    )
```
